32 devices in a mesh: dp: 8 (over z, y), tensor: 4 (over x, core).
Axes of the slice: x: 2, y: 2, z: 4, core: 2. Of those that a mesh axis runs over, the one named last changes fastest.
Arguments:
- tokens: bfloat16 [4096, 768], P('dp'), may hold values from -6 to 6
- cotangent: bfloat16 [4096, 768], P('dp'), may hold values from -6 to 6
- lengths: int32 [8, 16], P('dp'), may hold values from 0 to 512, as said below
- labels: int32 [8, 16], P('dp'), may hold values from 0 to 2
- w_qkv: bfloat16 [768, 3, 768], P(None, None, 'tensor'), may hold values from -0.21875 to 0.21875
- qv_bias: float32 [2, 768], P(None, 'tensor'), may hold values from -1.5 to 1.5
- w_out: bfloat16 [768, 768], P('tensor'), may hold values from -0.75 to 0.75
- branch_bias: float32 [2, 768], replicated, may hold values from -1.5 to 1.5
- norm_gain: float32 [2, 768], replicated, may hold values from 0.5 to 1.5
- norm_shift: float32 [2, 768], replicated, may hold values from -1.5 to 1.5
- w_up: bfloat16 [768, 3072], P(None, 'tensor'), may hold values from -0.21875 to 0.21875
- up_bias: bfloat16 [3072], P('tensor'), may hold values from -1.5 to 1.5
- w_down: bfloat16 [3072, 768], P('tensor'), may hold values from -0.109375 to 0.109375
- w_pool: bfloat16 [768, 768], replicated, may hold values from -0.21875 to 0.21875
- pool_bias: float32 [768], replicated, may hold values from -1.5 to 1.5
- w_class: bfloat16 [768, 3], replicated, may hold values from -0.625 to 0.625
- class_bias: float32 [3], replicated, may hold values from -2.5 to 2.5
Outputs:
- block_out: bfloat16 [4096, 768], P('dp')
- grad_tokens: bfloat16 [4096, 768], P('dp')
- ramp_loss: float32 [], replicated
- ramp_entropy: float32 [], replicated
- grad_qkv: float32 [768, 3, 768], P('dp', None, 'tensor')
- grad_qv_bias: float32 [2, 768], P(None, ('tensor', 'dp'))
- grad_out: float32 [768, 768], P('tensor', 'dp')
- grad_branch_bias: float32 [2, 768], P(None, 'dp')
- grad_norm_gain: float32 [2, 768], P(None, 'dp')
- grad_norm_shift: float32 [2, 768], P(None, 'dp')
- grad_up: float32 [768, 3072], P('dp', 'tensor')
- grad_up_bias: float32 [3072], P(('tensor', 'dp'))
- grad_down: float32 [3072, 768], P('tensor', 'dp')
- grad_pool: float32 [768, 768], P('dp')
- grad_pool_bias: float32 [768], P('dp')
- grad_class: float32 [768, 3], P('dp')
- grad_class_bias: float32 [3], replicated
The draws below stay inside these ranges and needn't reach their ends.
Inputs may be any that keep to these rules, and one draw needn't show every extreme that they name: In each packed row the lengths of its items stand in its first slots and the remaining slots hold 0; the first slot is at least 1 and a row's lengths sum to at most 512. Some row of every draw is a single item of 512 tokens.
All inputs are finite; a program needn't handle non-finite values.
Results may differ from the reference program's by a relative error of at most 0.02.
Values may be sent and summed in bfloat16 or wider, within the bound.
A program may use at most 128 MiB of HBM per device.

```python
import jax
import jax.numpy as jnp
from jax import lax

D = 768
HEADS = 12
HD = 64
FF = 3072
CLASSES = 3
SEQ = 512
SLOTS = 16
ROWS_DEV = 1
ROWS = 8
TOKENS = 4096
N_DP = 8
N_TENSOR = 4


def draw_lengths(key, part):
    row_order = jnp.arange(ROWS, dtype=jnp.int32)
    shortest = SEQ // 16
    longest = SEQ * 5 // 8
    spread = max(ROWS - 1, 1)
    mean_size = shortest + (longest - shortest) * (ROWS - 1 - row_order) // spread
    size_key = jax.random.fold_in(key, 11)
    long_key = jax.random.fold_in(key, 12)
    raw_draw = jax.random.randint(size_key, (ROWS, SLOTS), 0, 1 << 20, dtype=jnp.int32)
    item_sizes = 1 + raw_draw % (2 * mean_size[:, None])
    end_places = jnp.cumsum(item_sizes, axis=1, dtype=jnp.int32)
    slot_order = jnp.arange(SLOTS, dtype=jnp.int32)
    keep_slot = (end_places <= SEQ) | (slot_order == 0)[None, :]
    item_sizes = jnp.where(keep_slot, jnp.minimum(item_sizes, SEQ), 0)
    whole_row = (jax.random.randint(long_key, (ROWS,), 0, 8, dtype=jnp.int32) == 0) | (row_order == ROWS // 2)
    single = jnp.where(slot_order[None, :] == 0, SEQ, 0)
    return jnp.where(whole_row[:, None], single, item_sizes).astype(jnp.int32)


def plant(array, key, low, largest):
    longest = array.shape.index(max(array.shape))
    spots = []
    for shift in (0, 1):
        where = [jax.random.randint(jax.random.fold_in(key, axis), (), 0, length) for axis, length in enumerate(array.shape)]
        where[longest] = (where[longest] + shift) % array.shape[longest]
        spots.append(tuple(where))
    return array.at[spots[0]].set(low).at[spots[1]].set(largest)


def raised(values, stream_key, source, target, shards_of, factor):
    def block_of(dim):
        return (jnp.arange(values.shape[dim]) // (values.shape[dim] // shards_of)).reshape((-1,) + (1,) * (values.ndim - 1 - dim))

    near = jax.random.permutation(stream_key, shards_of)[block_of(target)]
    other_side = (block_of(target) + shards_of // 2) % shards_of
    return jnp.where((block_of(source) == near) | (block_of(source) == other_side), factor * values, values)


def block_levels(rng, extent, cuts, least, top_value):
    def one(position, shards_of):
        steps = jax.random.uniform(jax.random.fold_in(jax.random.fold_in(rng, 6), position), (shards_of,), jnp.float32, least / len(cuts), top_value / len(cuts))
        return jnp.repeat(jnp.exp(steps), extent[position] // shards_of).reshape((-1,) + (1,) * (len(extent) - position - 1))

    gain = one(*cuts[0])
    for cut in cuts[1:]:
        gain = gain * one(*cut)
    return gain


def bell_draw(key, extent, scale, most, shards=(), kind=jnp.bfloat16):
    array = jax.random.normal(key, extent, jnp.float32) * scale
    if len(shards) > 0:
        array = block_levels(key, extent, shards, -0.22, 0.18) * array
    return jnp.clip(array, min=-most, max=most).astype(kind)


def bell_draw_with(rng, shape, scale, reach, cuts, heavy, kind=jnp.bfloat16):
    result = scale * jax.random.normal(rng, shape, jnp.float32)
    if cuts:
        result = result * block_levels(rng, shape, cuts, -0.22, 0.18)
    return jnp.clip(raised(result, jax.random.fold_in(rng, 3), *heavy), -reach, reach).astype(kind)


def setup_inputs(seed: int = 0) -> dict:
    keys = jax.random.split(jax.random.key(seed), 18)
    tokens = bell_draw(keys[0], (TOKENS, D), 1.0, 6.0, ((0, 8),))
    cotangent = bell_draw_with(keys[1], (TOKENS, D), 1.0, 6.0, ((0, 8),), (0, 1, 8, 2.0))
    lengths = draw_lengths(jax.random.fold_in(keys[17], 71), 0)
    labels = plant(jax.random.randint(keys[3], (ROWS, SLOTS), 0, CLASSES), jax.random.fold_in(keys[3], 1), 0, CLASSES - 1).astype(jnp.int32)
    w_qkv = bell_draw(keys[4], (D, 3, D), D ** -0.5, 0.21875, ((2, 4),))
    qv_bias = bell_draw(keys[5], (2, D), 0.3, 1.5, ((1, 4),), jnp.float32)
    w_out = bell_draw(keys[6], (D, D), HD ** -0.5, 0.75, ((0, 4),))
    branch_bias = bell_draw(keys[7], (2, D), 0.3, 1.5, (), jnp.float32)
    norm_gain = jnp.clip(1.0 + 0.1 * jax.random.normal(keys[8], (2, D), jnp.float32), 0.5, 1.5)
    norm_shift = bell_draw(keys[9], (2, D), 0.3, 1.5, (), jnp.float32)
    w_up = bell_draw(keys[10], (D, FF), D ** -0.5, 0.21875, ((1, 4),))
    up_bias = bell_draw(keys[11], (FF,), 0.3, 1.5, ((0, 4),))
    w_down = bell_draw(keys[12], (FF, D), FF ** -0.5, 0.109375, ((0, 4),))
    w_pool = bell_draw(keys[13], (D, D), D ** -0.5, 0.21875)
    pool_bias = bell_draw(keys[14], (D,), 0.3, 1.5, (), jnp.float32)
    w_class = bell_draw(keys[15], (D, CLASSES), (D // 8) ** -0.5, 0.625)
    class_bias = bell_draw(keys[16], (CLASSES,), 0.5, 2.5, (), jnp.float32)
    return dict(tokens=tokens, cotangent=cotangent, lengths=lengths, labels=labels, w_qkv=w_qkv, qv_bias=qv_bias, w_out=w_out, branch_bias=branch_bias, norm_gain=norm_gain, norm_shift=norm_shift, w_up=w_up, up_bias=up_bias, w_down=w_down, w_pool=w_pool, pool_bias=pool_bias, w_class=w_class, class_bias=class_bias)


@jax.custom_vjp
def low(v):
    return lax.optimization_barrier(v.astype(jnp.bfloat16)).astype(jnp.float32)

@jax.custom_vjp
def low_back(v):
    return v

def low_keep(v):
    return (low(v), None)

def low_pass(kept, grad):
    return (grad,)

def back_keep(v):
    return (v, None)

def back_low(kept, grad):
    return (low(grad),)
low.defvjp(low_keep, low_pass)
low_back.defvjp(back_keep, back_low)
masked_score = -1e+30
norm_eps = 1e-12

def exact_dot(first_mat, second_mat):
    return jnp.dot(first_mat, second_mat, precision=lax.Precision.HIGHEST, preferred_element_type=jnp.float32)

def layer_norm(values, gain_row, shift_row):
    mean_row = lax.optimization_barrier(jnp.mean(values, axis=-1, keepdims=True))
    centered = values - mean_row
    variance = lax.optimization_barrier(jnp.mean(centered * centered, axis=-1, keepdims=True))
    return centered * lax.rsqrt(variance + norm_eps) * gain_row + shift_row

def row_attention(packed):
    queries, keys_row, values, segment = packed
    queries = queries.reshape(SEQ, HEADS, HD)
    keys_row = keys_row.reshape(SEQ, HEADS, HD)
    values = values.reshape(SEQ, HEADS, HD)
    raw_scores = jnp.einsum('qhd,khd->hqk', queries, keys_row, precision=lax.Precision.HIGHEST) * HD ** (-0.5)
    same_segment = (segment[:, None] == segment[None, :])[None]
    scores = jnp.where(same_segment, low_back(raw_scores), masked_score)
    row_top = lax.optimization_barrier(jnp.max(scores, axis=-1, keepdims=True))
    expo_terms = jnp.exp(scores - row_top)
    prob_rows = expo_terms / lax.optimization_barrier(jnp.sum(expo_terms, axis=-1, keepdims=True))
    mixed_rows = jnp.einsum('hqk,khd->qhd', low(prob_rows), values, precision=lax.Precision.HIGHEST)
    return mixed_rows.reshape(SEQ, D)

def group_objective(block_in, params, cot_rows, segment, live_token, first_index, item_live, label_hot, item_count):
    w_qkv, qv_bias, w_out, branch_bias, norm_gain, norm_shift, w_up, up_bias, w_down, w_pool, pool_bias, w_class, class_bias = params
    qkv_bias = jnp.concatenate([qv_bias[0], jnp.zeros_like(qv_bias[0]), qv_bias[1]])
    qkv_rows = low(low_back(exact_dot(block_in, w_qkv.reshape(D, 3 * D)) + qkv_bias))
    queries = qkv_rows[:, :D].reshape(ROWS_DEV, SEQ, D)
    keys_all = qkv_rows[:, D:2 * D].reshape(ROWS_DEV, SEQ, D)
    values = qkv_rows[:, 2 * D:].reshape(ROWS_DEV, SEQ, D)
    context = lax.map(jax.checkpoint(row_attention), (queries, keys_all, values, segment))
    context = low(low_back(context.reshape(ROWS_DEV * SEQ, D)))
    part_width = D // N_TENSOR
    pieces = [low(exact_dot(context[:, group_index * part_width:(group_index + 1) * part_width], w_out[group_index * part_width:(group_index + 1) * part_width])) for group_index in range(N_TENSOR)]
    summed = pieces[0]
    for piece_term in pieces[1:]:
        summed = summed + piece_term
    attention = low_back(summed) + branch_bias[0]
    hidden = layer_norm(block_in + attention, norm_gain[0], norm_shift[0])
    pre_act = low_back(exact_dot(low(hidden), w_up) + up_bias)
    act = jax.nn.gelu(pre_act, approximate=False)
    branch = low(low_back(exact_dot(low(act), w_down)))
    output = layer_norm(hidden + (branch + branch_bias[1]), norm_gain[1], norm_shift[1])
    picked = jnp.take(output, first_index, axis=0)
    pooled = jnp.tanh(low_back(exact_dot(low(picked), w_pool) + pool_bias))
    logits = exact_dot(low(pooled), w_class) + class_bias
    row_top = lax.optimization_barrier(jnp.max(logits, axis=1, keepdims=True))
    shifted = logits - row_top
    log_probs = shifted - jnp.log(lax.optimization_barrier(jnp.sum(jnp.exp(shifted), axis=1, keepdims=True)))
    item_ce = -lax.optimization_barrier(jnp.sum(label_hot * log_probs, axis=1)) * item_live
    item_ent = -lax.optimization_barrier(jnp.sum(jnp.exp(log_probs) * log_probs, axis=1)) * item_live
    objective = jnp.sum(item_ce) / item_count + jnp.sum(output * live_token[:, None] * cot_rows)
    return (objective, (output, jnp.sum(item_ce), jnp.sum(item_ent)))

def reference(tokens, cotangent, lengths, labels, w_qkv, qv_bias, w_out, branch_bias, norm_gain, norm_shift, w_up, up_bias, w_down, w_pool, pool_bias, w_class, class_bias):
    params = tuple((item.astype(jnp.float32) for item in (w_qkv, qv_bias, w_out, branch_bias, norm_gain, norm_shift, w_up, up_bias, w_down, w_pool, pool_bias, w_class, class_bias)))
    end_places = jnp.cumsum(lengths, axis=1, dtype=jnp.int32)
    starts = end_places - lengths
    places = jnp.arange(SEQ, dtype=jnp.int32)
    segment = lax.optimization_barrier(jnp.sum((end_places[:, None, :] <= places[None, :, None]).astype(jnp.int32), axis=2, dtype=jnp.int32))
    live_token = (places[None, :] < end_places[:, -1:]).astype(jnp.float32)
    item_live = (lengths > 0).astype(jnp.float32)
    item_count = jnp.sum(item_live)
    local_rows = jnp.arange(ROWS_DEV, dtype=jnp.int32)[None, :, None] * SEQ
    first_index = (local_rows + jnp.minimum(starts, SEQ - 1).reshape(N_DP, ROWS_DEV, SLOTS)).reshape(N_DP, ROWS_DEV * SLOTS)
    label_hot = (labels[..., None] == jnp.arange(CLASSES, dtype=jnp.int32)).astype(jnp.float32).reshape(N_DP, ROWS_DEV * SLOTS, CLASSES)
    group_data = (tokens.astype(jnp.float32).reshape(N_DP, ROWS_DEV * SEQ, D), cotangent.astype(jnp.float32).reshape(N_DP, ROWS_DEV * SEQ, D), segment.reshape(N_DP, ROWS_DEV, SEQ), live_token.reshape(N_DP, ROWS_DEV * SEQ), first_index, item_live.reshape(N_DP, ROWS_DEV * SLOTS), label_hot)

    def accumulate(carried, group_rows):
        gradients, side_sums = carried
        block_in, cot_rows, seg_rows, live_rows, first_rows, live_items, hot_rows = group_rows

        def objective_fn(block_value, param_set):
            return group_objective(block_value, param_set, cot_rows, seg_rows, live_rows, first_rows, live_items, hot_rows, item_count)
        objective_value, pullback, aux_out = jax.vjp(objective_fn, block_in, params, has_aux=True)
        d_block, d_params = pullback(jnp.ones_like(objective_value))
        gradients = jax.tree.map(jnp.add, gradients, d_params)
        side_sums = side_sums + jnp.stack([aux_out[1], aux_out[2]])
        return ((gradients, side_sums), (aux_out[0].astype(jnp.bfloat16), d_block.astype(jnp.bfloat16)))
    initial = (jax.tree.map(jnp.zeros_like, params), jnp.zeros((2,), jnp.float32))
    (gradients, side_sums), (block_rows, grad_rows) = lax.scan(accumulate, initial, group_data)
    block_out = block_rows.reshape(TOKENS, D)
    grad_tokens = grad_rows.reshape(TOKENS, D)
    ramp_loss = side_sums[0] / item_count
    ramp_entropy = side_sums[1] / item_count
    grad_qkv, grad_qv_bias, grad_out, grad_branch_bias, grad_norm_gain, grad_norm_shift, grad_up, grad_up_bias, grad_down, grad_pool, grad_pool_bias, grad_class, grad_class_bias = gradients
    return (block_out, grad_tokens, ramp_loss, ramp_entropy, grad_qkv, grad_qv_bias, grad_out, grad_branch_bias, grad_norm_gain, grad_norm_shift, grad_up, grad_up_bias, grad_down, grad_pool, grad_pool_bias, grad_class, grad_class_bias)
```

```python
from functools import partial

import jax
import jax.numpy as jnp
from jax import lax
from jax.experimental import pallas as pl
from jax.experimental.pallas import tpu as pltpu
from jax.sharding import PartitionSpec as P

HD = 64
MESH = pl.DeviceIdType.MESH
F32 = jnp.float32
BF16 = jnp.bfloat16
masked_score = -1e30
norm_eps = 1e-12
SQRT_HALF = 0.7071067811865476
PDF_SCALE = 0.3989422804014327
VEC_ROWS = 16


def dot_nn(a, b):
    return lax.dot_general(a, b, (((1,), (0,)), ((), ())), preferred_element_type=F32)


def dot_nt(a, b):
    return lax.dot_general(a, b, (((1,), (1,)), ((), ())), preferred_element_type=F32)


def dot_tn(a, b):
    return lax.dot_general(a, b, (((0,), (0,)), ((), ())), preferred_element_type=F32)


def row_mean(v):
    return jnp.sum(v, axis=1, keepdims=True) * (1.0 / v.shape[1])


def col_sum(v):
    return jnp.sum(v, axis=0, keepdims=True)


def norm_forward(values):
    centered = values - row_mean(values)
    inv_scale = lax.rsqrt(row_mean(centered * centered) + norm_eps)
    return centered * inv_scale, inv_scale


def norm_backward(gradient, normed, inv_scale, gain_row):
    scaled = gradient * gain_row
    inner = scaled - row_mean(scaled) - normed * row_mean(scaled * normed)
    return inner * inv_scale


def gelu_parts(pre_act):
    cdf = 0.5 * (1.0 + lax.erf(pre_act * SQRT_HALF))
    pdf = PDF_SCALE * jnp.exp(-0.5 * pre_act * pre_act)
    return pre_act * cdf, cdf + pre_act * pdf


class Copies:
    def __init__(self, send_sems, recv_sems):
        self.send_sems, self.recv_sems, self.used, self.open = send_sems, recv_sems, 0, []

    def start(self, src, dst, device):
        copy = pltpu.make_async_remote_copy(
            src_ref=src,
            dst_ref=dst,
            send_sem=self.send_sems.at[self.used],
            recv_sem=self.recv_sems.at[self.used],
            device_id=device,
            device_id_type=MESH,
        )
        self.used += 1
        copy.start()
        self.open.append(copy)
        return copy

    def finish(self):
        for copy in self.open:
            copy.wait_send()


class Loads:
    def __init__(self, sems):
        self.sems, self.used = sems, 0

    def start(self, src, dst):
        copy = pltpu.make_async_copy(src, dst, self.sems.at[self.used])
        self.used += 1
        copy.start()
        return copy


def remote_copy_count(groups):
    return 48 + 3 * (1 + 2 * groups) + 8 * groups


def layer_kernel(
    n_dp,
    tok_hbm,
    cot_hbm,
    len_ref,
    lab_ref,
    wqkv_hbm,
    qvb_ref,
    wout_hbm,
    bb_ref,
    ng_ref,
    ns_ref,
    wup_hbm,
    upb_ref,
    wdn_hbm,
    wpool_hbm,
    pb_ref,
    wcls_ref,
    cb_ref,
    bout_hbm,
    gtok_hbm,
    gqkvo_hbm,
    gup_hbm,
    gdn_hbm,
    gpool_hbm,
    vec_hbm,
    tok,
    cot,
    wt,
    wo,
    wup,
    wdn,
    wpool,
    small,
    bias_mask,
    k_nt,
    v_nt,
    k_tr,
    v_tr,
    q_tr,
    probs,
    ctx_all,
    hid,
    hid_low,
    hid_tr,
    tok_tr,
    n_one,
    n_two,
    scale_one,
    scale_two,
    act_low,
    d_gelu,
    acc,
    parts,
    parts_b,
    parts_c,
    out_low,
    d_sec,
    d_br,
    d_br_tr,
    d_pre_low,
    d_first,
    d_att,
    d_att_tr,
    d_ctx,
    d_kv_f32,
    d_kv_send,
    d_kv_recv,
    d_qkv,
    gt_low,
    g_send,
    g_recv,
    g_own,
    y_send,
    y_recv,
    z_send,
    z_recv,
    g_fin,
    pool_fin,
    items,
    items_c,
    picked_t,
    vec,
    vec_c,
    vec_s,
    vec_y,
    vec_z,
    vec_fin,
    cnt,
    cnt_y,
    cnt_s,
    cnt_z,
    load_sems,
    send_sems,
    recv_sems,
):
    groups = n_dp // 2
    dp = lax.axis_index("dp")
    me = lax.axis_index("tensor")
    x = me // 2
    c = lax.rem(me, 2)
    y = lax.rem(dp, 2)
    h = dp // 2
    core_dev = (dp, me + 1 - 2 * c)
    x_dev = (dp, 2 * (1 - x) + c)
    y_dev = (dp + 1 - 2 * y, me)

    def z_dev(k):
        return (lax.rem(h + k, groups) * 2 + y, me)

    token_count, width = tok.shape
    half = token_count // 2
    local_width = wo.shape[1]
    chip_width = 2 * local_width
    heads = chip_width // HD
    slots = len_ref.shape[1]
    shard = width // n_dp
    chunk = 128
    chunks = half // chunk
    tile = 256
    tiles = width // tile
    own_rows = pl.ds(pl.multiple_of(c * half, half), half)

    barrier = pltpu.get_barrier_semaphore()
    peers = [core_dev, x_dev, y_dev] + [z_dev(k) for k in range(1, groups)]
    for peer in peers:
        pl.semaphore_signal(barrier, inc=1, device_id=peer, device_id_type=MESH)

    loads = Loads(load_sems)
    remote = Copies(send_sems, recv_sems)
    load_tok = loads.start(tok_hbm, tok)
    load_wt = loads.start(wqkv_hbm, wt.at[c])
    load_wo = loads.start(wout_hbm, wo.at[me])
    load_wup = loads.start(wup_hbm, wup.at[c])
    load_wdn = loads.start(wdn_hbm, wdn.at[c])
    load_cot = loads.start(cot_hbm.at[own_rows], cot)
    load_pool = loads.start(wpool_hbm, wpool)

    lengths = [len_ref[0, i] for i in range(slots)]
    ends, total = [], 0
    for i in range(slots):
        total = total + lengths[i]
        ends.append(total)
    firsts = [jnp.minimum(ends[i] - lengths[i], token_count - 1) for i in range(slots)]
    key_place = lax.broadcasted_iota(jnp.int32, (token_count, 128), 0)
    query_place = lax.broadcasted_iota(jnp.int32, (8, half), 1) + c * half
    key_segment = jnp.zeros((token_count, 128), jnp.int32)
    query_segment = jnp.zeros((8, half), jnp.int32)
    for i in range(slots):
        key_segment = key_segment + (key_place >= ends[i]).astype(jnp.int32)
        query_segment = query_segment + (query_place >= ends[i]).astype(jnp.int32)
    for n in range(half // 128):
        cols = slice(n * 128, (n + 1) * 128)
        bias_mask[:, cols] = jnp.where(key_segment == query_segment[0:1, cols], 0.0, masked_score)
    item_row = lax.broadcasted_iota(jnp.int32, (slots, 128), 0)
    first_col = jnp.zeros((slots, 128), jnp.int32)
    len_col = jnp.zeros((slots, 128), jnp.int32)
    lab_col = jnp.zeros((slots, 128), jnp.int32)
    for i in range(slots):
        first_col = first_col + jnp.where(item_row == i, firsts[i], 0)
        len_col = len_col + jnp.where(item_row == i, lengths[i], 0)
        lab_col = lab_col + jnp.where(item_row == i, lab_ref[0, i], 0)
    live_all = jnp.where(len_col > 0, 1.0, 0.0)
    cnt[...] = jnp.broadcast_to(col_sum(live_all), cnt.shape)

    small[c] = jnp.concatenate(
        [
            upb_ref[...].astype(F32),
            jnp.concatenate([qvb_ref[...], jnp.zeros((2, width - local_width), F32)], axis=1),
            jnp.zeros((5, width), F32),
        ],
        axis=0,
    )
    vec[...] = jnp.zeros_like(vec)

    pl.semaphore_wait(barrier, len(peers))
    send_wt = remote.start(wqkv_hbm, wt.at[c], core_dev)
    send_small = remote.start(small.at[c], small.at[c], core_dev)
    send_wo_x = remote.start(wout_hbm, wo.at[me], x_dev)
    send_wo_c = remote.start(wout_hbm, wo.at[me], core_dev)
    send_cnt_y = remote.start(cnt, cnt_y, y_dev)
    send_wup = remote.start(wup_hbm, wup.at[c], core_dev)
    send_wdn = remote.start(wdn_hbm, wdn.at[c], core_dev)

    load_tok.wait()
    load_wt.wait()
    send_wt.wait_recv()
    send_small.wait_recv()

    def chip_rows(part):
        rows = slice(part * local_width, (part + 1) * local_width)
        return jnp.concatenate([wt[0, rows, :], wt[1, rows, :]], axis=0)

    def bias_row(part):
        return jnp.concatenate(
            [small[0, 1 + part : 2 + part, :local_width], small[1, 1 + part : 2 + part, :local_width]], axis=1
        )

    def bias_cols(part, columns):
        block = jnp.transpose(jnp.broadcast_to(bias_row(part), (128, chip_width)))
        return jnp.concatenate([block] * (columns // 128), axis=1)

    weights_q, weights_k, weights_v = chip_rows(0), chip_rows(1), chip_rows(2)
    q_tr[...] = (dot_nt(weights_q, tok[own_rows, :]) + bias_cols(0, half)).astype(BF16)
    k_nt[...] = dot_nt(tok[...], weights_k).astype(BF16)
    v_tr[...] = (dot_nt(weights_v, tok[...]) + bias_cols(1, token_count)).astype(BF16)

    half_row = lax.broadcasted_iota(jnp.int32, (128, half), 0) < HD
    inv_root = HD ** (-0.5)

    def half_of(block, side):
        zero = jnp.zeros_like(block)
        return jnp.where(half_row, block, zero) if side == 0 else jnp.where(half_row, zero, block)

    send_ctx = []
    for pair in range(heads // 2):
        pair_rows = slice(pair * 128, (pair + 1) * 128)
        for side in range(2):
            head = 2 * pair + side
            head_rows = slice(head * HD, (head + 1) * HD)
            scores = dot_nn(k_nt[:, pair_rows], half_of(q_tr[pair_rows, :], side)) * inv_root + bias_mask[...]
            terms = jnp.exp(scores - jnp.max(scores, axis=0, keepdims=True))
            weights = terms * (1.0 / col_sum(terms))
            probs[head] = weights
            ctx_all[x, head_rows, :] = dot_nn(v_tr[head_rows, :], weights.astype(BF16)).astype(BF16)
        send_ctx.append(remote.start(ctx_all.at[x, pair_rows], ctx_all.at[x, pair_rows], x_dev))
        if pair == 0:
            send_wo_x.wait_recv()
            other = 2 * (1 - x) + c
            send_wo_f = remote.start(wo.at[other], wo.at[other], core_dev)
            send_cnt_y.wait_recv()
            cnt_s[...] = cnt[...] + cnt_y[...]
            send_cnt_z = [remote.start(cnt_s, cnt_z.at[k - 1], z_dev(k)) for k in range(1, groups)]

    k_tr[...] = dot_nt(weights_k, tok[...]).astype(BF16)
    v_nt[...] = (dot_nt(tok[...], weights_v) + bias_row(1)).astype(BF16)
    tok_tr[...] = jnp.transpose(tok[own_rows, :])

    load_wo.wait()
    send_wo_c.wait_recv()
    send_wo_f.wait_recv()
    for copy in send_ctx:
        copy.wait_recv()

    for i in range(chunks):
        rows = slice(i * chunk, (i + 1) * chunk)
        attention = None
        for g in range(4):
            group_rows = slice((g % 2) * local_width, (g % 2 + 1) * local_width)
            piece = dot_tn(ctx_all[g // 2, group_rows, rows], wo[g]).astype(BF16).astype(F32)
            attention = piece if attention is None else attention + piece
        token_rows = pl.ds(pl.multiple_of(c * half + i * chunk, chunk), chunk)
        normed, inv_scale = norm_forward(tok[token_rows, :].astype(F32) + (attention + bb_ref[0:1, :]))
        n_one[rows, :] = normed
        scale_one[rows, :] = inv_scale
        value = normed * ng_ref[0:1, :] + ns_ref[0:1, :]
        hid[rows, :] = value
        hid_low[rows, :] = value.astype(BF16)

    load_wup.wait()
    load_wdn.wait()
    send_part = []
    for i in range(chunks):
        rows = slice(i * chunk, (i + 1) * chunk)
        for b in range(2):
            core = c if b == 0 else 1 - c
            if i == 0 and b == 1:
                send_wup.wait_recv()
            for n in range(tiles):
                cols = slice(n * tile, (n + 1) * tile)
                pre_act = dot_nn(hid_low[rows, :], wup[core, :, cols]) + small[core, 0:1, cols]
                value, slope = gelu_parts(pre_act)
                act_low[b, rows, cols] = value.astype(BF16)
                d_gelu[b, rows, cols] = slope
            if i == 0 and b == 1:
                send_wdn.wait_recv()
            product = dot_nn(act_low[b, rows, :], wdn[core])
            if b == 0:
                acc[...] = product
            else:
                parts[x, rows, :] = (acc[...] + product).astype(BF16)
        send_part.append(remote.start(parts.at[x, rows], parts.at[x, rows], x_dev))

    hid_tr[...] = jnp.transpose(hid_low[...])
    for k in range(groups - 1):
        send_cnt_z[k].wait_recv()
    item_count = cnt_s[...]
    for k in range(groups - 1):
        item_count = item_count + cnt_z[k]
    inv_count = 1.0 / item_count[0:1, 0:1]

    local_first = first_col[:, 0:1] - c * half
    picked = jnp.zeros((slots, width), F32)
    for i in range(chunks):
        rows = slice(i * chunk, (i + 1) * chunk)
        send_part[i].wait_recv()
        branch = parts[0, rows, :].astype(F32) + parts[1, rows, :].astype(F32)
        normed, inv_scale = norm_forward(hid[rows, :] + (branch + bb_ref[1:2, :]))
        n_two[rows, :] = normed
        scale_two[rows, :] = inv_scale
        low = (normed * ng_ref[1:2, :] + ns_ref[1:2, :]).astype(BF16)
        out_low[rows, :] = low
        places = lax.broadcasted_iota(jnp.int32, (slots, chunk), 1) + i * chunk
        picked = picked + dot_nn((places == local_first).astype(F32).astype(BF16), low)
    send_out = remote.start(out_low, bout_hbm.at[own_rows], core_dev)
    store_out = loads.start(out_low, bout_hbm.at[own_rows])

    load_pool.wait()
    picked_low = picked.astype(BF16)
    pooled = jnp.tanh(dot_nn(picked_low, wpool[...]) + pb_ref[...])
    pooled_low = pooled.astype(BF16)
    classes = wcls_ref.shape[0]
    class_rows = wcls_ref[...].astype(F32)
    class_pad = jnp.concatenate([class_rows, jnp.zeros((16 - classes, width), F32)], axis=0)
    class_lane = lax.broadcasted_iota(jnp.int32, (slots, 16), 1)
    class_bias = jnp.zeros((slots, 16), F32)
    for k in range(classes):
        class_bias = class_bias + jnp.where(class_lane == k, cb_ref[0, k], 0.0)
    logits = jnp.where(class_lane < classes, dot_nt(pooled_low, class_pad.astype(BF16)) + class_bias, masked_score)
    shifted = logits - jnp.max(logits, axis=1, keepdims=True)
    log_probs = shifted - jnp.log(jnp.sum(jnp.exp(shifted), axis=1, keepdims=True))
    class_probs = jnp.exp(log_probs)
    label_hot = jnp.where(class_lane == lab_col[:, 0:1], 1.0, 0.0)
    owned = jnp.where((local_first >= 0) & (local_first < half), live_all[:, 0:1], 0.0)
    item_ce = -jnp.sum(label_hot * log_probs, axis=1, keepdims=True) * owned
    item_ent = -jnp.sum(class_probs * log_probs, axis=1, keepdims=True) * owned
    d_logits = (class_probs - label_hot) * (owned * inv_count)
    d_pooled = jnp.zeros((slots, width), F32)
    for k in range(classes):
        d_pooled = d_pooled + d_logits[:, k : k + 1] * class_rows[k : k + 1, :]
        vec[7 + k : 8 + k, :] = col_sum(d_logits[:, k : k + 1] * pooled_low.astype(F32))
    d_pre = (d_pooled * (1.0 - pooled * pooled)).astype(BF16)
    vec[6:7, :] = col_sum(d_pre.astype(F32))
    lane = lax.broadcasted_iota(jnp.int32, (1, 128), 1)
    vec[10:11, 0:128] = jnp.where(lane == 0, col_sum(item_ce), 0.0) + jnp.where(lane == 1, col_sum(item_ent), 0.0)
    vec[10:11, 128:144] = col_sum(d_logits)
    items[0] = picked_low
    items[1] = d_pre
    send_items = remote.start(items, items_c, core_dev)
    d_picked = dot_nt(d_pre, wpool[...])
    d_high = d_picked.astype(BF16)
    d_both = jnp.concatenate([d_high, (d_picked - d_high.astype(F32)).astype(BF16)], axis=0)
    lane_item = lax.broadcasted_iota(jnp.int32, (1, 2 * slots), 1)
    first_row = jnp.zeros((1, 2 * slots), jnp.int32)
    for i in range(slots):
        first_row = first_row + jnp.where((lane_item == i) | (lane_item == i + slots), firsts[i], 0)

    load_cot.wait()
    gain_two = shift_two = bias_two = None
    up_sums = [[None] * tiles, [None] * tiles]
    send_part_b = []
    for i in range(chunks):
        rows = slice(i * chunk, (i + 1) * chunk)
        places = lax.broadcasted_iota(jnp.int32, (chunk, 2 * slots), 0) + (c * half + i * chunk)
        spread = dot_nn((places == first_row).astype(F32).astype(BF16), d_both)
        token_place = lax.broadcasted_iota(jnp.int32, (chunk, 1), 0) + (c * half + i * chunk)
        live = jnp.where(token_place < total, 1.0, 0.0)
        d_output = cot[rows, :].astype(F32) * live + spread
        normed = n_two[rows, :]
        gain_sum, shift_sum = col_sum(d_output * normed), col_sum(d_output)
        d_second = norm_backward(d_output, normed, scale_two[rows, :], ng_ref[1:2, :])
        bias_sum = col_sum(d_second)
        gain_two = gain_sum if i == 0 else gain_two + gain_sum
        shift_two = shift_sum if i == 0 else shift_two + shift_sum
        bias_two = bias_sum if i == 0 else bias_two + bias_sum
        d_sec[rows, :] = d_second
        d_br[rows, :] = d_second.astype(BF16)
        for b in range(2):
            core = c if b == 0 else 1 - c
            for n in range(tiles):
                cols = slice(n * tile, (n + 1) * tile)
                d_act = dot_nt(d_br[rows, :], wdn[core, cols, :])
                low = (d_act * d_gelu[b, rows, cols]).astype(BF16)
                d_pre_low[b, rows, cols] = low
                up_sum = col_sum(low.astype(F32))
                up_sums[b][n] = up_sum if i == 0 else up_sums[b][n] + up_sum
            product = dot_nt(d_pre_low[b, rows, :], wup[core])
            if b == 0:
                acc[...] = product
            else:
                parts_b[x, rows, :] = (acc[...] + product).astype(BF16)
        send_part_b.append(remote.start(parts_b.at[x, rows], parts_b.at[x, rows], x_dev))
    vec[1:2, :] = bias_two
    vec[3:4, :] = gain_two
    vec[5:6, :] = shift_two
    vec[pl.ds(11 + c, 1), :] = jnp.concatenate(up_sums[0], axis=1)
    vec[pl.ds(12 - c, 1), :] = jnp.concatenate(up_sums[1], axis=1)

    def place_blocks(store, product_of):
        for n in range(tiles):
            cols = slice(n * tile, (n + 1) * tile)
            product = product_of(cols)
            for j in range(n_dp):
                store(j % 2, j // 2, cols, product[j * shard : (j + 1) * shard, :])

    def fill_send(block, product_of):
        def store(low_index, high_index, cols, value):
            g_send[block, low_index, high_index, :, cols] = value.astype(BF16)

        place_blocks(store, product_of)
        return remote.start(g_send.at[block], g_recv.at[block], core_dev)

    def fill_own(block, product_of):
        def store(low_index, high_index, cols, value):
            g_own[block, low_index, high_index, :, cols] = value

        place_blocks(store, product_of)

    def start_y(block, core_copy):
        core_copy.wait_recv()
        copies = []
        for k in list(range(1, groups)) + [0]:
            other = lax.rem(h + k, groups)
            y_send[block, k] = (g_own[block, 1 - y, other] + g_recv[block, 1 - y, other].astype(F32)).astype(BF16)
            copies.append(remote.start(y_send.at[block, k], y_recv.at[block, k], y_dev))
        return copies

    def own_y_sum(block, k):
        other = lax.rem(h + k, groups)
        return (
            g_own[block, y, other] + g_recv[block, y, other].astype(F32) + y_recv[block, k].astype(F32)
        )

    def start_z(block, k, copy):
        copy.wait_recv()
        z_send[block, k - 1] = own_y_sum(block, k).astype(BF16)
        return remote.start(z_send.at[block, k - 1], z_recv.at[block, k - 1], z_dev(k))

    def finish_z(block, y_copies, z_copies, out):
        y_copies[groups - 1].wait_recv()
        result = own_y_sum(block, 0)
        for k in range(1, groups):
            z_copies[k - 1].wait_recv()
            result = result + z_recv[block, k - 1].astype(F32)
        g_fin[block] = result
        return loads.start(g_fin.at[block], out)

    DOWN, UP, QKVO = 0, 1, 2
    d_br_tr[...] = jnp.transpose(d_br[...])
    core_down = fill_send(DOWN, lambda cols: dot_nn(d_br_tr[...], act_low[1, :, cols]))
    core_up = fill_send(UP, lambda cols: dot_nn(hid_tr[...], d_pre_low[1, :, cols]))
    fill_own(DOWN, lambda cols: dot_nn(d_br_tr[...], act_low[0, :, cols]))
    y_down = start_y(DOWN, core_down)
    fill_own(UP, lambda cols: dot_nn(hid_tr[...], d_pre_low[0, :, cols]))
    y_up = start_y(UP, core_up)

    send_items.wait_recv()
    item_slots = (h * 2 + y) * slots
    own_items = pl.ds(pl.multiple_of(item_slots, slots), slots)
    for part in range(2):
        picked_t[part, own_items, :] = items[part] + items_c[part]
    send_items_y = [
        remote.start(picked_t.at[part, own_items], picked_t.at[part, own_items], y_dev) for part in range(2)
    ]

    gain_one = shift_one = bias_one = None
    for i in range(chunks):
        rows = slice(i * chunk, (i + 1) * chunk)
        send_part_b[i].wait_recv()
        d_hidden = parts_b[0, rows, :].astype(F32) + parts_b[1, rows, :].astype(F32) + d_sec[rows, :]
        normed = n_one[rows, :]
        gain_sum, shift_sum = col_sum(d_hidden * normed), col_sum(d_hidden)
        gradient = norm_backward(d_hidden, normed, scale_one[rows, :], ng_ref[0:1, :])
        bias_sum = col_sum(gradient)
        gain_one = gain_sum if i == 0 else gain_one + gain_sum
        shift_one = shift_sum if i == 0 else shift_one + shift_sum
        bias_one = bias_sum if i == 0 else bias_one + bias_sum
        d_first[rows, :] = gradient
        d_att[rows, :] = gradient.astype(BF16)
    vec[0:1, :] = bias_one
    vec[2:3, :] = gain_one
    vec[4:5, :] = shift_one

    chip_out = jnp.concatenate([wo[2 * x], wo[2 * x + 1]], axis=0)
    d_ctx[...] = dot_nt(chip_out, d_att[...]).astype(BF16)
    d_att_tr[...] = jnp.transpose(d_att[...])

    for pair in range(heads // 2):
        pair_rows = slice(pair * 128, (pair + 1) * 128)
        for side in range(2):
            head = 2 * pair + side
            head_rows = slice(head * HD, (head + 1) * HD)
            core, place = head // (heads // 2), (head % (heads // 2)) * HD
            d_probs = dot_nn(v_nt[:, pair_rows], half_of(d_ctx[pair_rows, :], side))
            weights = probs[head]
            delta = col_sum(weights * d_probs)
            d_scores = (weights * (d_probs - delta)).astype(BF16)
            d_value = dot_nt(d_ctx[head_rows, :], weights.astype(BF16))
            d_key = dot_nt(q_tr[head_rows, :], d_scores) * inv_root
            d_query = dot_nn(k_tr[head_rows, :], d_scores) * inv_root
            d_qkv[core, place : place + HD, :] = d_query.astype(BF16)
            for part, value in ((0, d_key), (1, d_value)):
                part_rows = slice(part * local_width + place, part * local_width + place + HD)
                for side_half in range(2):
                    lanes = slice(side_half * half, (side_half + 1) * half)
                    d_kv_f32[side_half, core, part_rows, :] = value[:, lanes]
                    d_kv_send[side_half, core, part_rows, :] = value[:, lanes].astype(BF16)
    send_kv = remote.start(d_kv_send.at[1 - c], d_kv_recv, core_dev)

    z_down = [start_z(DOWN, k, y_down[k - 1]) for k in range(1, groups)]
    for part in range(2):
        send_items_y[part].wait_recv()
    both_items = pl.ds(pl.multiple_of(h * 2 * slots, 2 * slots), 2 * slots)
    send_items_z = [
        remote.start(picked_t.at[part, both_items], picked_t.at[part, both_items], z_dev(k))
        for k in range(1, groups)
        for part in range(2)
    ]

    send_kv.wait_recv()
    for core in range(2):
        d_qkv[core, local_width:, :] = (d_kv_f32[c, core] + d_kv_recv[core].astype(F32)).astype(BF16)

    send_part_c = []
    for i in range(chunks):
        rows = slice(i * chunk, (i + 1) * chunk)
        partial_sum = dot_tn(d_qkv[0, :, rows], wt[0]) + dot_tn(d_qkv[1, :, rows], wt[1])
        parts_c[x, rows, :] = partial_sum.astype(BF16)
        send_part_c.append(remote.start(parts_c.at[x, rows], parts_c.at[x, rows], x_dev))

    def fill_qkvo(core, out, dtype):
        context_rows = pl.ds(pl.multiple_of(core * local_width, local_width), local_width)
        first_part = dot_nt(tok_tr[...], d_qkv[core])
        second_part = dot_nt(d_att_tr[...], ctx_all[x, context_rows, :])
        both = jnp.concatenate([first_part, second_part], axis=1).astype(dtype)
        for j in range(n_dp):
            out[QKVO, j % 2, j // 2] = both[j * shard : (j + 1) * shard, :]

    fill_qkvo(1 - c, g_send, BF16)
    core_qkvo = remote.start(g_send.at[QKVO], g_recv.at[QKVO], core_dev)
    fill_qkvo(c, g_own, F32)
    ones = jnp.ones((8, half), BF16)
    sums = [dot_nt(ones, d_qkv[core])[0:1, :] for core in range(2)]
    vec[13:14, :] = jnp.concatenate(
        [s[:, :local_width] for s in sums] + [s[:, 2 * local_width :] for s in sums], axis=1
    )
    send_vec = remote.start(vec, vec_c, core_dev)
    y_qkvo = start_y(QKVO, core_qkvo)
    send_vec.wait_recv()
    vec_s[...] = vec[...] + vec_c[...]
    send_vec_y = remote.start(vec_s, vec_y, y_dev)

    z_up = [start_z(UP, k, y_up[k - 1]) for k in range(1, groups)]

    for i in range(chunks):
        rows = slice(i * chunk, (i + 1) * chunk)
        send_part_c[i].wait_recv()
        total_grad = parts_c[0, rows, :].astype(F32) + parts_c[1, rows, :].astype(F32) + d_first[rows, :]
        gt_low[rows, :] = total_grad.astype(BF16)
    send_gt = remote.start(gt_low, gtok_hbm.at[own_rows], core_dev)
    store_gt = loads.start(gt_low, gtok_hbm.at[own_rows])

    for copy in send_items_z:
        copy.wait_recv()
    pool_all = dot_tn(picked_t[0], picked_t[1])
    pool_fin[...] = pool_all
    store_pool = loads.start(pool_fin.at[pl.ds(pl.multiple_of(dp * shard, 8), shard)], gpool_hbm)

    store_down = finish_z(DOWN, y_down, z_down, gdn_hbm)
    send_vec_y.wait_recv()
    vec_z[h] = vec_s[...] + vec_y[...]
    send_vec_z = [remote.start(vec_z.at[h], vec_z.at[h], z_dev(k)) for k in range(1, groups)]
    z_qkvo = [start_z(QKVO, k, y_qkvo[k - 1]) for k in range(1, groups)]
    store_up = finish_z(UP, y_up, z_up, gup_hbm)
    for copy in send_vec_z:
        copy.wait_recv()
    vec_total = vec_z[0]
    for k in range(1, groups):
        vec_total = vec_total + vec_z[k]
    vec_fin[...] = vec_total
    vec_fin[14:15, 0:128] = item_count[0:1, :]
    store_vec = loads.start(vec_fin, vec_hbm)
    store_qkvo = finish_z(QKVO, y_qkvo, z_qkvo, gqkvo_hbm)

    send_out.wait_recv()
    send_gt.wait_recv()
    for store in (store_out, store_gt, store_pool, store_down, store_up, store_vec, store_qkvo):
        store.wait()
    remote.finish()


def place_kernel(
    n_dp,
    bout_in,
    gtok_in,
    gqkvo_in,
    gup_in,
    gdn_in,
    gpool_in,
    vec_in,
    bout,
    gtok,
    loss,
    entropy,
    gqkv,
    gqv,
    gout,
    gbranch,
    ggain,
    gshift,
    gup,
    gupb,
    gdn,
    gpool,
    gpoolb,
    gclass,
    gclassb,
    sems,
):
    copies = []
    for i, (src, dst) in enumerate(
        ((bout_in, bout), (gtok_in, gtok), (gup_in, gup), (gdn_in, gdn), (gpool_in, gpool))
    ):
        copy = pltpu.make_async_copy(src, dst, sems.at[i])
        copy.start()
        copies.append(copy)
    dp = lax.axis_index("dp")
    c = lax.rem(lax.axis_index("tensor"), 2)
    width = vec_in.shape[1]
    shard = width // n_dp
    local_width = gout.shape[0]
    for part in range(3):
        gqkv[part] = gqkvo_in[:, part * local_width : (part + 1) * local_width]
    gout[...] = jnp.transpose(gqkvo_in[:, 3 * local_width :])
    sums = vec_in[...]
    mine = pltpu.roll(sums, lax.rem(width - dp * shard, width), axis=1)
    gbranch[...] = mine[0:2, :shard]
    ggain[...] = mine[2:4, :shard]
    gshift[...] = mine[4:6, :shard]
    gpoolb[...] = mine[6:7, :shard]
    gclass[...] = mine[7 : 7 + gclass.shape[0], :shard]
    gupb[...] = jnp.where(c == 0, mine[11:12, :shard], mine[12:13, :shard])
    small = local_width // n_dp
    quarter = pltpu.roll(sums, lax.rem(width - (c * local_width + dp * small), width), axis=1)
    gqv[0:1, :] = quarter[13:14, :small]
    gqv[1:2, :] = quarter[13:14, 2 * local_width : 2 * local_width + small]
    inv_count = 1.0 / sums[14:15, 0:1]
    loss[...] = sums[10:11, 0:1] * inv_count
    entropy[...] = sums[10:11, 1:2] * inv_count
    gclassb[...] = sums[10:11, 128 : 128 + gclassb.shape[1]]
    for copy in copies:
        copy.wait()


def on_device(
    n_dp,
    tokens,
    cotangent,
    lengths,
    labels,
    w_qkv,
    qv_bias,
    w_out,
    branch_bias,
    norm_gain,
    norm_shift,
    w_up,
    up_bias,
    w_down,
    w_pool,
    pool_bias,
    w_class,
    class_bias,
):
    token_count, width = tokens.shape
    local_width = w_out.shape[0]
    chip_width = 2 * local_width
    hidden = w_up.shape[1]
    classes = w_class.shape[1]
    slots = lengths.shape[1]
    groups = n_dp // 2
    shard = width // n_dp
    half = token_count // 2
    heads = chip_width // HD
    assert hidden == width and 4 * local_width == width and lengths.shape[0] == 1
    shape = jax.ShapeDtypeStruct
    anywhere = pl.BlockSpec(memory_space=pl.ANY)
    vmem = pl.BlockSpec(memory_space=pltpu.VMEM)
    smem = pl.BlockSpec(memory_space=pltpu.SMEM)
    block = (2, groups, shard, width)
    copies = remote_copy_count(groups)
    V = pltpu.VMEM
    scratch = [
        V((token_count, width), BF16),
        V((half, width), BF16),
        V((2, 3 * local_width, width), BF16),
        V((4, local_width, width), BF16),
        V((2, width, hidden), BF16),
        V((2, hidden, width), BF16),
        V((width, width), BF16),
        V((2, 8, width), F32),
        V((token_count, half), F32),
        V((token_count, chip_width), BF16),
        V((token_count, chip_width), BF16),
        V((chip_width, token_count), BF16),
        V((chip_width, token_count), BF16),
        V((chip_width, half), BF16),
        V((heads, token_count, half), F32),
        V((2, chip_width, half), BF16),
        V((half, width), F32),
        V((half, width), BF16),
        V((width, half), BF16),
        V((width, half), BF16),
        V((half, width), F32),
        V((half, width), F32),
        V((half, 1), F32),
        V((half, 1), F32),
        V((2, half, hidden), BF16),
        V((2, half, hidden), F32),
        V((128, width), F32),
        V((2, half, width), BF16),
        V((2, half, width), BF16),
        V((2, half, width), BF16),
        V((half, width), BF16),
        V((half, width), F32),
        V((half, width), BF16),
        V((width, half), BF16),
        V((2, half, hidden), BF16),
        V((half, width), F32),
        V((half, width), BF16),
        V((width, half), BF16),
        V((chip_width, half), BF16),
        V((2, 2, 2 * local_width, half), F32),
        V((2, 2, 2 * local_width, half), BF16),
        V((2, 2 * local_width, half), BF16),
        V((2, 3 * local_width, half), BF16),
        V((half, width), BF16),
        V((3,) + block, BF16),
        V((3,) + block, BF16),
        V((3,) + block, F32),
        V((3, groups, shard, width), BF16),
        V((3, groups, shard, width), BF16),
        V((3, groups - 1, shard, width), BF16),
        V((3, groups - 1, shard, width), BF16),
        V((3, shard, width), F32),
        V((width, width), F32),
        V((2, slots, width), BF16),
        V((2, slots, width), BF16),
        V((2, n_dp * slots, width), BF16),
        V((VEC_ROWS, width), F32),
        V((VEC_ROWS, width), F32),
        V((VEC_ROWS, width), F32),
        V((VEC_ROWS, width), F32),
        V((groups, VEC_ROWS, width), F32),
        V((VEC_ROWS, width), F32),
        V((8, 128), F32),
        V((8, 128), F32),
        V((8, 128), F32),
        V((groups - 1, 8, 128), F32),
        pltpu.SemaphoreType.DMA((20,)),
        pltpu.SemaphoreType.DMA((copies,)),
        pltpu.SemaphoreType.DMA((copies,)),
    ]
    found = pl.pallas_call(
        partial(layer_kernel, n_dp),
        out_shape=[
            shape((token_count, width), BF16),
            shape((token_count, width), BF16),
            shape((shard, width), F32),
            shape((shard, width), F32),
            shape((shard, width), F32),
            shape((shard, width), F32),
            shape((VEC_ROWS, width), F32),
        ],
        in_specs=[
            anywhere,
            anywhere,
            smem,
            smem,
            anywhere,
            vmem,
            anywhere,
            vmem,
            vmem,
            vmem,
            anywhere,
            vmem,
            anywhere,
            anywhere,
            vmem,
            vmem,
            smem,
        ],
        out_specs=[anywhere] * 7,
        scratch_shapes=scratch,
        compiler_params=pltpu.CompilerParams(
            collective_id=0, has_side_effects=True, vmem_limit_bytes=62 * 1024 * 1024
        ),
        name="layer",
    )(
        tokens,
        cotangent,
        lengths,
        labels,
        jnp.transpose(w_qkv, (1, 2, 0)).reshape(3 * local_width, width),
        qv_bias,
        w_out,
        branch_bias,
        norm_gain,
        norm_shift,
        w_up,
        up_bias.reshape(1, hidden),
        w_down,
        w_pool,
        pool_bias.reshape(1, width),
        w_class.T,
        class_bias.reshape(1, classes),
    )
    small = local_width // n_dp
    placed = pl.pallas_call(
        partial(place_kernel, n_dp),
        out_shape=[
            shape((token_count, width), BF16),
            shape((token_count, width), BF16),
            shape((1, 1), F32),
            shape((1, 1), F32),
            shape((3, shard, local_width), F32),
            shape((2, small), F32),
            shape((local_width, shard), F32),
            shape((2, shard), F32),
            shape((2, shard), F32),
            shape((2, shard), F32),
            shape((shard, hidden), F32),
            shape((1, hidden // n_dp), F32),
            shape((shard, hidden), F32),
            shape((shard, width), F32),
            shape((1, shard), F32),
            shape((classes, shard), F32),
            shape((1, classes), F32),
        ],
        in_specs=[anywhere, anywhere, vmem, anywhere, anywhere, anywhere, vmem],
        out_specs=[anywhere] * 2 + [vmem] * 8 + [anywhere, vmem, anywhere, anywhere] + [vmem] * 3,
        scratch_shapes=[pltpu.SemaphoreType.DMA((5,))],
        name="place",
    )(*found)
    (
        block_out,
        grad_tokens,
        loss,
        entropy,
        grad_qkv,
        grad_qv,
        grad_out,
        grad_branch,
        grad_gain,
        grad_shift,
        grad_up,
        grad_upb,
        grad_down,
        grad_pool,
        grad_poolb,
        grad_class,
        grad_classb,
    ) = placed
    return (
        block_out,
        grad_tokens,
        loss.reshape(()),
        entropy.reshape(()),
        jnp.transpose(grad_qkv, (1, 0, 2)),
        grad_qv,
        grad_out,
        grad_branch,
        grad_gain,
        grad_shift,
        grad_up,
        grad_upb.reshape(-1),
        grad_down.T,
        grad_pool,
        grad_poolb.reshape(-1),
        grad_class.T,
        grad_classb.reshape(-1),
    )


def solution(mesh):
    in_specs = (
        P("dp", None),
        P("dp", None),
        P("dp", None),
        P("dp", None),
        P(None, None, "tensor"),
        P(None, "tensor"),
        P("tensor", None),
        P(),
        P(),
        P(),
        P(None, "tensor"),
        P("tensor"),
        P("tensor", None),
        P(),
        P(),
        P(),
        P(),
    )
    out_specs = (
        P("dp", None),
        P("dp", None),
        P(),
        P(),
        P("dp", None, "tensor"),
        P(None, ("tensor", "dp")),
        P("tensor", "dp"),
        P(None, "dp"),
        P(None, "dp"),
        P(None, "dp"),
        P("dp", "tensor"),
        P(("tensor", "dp")),
        P("tensor", "dp"),
        P("dp", None),
        P("dp"),
        P("dp", None),
        P(),
    )
    return jax.shard_map(
        partial(on_device, mesh.shape["dp"]),
        mesh=mesh,
        in_specs=in_specs,
        out_specs=out_specs,
        check_vma=False,
    )
```

```python
from functools import partial

import jax
import jax.numpy as jnp
from jax import lax
from jax.experimental import pallas as pl
from jax.experimental.pallas import tpu as pltpu
from jax.sharding import PartitionSpec as P

HD = 64
MESH = pl.DeviceIdType.MESH
F32 = jnp.float32
BF16 = jnp.bfloat16
masked_score = -1e30
norm_eps = 1e-12
SQRT_HALF = 0.7071067811865476
PDF_SCALE = 0.3989422804014327
VEC_ROWS = 16
PLAN = (
    "I_y", "fdS", "fdO", "fuS", "fuO", "ln1b0", "FD_11", "FD_10", "I_r", "FU_11",
    "FU_10", "ln1b1", "dctx", "ab0", "ab1", "FD_01", "ab2", "FU_01", "ab3", "ab4",
    "SD_1", "ab5", "dattT", "FD_00", "SU_1", "dsum", "fqS", "SD_0", "dtok0", "I_q",
    "dtok1", "SU_0", "fqO", "qv", "V_y", "FU_00", "LD", "gtok0", "I_c", "FQ_11",
    "pool", "LU", "V_r", "gtok1", "FQ_10", "FQ_01", "ED", "SQ_1", "FQ_00", "SQ_0",
    "V_q", "EU", "LQ", "V_e", "EQ",
)
VMEM_LIMIT = 56 * 1024 * 1024


def dot_nn(a, b):
    return lax.dot_general(a, b, (((1,), (0,)), ((), ())), preferred_element_type=F32)


def dot_nt(a, b):
    return lax.dot_general(a, b, (((1,), (1,)), ((), ())), preferred_element_type=F32)


def dot_tn(a, b):
    return lax.dot_general(a, b, (((0,), (0,)), ((), ())), preferred_element_type=F32)


def row_mean(v):
    return jnp.sum(v, axis=1, keepdims=True) * (1.0 / v.shape[1])


def col_sum(v):
    return jnp.sum(v, axis=0, keepdims=True)


def norm_forward(values):
    centered = values - row_mean(values)
    inv_scale = lax.rsqrt(row_mean(centered * centered) + norm_eps)
    return centered * inv_scale, inv_scale


def norm_backward(gradient, normed, inv_scale, gain_row):
    scaled = gradient * gain_row
    inner = scaled - row_mean(scaled) - normed * row_mean(scaled * normed)
    return inner * inv_scale


def gelu_parts(pre_act):
    cdf = 0.5 * (1.0 + lax.erf(pre_act * SQRT_HALF))
    pdf = PDF_SCALE * jnp.exp(-0.5 * pre_act * pre_act)
    return pre_act * cdf, cdf + pre_act * pdf


class Stop(Exception):
    pass


STOP = None


def mark(name):
    if STOP is not None and name == STOP:
        raise Stop()


class Tracked:
    def __init__(self, copy):
        self.copy, self.received = copy, False

    def wait_recv(self):
        if not self.received:
            self.received = True
            self.copy.wait_recv()

    def wait_send(self):
        self.copy.wait_send()


class Copies:
    def __init__(self, send_sems, recv_sems):
        self.send_sems, self.recv_sems, self.used, self.open = send_sems, recv_sems, 0, []

    def start(self, src, dst, device):
        copy = pltpu.make_async_remote_copy(
            src_ref=src,
            dst_ref=dst,
            send_sem=self.send_sems.at[self.used],
            recv_sem=self.recv_sems.at[self.used],
            device_id=device,
            device_id_type=MESH,
        )
        self.used += 1
        copy.start()
        copy = Tracked(copy)
        self.open.append(copy)
        return copy

    def finish(self):
        for copy in self.open:
            copy.wait_send()


class Loads:
    def __init__(self, sems):
        self.sems, self.used = sems, 0

    def start(self, src, dst):
        copy = pltpu.make_async_copy(src, dst, self.sems.at[self.used])
        self.used += 1
        copy.start()
        return copy


def remote_copy_count(pairs):
    return 40 + 3 * (2 + 4 * pairs) + 4 * pairs


def layer_kernel(
    n_dp,
    tok_hbm,
    cot_hbm,
    len_ref,
    lab_ref,
    wqkv_hbm,
    qvb_ref,
    wout_hbm,
    bb_ref,
    ng_ref,
    ns_ref,
    wup_hbm,
    upb_ref,
    wdn_hbm,
    wpool_hbm,
    pb_ref,
    wcls_ref,
    cb_ref,
    bout_out,
    gtok_out,
    gqkvo_out,
    gup_out,
    gdn_out,
    gpool_out,
    vec_out,
    tok,
    cot,
    wt,
    wo,
    wup,
    wdn,
    wpool,
    up_bias,
    bias_mask,
    k_pad,
    v_pad,
    k_tr,
    v_tr,
    q_pad,
    q_away,
    probs,
    ctx,
    hid,
    hid_low,
    hid_tr,
    tok_tr,
    n_one,
    scale_one,
    act_low,
    d_gelu,
    acc,
    parts,
    d_sec,
    d_br,
    d_br_tr,
    d_pre_low,
    d_first,
    d_att,
    d_att_tr,
    d_ctx,
    d_kv_f32,
    d_kv_send,
    d_kv_recv,
    d_qkv,
    g_send,
    g_recv,
    g_own,
    first_send,
    first_recv,
    second_send,
    second_recv,
    last_send,
    last_recv,
    pool_fin,
    items,
    items_c,
    item_all,
    vec,
    vec_c,
    vec_s,
    vec_y,
    vec_t,
    vec_r,
    vec_q,
    cnt,
    cnt_y,
    cnt_s,
    cnt_r,
    cnt_q,
    load_sems,
    send_sems,
    recv_sems,
):
    pairs = n_dp // 4
    dp = lax.axis_index("dp")
    me = lax.axis_index("tensor")
    x = me // 2
    c = lax.rem(me, 2)
    y = lax.rem(dp, 2)
    r = lax.rem(dp // 2, 2)
    q = dp // 4
    core_dev = (dp, me + 1 - 2 * c)
    x_dev = (dp, 2 * (1 - x) + c)
    y_dev = (dp + 1 - 2 * y, me)
    r_dev = (dp + 2 - 4 * r, me)

    def q_of(k):
        return lax.rem(q + k, pairs)

    def q_dev(k):
        return (q_of(k) * 4 + r * 2 + y, me)

    away = range(1, pairs)
    token_count, width = tok.shape
    half = token_count // 2
    local_width = wo.shape[1]
    heads = local_width // HD
    slots = len_ref.shape[1]
    shard = width // n_dp
    chunk = 128
    chunks = half // chunk
    tile = 256
    tiles = width // tile
    own_rows = pl.ds(pl.multiple_of(c * half, half), half)
    away_rows = pl.ds(pl.multiple_of((1 - c) * half, half), half)

    barrier = pltpu.get_barrier_semaphore()
    peers = [core_dev, x_dev, y_dev, r_dev] + [q_dev(k) for k in away]
    for peer in peers:
        pl.semaphore_signal(barrier, inc=1, device_id=peer, device_id_type=MESH)

    loads = Loads(load_sems)
    remote = Copies(send_sems, recv_sems)
    load_tok = loads.start(tok_hbm, tok)
    load_wt = loads.start(wqkv_hbm, wt.at[c])
    load_wo = loads.start(wout_hbm, wo.at[c])
    load_wup = loads.start(wup_hbm, wup.at[c])
    load_wdn = loads.start(wdn_hbm, wdn.at[c])
    load_pool = loads.start(wpool_hbm, wpool)
    load_cot = loads.start(cot_hbm.at[own_rows], cot)

    lengths = [len_ref[0, i] for i in range(slots)]
    ends, total = [], 0
    for i in range(slots):
        total = total + lengths[i]
        ends.append(total)
    firsts = [jnp.minimum(ends[i] - lengths[i], token_count - 1) for i in range(slots)]
    key_place = lax.broadcasted_iota(jnp.int32, (token_count, 128), 0)
    query_place = lax.broadcasted_iota(jnp.int32, (8, half), 1) + c * half
    key_segment = jnp.zeros((token_count, 128), jnp.int32)
    query_segment = jnp.zeros((8, half), jnp.int32)
    for i in range(slots):
        key_segment = key_segment + (key_place >= ends[i]).astype(jnp.int32)
        query_segment = query_segment + (query_place >= ends[i]).astype(jnp.int32)
    for n in range(half // 128):
        cols = slice(n * 128, (n + 1) * 128)
        bias_mask[:, cols] = jnp.where(key_segment == query_segment[0:1, cols], 0.0, masked_score)
    item_row = lax.broadcasted_iota(jnp.int32, (slots, 128), 0)
    first_col = jnp.zeros((slots, 128), jnp.int32)
    len_col = jnp.zeros((slots, 128), jnp.int32)
    lab_col = jnp.zeros((slots, 128), jnp.int32)
    for i in range(slots):
        first_col = first_col + jnp.where(item_row == i, firsts[i], 0)
        len_col = len_col + jnp.where(item_row == i, lengths[i], 0)
        lab_col = lab_col + jnp.where(item_row == i, lab_ref[0, i], 0)
    live_all = jnp.where(len_col > 0, 1.0, 0.0)
    cnt[...] = jnp.broadcast_to(col_sum(live_all), cnt.shape)
    lane_item = lax.broadcasted_iota(jnp.int32, (1, 2 * slots), 1)
    first_row = jnp.zeros((1, 2 * slots), jnp.int32)
    for i in range(slots):
        first_row = first_row + jnp.where((lane_item == i) | (lane_item == i + slots), firsts[i], 0)

    up_bias[c] = jnp.broadcast_to(upb_ref[...].astype(F32).reshape(1, width), (8, width))
    vec[...] = jnp.zeros_like(vec)
    pad_rows = q_pad.shape[1] - local_width
    for b in range(2):
        q_pad[b, local_width:, :] = jnp.zeros((pad_rows, half), BF16)
        d_ctx[b, local_width:, :] = jnp.zeros((pad_rows, half), BF16)
        v_pad[b, :, local_width:] = jnp.zeros((token_count, pad_rows), BF16)

    def bias_cols(part, columns):
        row = qvb_ref[part : part + 1, :]
        block = jnp.transpose(jnp.broadcast_to(row, (128, local_width)))
        return jnp.concatenate([block] * (columns // 128), axis=1)

    load_tok.wait()
    load_wt.wait()
    rows_q, rows_k, rows_v = [slice(p * local_width, (p + 1) * local_width) for p in range(3)]
    query_bias = bias_cols(0, half)
    q_away[...] = (dot_nt(wt[c, rows_q, :], tok[away_rows, :]) + query_bias).astype(BF16)
    wide_k = jnp.concatenate([wt[c, rows_k, :], jnp.zeros((pad_rows, width), BF16)], axis=0)
    k_pad[c] = dot_nt(tok[...], wide_k).astype(BF16)
    v_tr[c] = (dot_nt(wt[c, rows_v, :], tok[...]) + bias_cols(1, token_count)).astype(BF16)
    q_pad[c, 0:local_width, :] = (dot_nt(wt[c, rows_q, :], tok[own_rows, :]) + query_bias).astype(BF16)

    pl.semaphore_wait(barrier, len(peers))
    mark("sends")
    send_q = remote.start(q_away, q_pad.at[c, pl.ds(0, local_width)], core_dev)
    send_k = remote.start(k_pad.at[c], k_pad.at[c], core_dev)
    send_v = remote.start(v_tr.at[c], v_tr.at[c], core_dev)
    send_wo = remote.start(wout_hbm, wo.at[c], core_dev)
    send_bias = remote.start(up_bias.at[c], up_bias.at[c], core_dev)
    send_wup = remote.start(wup_hbm, wup.at[c], core_dev)
    send_wdn = remote.start(wdn_hbm, wdn.at[c], core_dev)
    send_cnt_y = remote.start(cnt, cnt_y, y_dev)
    send_wt = remote.start(wqkv_hbm, wt.at[c], core_dev)

    half_row = lax.broadcasted_iota(jnp.int32, (128, half), 0) < HD
    inv_root = HD ** (-0.5)

    def half_of(block, i):
        if i == heads - 1 and i % 2 == 0:
            return block
        zero = jnp.zeros_like(block)
        return jnp.where(half_row, block, zero) if i % 2 == 0 else jnp.where(half_row, zero, block)

    def pair_of(i):
        return slice((i // 2) * 128, (i // 2 + 1) * 128)

    def attend(core):
        for i in range(heads):
            head_rows = slice(i * HD, (i + 1) * HD)
            scores = dot_nn(k_pad[core, :, pair_of(i)], half_of(q_pad[core, pair_of(i), :], i))
            scores = scores * inv_root + bias_mask[...]
            terms = jnp.exp(scores - jnp.max(scores, axis=0, keepdims=True))
            weights = terms * (1.0 / col_sum(terms))
            probs[core, i] = weights
            ctx[core, head_rows, :] = dot_nn(v_tr[core, head_rows, :], weights.astype(BF16)).astype(BF16)

    mark("attn_own")
    attend(c)
    send_q.wait_recv()
    send_k.wait_recv()
    send_v.wait_recv()
    mark("attn_other")
    attend(1 - c)
    mark("out")
    load_wo.wait()
    send_wo.wait_recv()

    def chunk_of(i):
        return slice(i * chunk, (i + 1) * chunk)

    def exchange(which, i):
        block = parts.at[which, x, chunk_of(i)]
        return remote.start(block, block, x_dev)

    def both_parts(which, i):
        return parts[which, 0, chunk_of(i), :].astype(F32) + parts[which, 1, chunk_of(i), :].astype(F32)

    ATT, FFN, HIDDEN, TOKEN = 0, 1, 2, 3
    send_att = []
    for i in range(chunks):
        rows = chunk_of(i)
        partial_sum = dot_tn(ctx[0, :, rows], wo[0]) + dot_tn(ctx[1, :, rows], wo[1])
        parts[ATT, x, rows, :] = partial_sum.astype(BF16)
        send_att.append(exchange(ATT, i))
    send_cnt_y.wait_recv()
    cnt_s[...] = cnt[...] + cnt_y[...]
    send_cnt_r = remote.start(cnt_s, cnt_r, r_dev)

    mark("transposes")
    for b in range(2):
        k_tr[b] = jnp.transpose(k_pad[b])[0:local_width, :]
        v_pad[b, :, 0:local_width] = jnp.transpose(v_tr[b])
    tok_tr[...] = jnp.transpose(tok[own_rows, :])

    mark("ffn_f")
    load_wup.wait()
    load_wdn.wait()
    send_ffn = []
    for i in range(chunks):
        rows = chunk_of(i)
        send_att[i].wait_recv()
        token_rows = pl.ds(pl.multiple_of(c * half + i * chunk, chunk), chunk)
        attention = both_parts(ATT, i) + bb_ref[0:1, :]
        normed, inv_scale = norm_forward(tok[token_rows, :].astype(F32) + attention)
        n_one[rows, :] = normed
        scale_one[rows, :] = inv_scale
        value = normed * ng_ref[0:1, :] + ns_ref[0:1, :]
        hid[rows, :] = value
        hid_low[rows, :] = value.astype(BF16)
        for b in range(2):
            core = c if b == 0 else 1 - c
            if i == 0 and b == 1:
                send_bias.wait_recv()
                send_wup.wait_recv()
            for n in range(tiles):
                cols = slice(n * tile, (n + 1) * tile)
                pre_act = dot_nn(hid_low[rows, :], wup[core, :, cols]) + up_bias[core, 0:1, cols]
                value, slope = gelu_parts(pre_act)
                act_low[b, rows, cols] = value.astype(BF16)
                d_gelu[b, rows, cols] = slope
            if i == 0 and b == 1:
                send_wdn.wait_recv()
            product = dot_nn(act_low[b, rows, :], wdn[core])
            if b == 0:
                acc[...] = product
            else:
                parts[FFN, x, rows, :] = (acc[...] + product).astype(BF16)
        send_ffn.append(exchange(FFN, i))
        if i == 0:
            send_cnt_r.wait_recv()
            cnt_q[q] = cnt_s[...] + cnt_r[...]
            send_cnt_q = [remote.start(cnt_q.at[q], cnt_q.at[q], q_dev(k)) for k in away]

    mark("hid_tr")
    hid_tr[...] = jnp.transpose(hid_low[...])
    load_pool.wait()
    load_cot.wait()
    for copy in send_cnt_q:
        copy.wait_recv()
    item_count = cnt_q[0]
    for k in away:
        item_count = item_count + cnt_q[k]
    inv_count = 1.0 / item_count[0:1, 0:1]

    classes = wcls_ref.shape[0]
    class_rows = wcls_ref[...].astype(F32)
    class_pad = jnp.concatenate([class_rows, jnp.zeros((16 - classes, width), F32)], axis=0).astype(BF16)
    class_lane = lax.broadcasted_iota(jnp.int32, (slots, 16), 1)
    class_bias = jnp.zeros((slots, 16), F32)
    for k in range(classes):
        class_bias = class_bias + jnp.where(class_lane == k, cb_ref[0, k], 0.0)
    label_hot = jnp.where(class_lane == lab_col[:, 0:1], 1.0, 0.0)
    lane = lax.broadcasted_iota(jnp.int32, (1, 128), 1)

    def add_rows(first, value):
        vec[first : first + value.shape[0], 0 : value.shape[1]] += value

    mark("ln2")
    up_sums = [[None] * tiles, [None] * tiles]
    send_hidden = []
    for i in range(chunks):
        rows = chunk_of(i)
        place = c * half + i * chunk
        send_ffn[i].wait_recv()
        normed, inv_scale = norm_forward(hid[rows, :] + (both_parts(FFN, i) + bb_ref[1:2, :]))
        low = (normed * ng_ref[1:2, :] + ns_ref[1:2, :]).astype(BF16)
        bout_out[pl.ds(pl.multiple_of(place, chunk), chunk), :] = low

        local_first = first_col[:, 0:1] - place
        pick = (lax.broadcasted_iota(jnp.int32, (slots, chunk), 1) == local_first).astype(F32).astype(BF16)
        picked = dot_nn(pick, low).astype(BF16)
        pooled = jnp.tanh(dot_nn(picked, wpool[...]) + pb_ref[...].reshape(1, width))
        pooled_low = pooled.astype(BF16)
        logits = jnp.where(class_lane < classes, dot_nt(pooled_low, class_pad) + class_bias, masked_score)
        shifted = logits - jnp.max(logits, axis=1, keepdims=True)
        log_probs = shifted - jnp.log(jnp.sum(jnp.exp(shifted), axis=1, keepdims=True))
        class_probs = jnp.exp(log_probs)
        owned = jnp.where((local_first >= 0) & (local_first < chunk), live_all[:, 0:1], 0.0)
        item_ce = -jnp.sum(label_hot * log_probs, axis=1, keepdims=True) * owned
        item_ent = -jnp.sum(class_probs * log_probs, axis=1, keepdims=True) * owned
        d_logits = (class_probs - label_hot) * (owned * inv_count)
        d_pooled = jnp.zeros((slots, width), F32)
        for k in range(classes):
            d_pooled = d_pooled + d_logits[:, k : k + 1] * class_rows[k : k + 1, :]
            add_rows(7 + k, col_sum(d_logits[:, k : k + 1] * pooled_low.astype(F32)))
        d_pre = (d_pooled * (1.0 - pooled * pooled)).astype(BF16)
        add_rows(6, col_sum(d_pre.astype(F32)))
        add_rows(
            10, jnp.where(lane == 0, col_sum(item_ce), 0.0) + jnp.where(lane == 1, col_sum(item_ent), 0.0)
        )
        vec[10:11, 128:144] += col_sum(d_logits)
        if i == 0:
            items[0] = picked
            items[1] = d_pre
        else:
            items[0] += picked
            items[1] += d_pre
        if i == chunks - 1:
            send_items = remote.start(items.at[1 - c], items_c, core_dev)
        d_picked = dot_nt(d_pre, wpool[...])
        d_high = d_picked.astype(BF16)
        d_both = jnp.concatenate([d_high, (d_picked - d_high.astype(F32)).astype(BF16)], axis=0)

        token_place = lax.broadcasted_iota(jnp.int32, (chunk, 2 * slots), 0) + place
        spread = dot_nn((token_place == first_row).astype(F32).astype(BF16), d_both)
        live = jnp.where(token_place[:, 0:1] < total, 1.0, 0.0)
        d_output = cot[rows, :].astype(F32) * live + spread
        add_rows(3, col_sum(d_output * normed))
        add_rows(5, col_sum(d_output))
        d_second = norm_backward(d_output, normed, inv_scale, ng_ref[1:2, :])
        add_rows(1, col_sum(d_second))
        d_sec[rows, :] = d_second
        d_br[rows, :] = d_second.astype(BF16)
        for b in range(2):
            core = c if b == 0 else 1 - c
            for n in range(tiles):
                cols = slice(n * tile, (n + 1) * tile)
                d_act = dot_nt(d_br[rows, :], wdn[core, cols, :])
                low = (d_act * d_gelu[b, rows, cols]).astype(BF16)
                d_pre_low[b, rows, cols] = low
                up_sum = col_sum(low.astype(F32))
                up_sums[b][n] = up_sum if i == 0 else up_sums[b][n] + up_sum
            product = dot_nt(d_pre_low[b, rows, :], wup[core])
            if b == 0:
                acc[...] = product
            else:
                parts[HIDDEN, x, rows, :] = (acc[...] + product).astype(BF16)
        send_hidden.append(exchange(HIDDEN, i))
    vec[pl.ds(11 + c, 1), :] = jnp.concatenate(up_sums[0], axis=1)
    vec[pl.ds(12 - c, 1), :] = jnp.concatenate(up_sums[1], axis=1)
    send_out = remote.start(bout_out.at[own_rows], bout_out.at[own_rows], core_dev)

    DOWN, UP, QKVO = 0, 1, 2
    along = {DOWN: (r, y, r_dev, y_dev), UP: (y, r, y_dev, r_dev), QKVO: (y, r, y_dev, r_dev)}
    row_major = {DOWN: True, UP: False, QKVO: False}
    reach = {1: list(away), 0: [0]}
    slot_of = {(flip, k): (1 - flip) * pairs + (k - 1) % pairs for flip in range(2) for k in range(pairs)}
    sent = {}
    step = {}

    def store_blocks(out, block, cols, product):
        for j in range(n_dp):
            value = product[j * shard : (j + 1) * shard, :].astype(out.dtype)
            bits = (j % 2, (j // 2) % 2)
            if row_major[block]:
                bits = bits[::-1]
            out[block, bits[0], bits[1], j // 4, :, cols] = value

    def fill(out, block, product_of):
        for n in range(tiles):
            cols = slice(n * tile, (n + 1) * tile)
            store_blocks(out, block, cols, product_of(cols))

    def core_send(block):
        first = along[block][0]
        for name, side in (("away", 1 - first), ("kept", first)):
            sent[block, name] = remote.start(g_send.at[block, side], g_recv.at[block, side], core_dev)

    def after_core(block, name, first_value, second_value, q_index):
        sent[block, name].wait_recv()
        index = (block, first_value, second_value, q_index)
        return g_own[index] + g_recv[index].astype(F32)

    def first_step(block, flip, group):
        first, second, device, _ = along[block]
        for k in reach[group]:
            slot = slot_of[flip, k]
            value = after_core(block, "away", 1 - first, 1 - second if flip else second, q_of(k))
            first_send[block, slot] = value.astype(BF16)
            sent[block, 1, flip, k] = remote.start(first_send.at[block, slot], first_recv.at[block, slot], device)

    def first_sum(block, flip, k):
        first, second, _, _ = along[block]
        sent[block, 1, flip, k].wait_recv()
        value = after_core(block, "kept", first, 1 - second if flip else second, q_of(k))
        return value + first_recv[block, slot_of[flip, k]].astype(F32)

    def second_step(block, group):
        for k in reach[group]:
            second_send[block, k] = first_sum(block, 1, k).astype(BF16)
            sent[block, 2, k] = remote.start(second_send.at[block, k], second_recv.at[block, k], along[block][3])

    def second_sum(block, k):
        sent[block, 2, k].wait_recv()
        return first_sum(block, 0, k) + second_recv[block, k].astype(F32)

    def last_step(block):
        for k in away:
            last_send[block, k - 1] = second_sum(block, k).astype(BF16)
            sent[block, 3, k] = remote.start(last_send.at[block, k - 1], last_recv.at[block, k - 1], q_dev(k))

    def end_step(block, out):
        result = second_sum(block, 0)
        for k in away:
            sent[block, 3, k].wait_recv()
            result = result + last_recv[block, k - 1].astype(F32)
        out[...] = result

    for letter, block, out in (("D", DOWN, gdn_out), ("U", UP, gup_out), ("Q", QKVO, gqkvo_out)):
        for group in range(2):
            for flip in range(2):
                step["F%s_%d%d" % (letter, flip, group)] = partial(first_step, block, flip, group)
            step["S%s_%d" % (letter, group)] = partial(second_step, block, group)
        step["L" + letter] = partial(last_step, block)
        step["E" + letter] = partial(end_step, block, out)

    def fill_down_send():
        d_br_tr[...] = jnp.transpose(d_br[...])
        fill(g_send, DOWN, lambda cols: dot_nn(d_br_tr[...], act_low[1, :, cols]))
        core_send(DOWN)

    def fill_up_send():
        fill(g_send, UP, lambda cols: dot_nn(hid_tr[...], d_pre_low[1, :, cols]))
        core_send(UP)

    step["fdS"] = fill_down_send
    step["fdO"] = lambda: fill(g_own, DOWN, lambda cols: dot_nn(d_br_tr[...], act_low[0, :, cols]))
    step["fuS"] = fill_up_send
    step["fuO"] = lambda: fill(g_own, UP, lambda cols: dot_nn(hid_tr[...], d_pre_low[0, :, cols]))

    def item_rows(first, count):
        return pl.ds(pl.multiple_of(first * slots, count * slots), count * slots)

    def pass_items(name, rows, devices):
        sent[name] = [remote.start(item_all.at[c, rows], item_all.at[c, rows], device) for device in devices]

    def settle(name):
        for copy in sent[name]:
            copy.wait_recv()

    def items_y():
        send_items.wait_recv()
        item_all[c, item_rows(dp, 1), :] = items[c] + items_c[...]
        pass_items("items_y", item_rows(dp, 1), [y_dev])

    def items_r():
        settle("items_y")
        pass_items("items_r", item_rows(dp - y, 2), [r_dev])

    def items_q():
        settle("items_r")
        pass_items("items_q", item_rows(q * 4, 4), [q_dev(k) for k in away])

    def items_core():
        settle("items_q")
        sent["items_core"] = [remote.start(item_all.at[c], item_all.at[c], core_dev)]

    def pool():
        settle("items_core")
        pool_fin[...] = dot_tn(item_all[0], item_all[1])
        gpool_out[...] = pool_fin[pl.ds(pl.multiple_of(dp * shard, 8), shard), :]

    step.update(I_y=items_y, I_r=items_r, I_q=items_q, I_c=items_core, pool=pool)

    def norm_one_back(i):
        rows = chunk_of(i)
        send_hidden[i].wait_recv()
        d_hidden = both_parts(HIDDEN, i) + d_sec[rows, :]
        normed = n_one[rows, :]
        add_rows(2, col_sum(d_hidden * normed))
        add_rows(4, col_sum(d_hidden))
        gradient = norm_backward(d_hidden, normed, scale_one[rows, :], ng_ref[0:1, :])
        add_rows(0, col_sum(gradient))
        d_first[rows, :] = gradient
        d_att[rows, :] = gradient.astype(BF16)

    def context_back():
        for b in range(2):
            d_ctx[b, 0:local_width, :] = dot_nt(wo[b], d_att[...]).astype(BF16)

    def head_back(n):
        b, i = n // heads, n % heads
        head_rows = slice(i * HD, (i + 1) * HD)
        d_probs = dot_nn(v_pad[b, :, pair_of(i)], half_of(d_ctx[b, pair_of(i), :], i))
        weights = probs[b, i]
        delta = col_sum(weights * d_probs)
        d_scores = (weights * (d_probs - delta)).astype(BF16)
        d_value = dot_nt(d_ctx[b, head_rows, :], weights.astype(BF16))
        d_key = dot_nt(q_pad[b, head_rows, :], d_scores) * inv_root
        d_query = dot_nn(k_tr[b, head_rows, :], d_scores) * inv_root
        d_qkv[b, head_rows, :] = d_query.astype(BF16)
        for part, value in ((0, d_key), (1, d_value)):
            part_rows = slice(part * local_width + i * HD, part * local_width + (i + 1) * HD)
            for side in range(2):
                lanes = slice(side * half, (side + 1) * half)
                d_kv_f32[side, b, part_rows, :] = value[:, lanes]
                d_kv_send[side, b, part_rows, :] = value[:, lanes].astype(BF16)
        if n == 2 * heads - 1:
            sent["kv"] = remote.start(d_kv_send.at[1 - c], d_kv_recv, core_dev)

    def turn_attention():
        d_att_tr[...] = jnp.transpose(d_att[...])

    def join_cores():
        sent["kv"].wait_recv()
        for b in range(2):
            d_qkv[b, local_width:, :] = (d_kv_f32[c, b] + d_kv_recv[b].astype(F32)).astype(BF16)

    for i in range(chunks):
        step["ln1b%d" % i] = partial(norm_one_back, i)
    step["dctx"] = context_back
    for n in range(2 * heads):
        step["ab%d" % n] = partial(head_back, n)
    step["dattT"] = turn_attention
    step["dsum"] = join_cores

    def fill_qkvo(core, out):
        first_part = dot_nt(tok_tr[...], d_qkv[core])
        second_part = dot_nt(d_att_tr[...], ctx[core])
        store_blocks(out, QKVO, slice(0, width), jnp.concatenate([first_part, second_part], axis=1))

    def fill_qkvo_send():
        fill_qkvo(1 - c, g_send)
        core_send(QKVO)

    def token_part(i):
        send_wt.wait_recv()
        rows = chunk_of(i)
        partial_sum = dot_tn(d_qkv[0, :, rows], wt[0]) + dot_tn(d_qkv[1, :, rows], wt[1])
        parts[TOKEN, x, rows, :] = partial_sum.astype(BF16)
        sent["token", i] = exchange(TOKEN, i)

    def token_end(i):
        sent["token", i].wait_recv()
        rows = chunk_of(i)
        place = pl.ds(pl.multiple_of(c * half + i * chunk, chunk), chunk)
        gtok_out[place, :] = (both_parts(TOKEN, i) + d_first[rows, :]).astype(BF16)
        if i == chunks - 1:
            sent["gtok"] = remote.start(gtok_out.at[own_rows], gtok_out.at[own_rows], core_dev)

    step["fqS"] = fill_qkvo_send
    step["fqO"] = lambda: fill_qkvo(c, g_own)
    for i in range(chunks):
        step["dtok%d" % i] = partial(token_part, i)
        step["gtok%d" % i] = partial(token_end, i)

    def vec_core():
        ones = jnp.ones((8, half), BF16)
        sums = [dot_nt(ones, d_qkv[b])[0:1, :] for b in range(2)]
        columns = [v[:, :local_width] for v in sums] + [v[:, 2 * local_width :] for v in sums]
        vec[13:14, :] = jnp.concatenate(columns, axis=1)
        vec[14:15, 0:128] = item_count[0:1, :]
        sent["vec"] = remote.start(vec, vec_c, core_dev)

    def vec_along_y():
        sent["vec"].wait_recv()
        vec_s[...] = vec[...] + vec_c[...]
        sent["vec_y"] = remote.start(vec_s, vec_y, y_dev)

    def vec_along_r():
        sent["vec_y"].wait_recv()
        vec_t[...] = vec_s[...] + vec_y[...]
        sent["vec_r"] = remote.start(vec_t, vec_r, r_dev)

    def vec_along_q():
        sent["vec_r"].wait_recv()
        vec_q[q] = vec_t[...] + vec_r[...]
        sent["vec_q"] = [remote.start(vec_q.at[q], vec_q.at[q], q_dev(k)) for k in away]

    def vec_end():
        settle("vec_q")
        vec_total = vec_q[0]
        for k in away:
            vec_total = vec_total + vec_q[k]
        vec_out[...] = vec_total

    step.update(qv=vec_core, V_y=vec_along_y, V_r=vec_along_r, V_q=vec_along_q, V_e=vec_end)

    assert sorted(PLAN) == sorted(step)
    for name in PLAN:
        mark(name)
        step[name]()
    mark("finish")
    send_out.wait_recv()
    sent["gtok"].wait_recv()
    remote.finish()


def place_kernel(
    n_dp,
    bout_in,
    gtok_in,
    gqkvo_in,
    gup_in,
    gdn_in,
    gpool_in,
    vec_in,
    bout,
    gtok,
    loss,
    entropy,
    gqkv,
    gqv,
    gout,
    gbranch,
    ggain,
    gshift,
    gup,
    gupb,
    gdn,
    gpool,
    gpoolb,
    gclass,
    gclassb,
    sems,
):
    moves = ((bout_in, bout), (gtok_in, gtok), (gup_in, gup), (gdn_in, gdn), (gpool_in, gpool))
    copies = [pltpu.make_async_copy(src, dst, sems.at[i]) for i, (src, dst) in enumerate(moves)]
    for copy in copies:
        copy.start()
    dp = lax.axis_index("dp")
    c = lax.rem(lax.axis_index("tensor"), 2)
    width = vec_in.shape[1]
    shard = width // n_dp
    local_width = gout.shape[0]
    for part in range(3):
        gqkv[part] = gqkvo_in[:, part * local_width : (part + 1) * local_width]
    gout[...] = jnp.transpose(gqkvo_in[:, 3 * local_width :])
    sums = vec_in[...]
    mine = pltpu.roll(sums, lax.rem(width - dp * shard, width), axis=1)
    gbranch[...] = mine[0:2, :shard]
    ggain[...] = mine[2:4, :shard]
    gshift[...] = mine[4:6, :shard]
    gpoolb[...] = mine[6:7, :shard]
    gclass[...] = mine[7 : 7 + gclass.shape[0], :shard]
    gupb[...] = jnp.where(c == 0, mine[11:12, :shard], mine[12:13, :shard])
    small = local_width // n_dp
    quarter = pltpu.roll(sums, lax.rem(width - (c * local_width + dp * small), width), axis=1)
    gqv[0:1, :] = quarter[13:14, :small]
    gqv[1:2, :] = quarter[13:14, 2 * local_width : 2 * local_width + small]
    inv_count = 2.0 * n_dp / sums[14:15, 0:1]
    loss[...] = sums[10:11, 0:1] * inv_count
    entropy[...] = sums[10:11, 1:2] * inv_count
    gclassb[...] = sums[10:11, 128 : 128 + gclassb.shape[1]]
    for copy in copies:
        copy.wait()


def on_device(
    n_dp,
    tokens,
    cotangent,
    lengths,
    labels,
    w_qkv,
    qv_bias,
    w_out,
    branch_bias,
    norm_gain,
    norm_shift,
    w_up,
    up_bias,
    w_down,
    w_pool,
    pool_bias,
    w_class,
    class_bias,
):
    token_count, width = tokens.shape
    local_width = w_out.shape[0]
    hidden = w_up.shape[1]
    classes = w_class.shape[1]
    slots = lengths.shape[1]
    pairs = n_dp // 4
    shard = width // n_dp
    half = token_count // 2
    heads = local_width // HD
    padded = (local_width + 127) // 128 * 128
    assert hidden == width and 4 * local_width == width and lengths.shape[0] == 1
    shape = jax.ShapeDtypeStruct
    anywhere = pl.BlockSpec(memory_space=pl.ANY)
    vmem = pl.BlockSpec(memory_space=pltpu.VMEM)
    smem = pl.BlockSpec(memory_space=pltpu.SMEM)
    blocks = (3, 2, 2, pairs, shard, width)
    copies = remote_copy_count(pairs)
    V = pltpu.VMEM
    scratch = dict(
        tok=V((token_count, width), BF16),
        cot=V((half, width), BF16),
        wt=V((2, 3 * local_width, width), BF16),
        wo=V((2, local_width, width), BF16),
        wup=V((2, width, hidden), BF16),
        wdn=V((2, hidden, width), BF16),
        wpool=V((width, width), BF16),
        up_bias=V((2, 8, width), F32),
        bias_mask=V((token_count, half), F32),
        k_pad=V((2, token_count, padded), BF16),
        v_pad=V((2, token_count, padded), BF16),
        k_tr=V((2, local_width, token_count), BF16),
        v_tr=V((2, local_width, token_count), BF16),
        q_pad=V((2, padded, half), BF16),
        q_away=V((local_width, half), BF16),
        probs=V((2, heads, token_count, half), F32),
        ctx=V((2, local_width, half), BF16),
        hid=V((half, width), F32),
        hid_low=V((half, width), BF16),
        hid_tr=V((width, half), BF16),
        tok_tr=V((width, half), BF16),
        n_one=V((half, width), F32),
        scale_one=V((half, 1), F32),
        act_low=V((2, half, hidden), BF16),
        d_gelu=V((2, half, hidden), F32),
        acc=V((128, width), F32),
        parts=V((4, 2, half, width), BF16),
        d_sec=V((half, width), F32),
        d_br=V((half, width), BF16),
        d_br_tr=V((width, half), BF16),
        d_pre_low=V((2, half, hidden), BF16),
        d_first=V((half, width), F32),
        d_att=V((half, width), BF16),
        d_att_tr=V((width, half), BF16),
        d_ctx=V((2, padded, half), BF16),
        d_kv_f32=V((2, 2, 2 * local_width, half), F32),
        d_kv_send=V((2, 2, 2 * local_width, half), BF16),
        d_kv_recv=V((2, 2 * local_width, half), BF16),
        d_qkv=V((2, 3 * local_width, half), BF16),
        g_send=V(blocks, BF16),
        g_recv=V(blocks, BF16),
        g_own=V(blocks, F32),
        first_send=V((3, 2 * pairs, shard, width), BF16),
        first_recv=V((3, 2 * pairs, shard, width), BF16),
        second_send=V((3, pairs, shard, width), BF16),
        second_recv=V((3, pairs, shard, width), BF16),
        last_send=V((3, pairs - 1, shard, width), BF16),
        last_recv=V((3, pairs - 1, shard, width), BF16),
        pool_fin=V((width, width), F32),
        items=V((2, slots, width), BF16),
        items_c=V((slots, width), BF16),
        item_all=V((2, n_dp * slots, width), BF16),
        vec=V((VEC_ROWS, width), F32),
        vec_c=V((VEC_ROWS, width), F32),
        vec_s=V((VEC_ROWS, width), F32),
        vec_y=V((VEC_ROWS, width), F32),
        vec_t=V((VEC_ROWS, width), F32),
        vec_r=V((VEC_ROWS, width), F32),
        vec_q=V((pairs, VEC_ROWS, width), F32),
        cnt=V((8, 128), F32),
        cnt_y=V((8, 128), F32),
        cnt_s=V((8, 128), F32),
        cnt_r=V((8, 128), F32),
        cnt_q=V((pairs, 8, 128), F32),
    )
    found = pl.pallas_call(
        partial(layer_kernel, n_dp),
        out_shape=[
            V((token_count, width), BF16),
            V((token_count, width), BF16),
            V((shard, width), F32),
            V((shard, width), F32),
            V((shard, width), F32),
            V((shard, width), F32),
            V((VEC_ROWS, width), F32),
        ],
        in_specs=[
            anywhere,
            anywhere,
            smem,
            smem,
            anywhere,
            vmem,
            anywhere,
            vmem,
            vmem,
            vmem,
            anywhere,
            vmem,
            anywhere,
            anywhere,
            vmem,
            vmem,
            smem,
        ],
        out_specs=[vmem] * 7,
        scratch_shapes=list(scratch.values())
        + [
            pltpu.SemaphoreType.DMA((8,)),
            pltpu.SemaphoreType.DMA((copies,)),
            pltpu.SemaphoreType.DMA((copies,)),
        ],
        compiler_params=pltpu.CompilerParams(
            collective_id=0, has_side_effects=True, vmem_limit_bytes=VMEM_LIMIT
        ),
        name="layer",
    )(
        tokens,
        cotangent,
        lengths,
        labels,
        jnp.transpose(w_qkv, (1, 2, 0)).reshape(3 * local_width, width),
        qv_bias,
        w_out,
        branch_bias,
        norm_gain,
        norm_shift,
        w_up,
        up_bias,
        w_down,
        w_pool,
        pool_bias,
        w_class.T,
        class_bias.reshape(1, classes),
    )
    small = local_width // n_dp
    placed = pl.pallas_call(
        partial(place_kernel, n_dp),
        out_shape=[
            shape((token_count, width), BF16),
            shape((token_count, width), BF16),
            shape((1, 1), F32),
            shape((1, 1), F32),
            shape((3, shard, local_width), F32),
            shape((2, small), F32),
            shape((local_width, shard), F32),
            shape((2, shard), F32),
            shape((2, shard), F32),
            shape((2, shard), F32),
            shape((shard, hidden), F32),
            shape((1, hidden // n_dp), F32),
            shape((shard, hidden), F32),
            shape((shard, width), F32),
            shape((1, shard), F32),
            shape((classes, shard), F32),
            shape((1, classes), F32),
        ],
        in_specs=[vmem] * 7,
        out_specs=[anywhere] * 2 + [vmem] * 8 + [anywhere, vmem, anywhere, anywhere] + [vmem] * 3,
        scratch_shapes=[pltpu.SemaphoreType.DMA((5,))],
        name="place",
    )(*[pltpu.with_memory_space_constraint(value, pltpu.VMEM) for value in found])
    (
        block_out,
        grad_tokens,
        loss,
        entropy,
        grad_qkv,
        grad_qv,
        grad_out,
        grad_branch,
        grad_gain,
        grad_shift,
        grad_up,
        grad_upb,
        grad_down,
        grad_pool,
        grad_poolb,
        grad_class,
        grad_classb,
    ) = placed
    return (
        block_out,
        grad_tokens,
        loss.reshape(()),
        entropy.reshape(()),
        jnp.transpose(grad_qkv, (1, 0, 2)),
        grad_qv,
        grad_out,
        grad_branch,
        grad_gain,
        grad_shift,
        grad_up,
        grad_upb.reshape(-1),
        grad_down.T,
        grad_pool,
        grad_poolb.reshape(-1),
        grad_class.T,
        grad_classb.reshape(-1),
    )


def solution(mesh):
    in_specs = (
        P("dp", None),
        P("dp", None),
        P("dp", None),
        P("dp", None),
        P(None, None, "tensor"),
        P(None, "tensor"),
        P("tensor", None),
        P(),
        P(),
        P(),
        P(None, "tensor"),
        P("tensor"),
        P("tensor", None),
        P(),
        P(),
        P(),
        P(),
    )
    out_specs = (
        P("dp", None),
        P("dp", None),
        P(),
        P(),
        P("dp", None, "tensor"),
        P(None, ("tensor", "dp")),
        P("tensor", "dp"),
        P(None, "dp"),
        P(None, "dp"),
        P(None, "dp"),
        P("dp", "tensor"),
        P(("tensor", "dp")),
        P("tensor", "dp"),
        P("dp", None),
        P("dp"),
        P("dp", None),
        P(),
    )
    return jax.shard_map(
        partial(on_device, mesh.shape["dp"]),
        mesh=mesh,
        in_specs=in_specs,
        out_specs=out_specs,
        check_vma=False,
    )
```

```python
from functools import partial

import jax
import jax.numpy as jnp
from jax import lax
from jax.experimental import pallas as pl
from jax.experimental.pallas import tpu as pltpu
from jax.sharding import PartitionSpec as P

HD = 64
MESH = pl.DeviceIdType.MESH
F32 = jnp.float32
BF16 = jnp.bfloat16
masked_score = -1e30
norm_eps = 1e-12
SQRT_HALF = 0.7071067811865476
PDF_SCALE = 0.3989422804014327
VEC_ROWS = 16
ORDERS = "ryyyyyryy"
PLAN = (
    "fd", "FD0_11", "FD1_11", "FD0_10", "FD1_10", "FD0_01", "FD1_01", "FD0_00", "FD1_00", "fu",
    "ln1b0", "I_y", "FD2_11", "FD2_10", "SD0_1", "SD1_1", "SD0_0", "SD1_0", "ln1b1", "dctx",
    "ab0", "FD2_01", "ab1", "ab2", "FD2_00", "ab3", "ab4", "LD1", "FU0_11", "ab5",
    "SD2_1", "dattT", "FU0_10", "I_r", "SD2_0", "FU0_01", "dsum", "LD0", "dtok0", "dtok1",
    "FU0_00", "fq", "LD2", "FQ0_11", "FU1_11", "FQ0_10", "qv", "FU1_10", "FQ0_01", "FU1_01",
    "FQ0_00", "SU0_1", "ED1", "FU1_00", "SU0_0", "I_q", "FU2_11", "V_y", "ED0", "SQ0_1",
    "ED2", "SU1_1", "SQ0_0", "gtok0", "SU1_0", "FU2_10", "FU2_01", "LU0", "FU2_00", "SU2_1",
    "FQ1_11", "gtok1", "FQ1_10", "LQ0", "FQ1_01", "V_r", "LU1", "FQ1_00", "SU2_0", "FQ2_11",
    "I_c", "FQ2_10", "EU0", "LU2", "FQ2_01", "EQ0", "SQ1_1", "FQ2_00", "SQ1_0", "V_q",
    "EU1", "SQ2_1", "EU2", "pool", "SQ2_0", "LQ1", "LQ2", "V_e", "EQ1", "EQ2",
)
VMEM_LIMIT = 56 * 1024 * 1024


def dot_nn(a, b):
    return lax.dot_general(a, b, (((1,), (0,)), ((), ())), preferred_element_type=F32)


def dot_nt(a, b):
    return lax.dot_general(a, b, (((1,), (1,)), ((), ())), preferred_element_type=F32)


def dot_tn(a, b):
    return lax.dot_general(a, b, (((0,), (0,)), ((), ())), preferred_element_type=F32)


def row_mean(v):
    return jnp.sum(v, axis=1, keepdims=True) * (1.0 / v.shape[1])


def col_sum(v):
    return jnp.sum(v, axis=0, keepdims=True)


def norm_forward(values):
    centered = values - row_mean(values)
    inv_scale = lax.rsqrt(row_mean(centered * centered) + norm_eps)
    return centered * inv_scale, inv_scale


def norm_backward(gradient, normed, inv_scale, gain_row):
    scaled = gradient * gain_row
    inner = scaled - row_mean(scaled) - normed * row_mean(scaled * normed)
    return inner * inv_scale


def gelu_parts(pre_act):
    cdf = 0.5 * (1.0 + lax.erf(pre_act * SQRT_HALF))
    pdf = PDF_SCALE * jnp.exp(-0.5 * pre_act * pre_act)
    return pre_act * cdf, cdf + pre_act * pdf


class Stop(Exception):
    pass


STOP = None


def mark(name):
    if STOP is not None and name == STOP:
        raise Stop()


class Tracked:
    def __init__(self, copy):
        self.copy, self.received = copy, False

    def wait_recv(self):
        if not self.received:
            self.received = True
            self.copy.wait_recv()

    def wait_send(self):
        self.copy.wait_send()


class Copies:
    def __init__(self, send_sems, recv_sems):
        self.send_sems, self.recv_sems, self.used, self.open = send_sems, recv_sems, 0, []

    def start(self, src, dst, device):
        copy = pltpu.make_async_remote_copy(
            src_ref=src,
            dst_ref=dst,
            send_sem=self.send_sems.at[self.used],
            recv_sem=self.recv_sems.at[self.used],
            device_id=device,
            device_id_type=MESH,
        )
        self.used += 1
        copy.start()
        copy = Tracked(copy)
        self.open.append(copy)
        return copy

    def finish(self):
        for copy in self.open:
            copy.wait_send()


class Loads:
    def __init__(self, sems):
        self.sems, self.used = sems, 0

    def start(self, src, dst):
        copy = pltpu.make_async_copy(src, dst, self.sems.at[self.used])
        self.used += 1
        copy.start()
        return copy


def remote_copy_count(pairs):
    return 72 + 9 * 4 * pairs + 8 * pairs


def layer_kernel(
    n_dp,
    tok_hbm,
    cot_hbm,
    len_hbm,
    lab_hbm,
    wqkv_hbm,
    qvb_hbm,
    wout_hbm,
    bb_hbm,
    ng_hbm,
    ns_hbm,
    wup_hbm,
    upb_hbm,
    wdn_hbm,
    wpool_hbm,
    pb_hbm,
    wcls_hbm,
    cb_hbm,
    bout_out,
    gtok_out,
    gqkvo_out,
    gup_out,
    gdn_out,
    gpool_out,
    vec_out,
    len_ref,
    lab_ref,
    cb_ref,
    qvb_ref,
    bb_ref,
    ng_ref,
    ns_ref,
    upb_ref,
    pb_ref,
    wcls_ref,
    tok,
    cot,
    wt,
    wo,
    wup,
    wdn,
    wpool,
    wup_tr,
    wdn_tr,
    wpool_tr,
    up_bias,
    bias_mask,
    k_pad,
    v_pad,
    k_tr,
    v_tr,
    q_pad,
    q_away,
    probs,
    ctx,
    hid,
    hid_low,
    hid_tr,
    tok_tr,
    n_one,
    scale_one,
    act_low,
    d_gelu,
    acc,
    parts,
    d_sec,
    d_br,
    d_br_tr,
    d_br_peer,
    d_pre_low,
    d_pre_peer,
    act_peer,
    hid_peer,
    ctx_peer,
    d_att_peer,
    d_qkv_peer,
    d_first,
    d_att,
    d_att_tr,
    d_ctx,
    d_kv_f32,
    d_kv_send,
    d_kv_recv,
    d_qkv,
    g_low,
    first_recv,
    second_send,
    second_recv,
    last_send,
    last_recv,
    pool_fin,
    items,
    items_c,
    item_all,
    vec,
    vec_c,
    vec_s,
    vec_y,
    vec_t,
    vec_r,
    vec_q,
    cnt,
    cnt_y,
    cnt_s,
    cnt_r,
    cnt_q,
    load_sems,
    send_sems,
    recv_sems,
):
    pairs = n_dp // 4
    dp = lax.axis_index("dp")
    me = lax.axis_index("tensor")
    x = me // 2
    c = lax.rem(me, 2)
    y = lax.rem(dp, 2)
    r = lax.rem(dp // 2, 2)
    q = dp // 4
    core_dev = (dp, me + 1 - 2 * c)
    x_dev = (dp, 2 * (1 - x) + c)
    y_dev = (dp + 1 - 2 * y, me)
    r_dev = (dp + 2 - 4 * r, me)

    def q_of(k):
        return lax.rem(q + k, pairs)

    def q_dev(k):
        return (q_of(k) * 4 + r * 2 + y, me)

    away = range(1, pairs)
    token_count, width = tok.shape
    half = token_count // 2
    local_width = wo.shape[1]
    heads = local_width // HD
    slots = len_ref.shape[1]
    shard = width // n_dp
    chunk = 128
    chunks = half // chunk
    fine = 128
    fines = half // fine
    tile = 256
    tiles = width // tile
    own_rows = pl.ds(pl.multiple_of(c * half, half), half)
    away_rows = pl.ds(pl.multiple_of((1 - c) * half, half), half)

    barrier = pltpu.get_barrier_semaphore()
    peers = [core_dev, x_dev, y_dev, r_dev] + [q_dev(k) for k in away]
    for peer in peers:
        pl.semaphore_signal(barrier, inc=1, device_id=peer, device_id_type=MESH)

    loads = Loads(load_sems)
    remote = Copies(send_sems, recv_sems)
    load_len = loads.start(len_hbm, len_ref)
    load_tok = loads.start(tok_hbm, tok)
    load_wt = loads.start(wqkv_hbm, wt.at[c])
    load_qvb = loads.start(qvb_hbm, qvb_ref)
    load_upb = loads.start(upb_hbm, upb_ref)
    load_lab = loads.start(lab_hbm, lab_ref)
    load_small = [
        loads.start(src, dst)
        for src, dst in (
            (cb_hbm, cb_ref),
            (bb_hbm, bb_ref),
            (ng_hbm, ng_ref),
            (ns_hbm, ns_ref),
            (pb_hbm, pb_ref),
            (wcls_hbm, wcls_ref),
        )
    ]
    load_wo = loads.start(wout_hbm, wo.at[c])
    load_wup = loads.start(wup_hbm, wup.at[c])
    load_wdn = loads.start(wdn_hbm, wdn.at[c])
    load_pool = loads.start(wpool_hbm, wpool)
    load_cot = loads.start(cot_hbm.at[own_rows], cot)

    load_len.wait()
    load_lab.wait()
    lengths = [len_ref[0, i] for i in range(slots)]
    ends, total = [], 0
    for i in range(slots):
        total = total + lengths[i]
        ends.append(total)
    firsts = [jnp.minimum(ends[i] - lengths[i], token_count - 1) for i in range(slots)]
    key_place = lax.broadcasted_iota(jnp.int32, (token_count, 128), 0)
    query_place = lax.broadcasted_iota(jnp.int32, (8, half), 1) + c * half
    key_segment = jnp.zeros((token_count, 128), jnp.int32)
    query_segment = jnp.zeros((8, half), jnp.int32)
    for i in range(slots):
        key_segment = key_segment + (key_place >= ends[i]).astype(jnp.int32)
        query_segment = query_segment + (query_place >= ends[i]).astype(jnp.int32)
    for n in range(half // 128):
        cols = slice(n * 128, (n + 1) * 128)
        bias_mask[:, cols] = jnp.where(key_segment == query_segment[0:1, cols], 0.0, masked_score)
    item_row = lax.broadcasted_iota(jnp.int32, (slots, 128), 0)
    first_col = jnp.zeros((slots, 128), jnp.int32)
    len_col = jnp.zeros((slots, 128), jnp.int32)
    lab_col = jnp.zeros((slots, 128), jnp.int32)
    for i in range(slots):
        first_col = first_col + jnp.where(item_row == i, firsts[i], 0)
        len_col = len_col + jnp.where(item_row == i, lengths[i], 0)
        lab_col = lab_col + jnp.where(item_row == i, lab_ref[0, i], 0)
    live_all = jnp.where(len_col > 0, 1.0, 0.0)
    cnt[...] = jnp.broadcast_to(col_sum(live_all), cnt.shape)
    lane_item = lax.broadcasted_iota(jnp.int32, (1, 2 * slots), 1)
    first_row = jnp.zeros((1, 2 * slots), jnp.int32)
    for i in range(slots):
        first_row = first_row + jnp.where((lane_item == i) | (lane_item == i + slots), firsts[i], 0)

    load_upb.wait()
    up_bias[c] = jnp.broadcast_to(upb_ref[...].astype(F32).reshape(1, width), (8, width))
    vec[...] = jnp.zeros_like(vec)
    pad_rows = q_pad.shape[1] - local_width
    for b in range(2):
        q_pad[b, local_width:, :] = jnp.zeros((pad_rows, half), BF16)
        d_ctx[b, local_width:, :] = jnp.zeros((pad_rows, half), BF16)
        v_pad[b, :, local_width:] = jnp.zeros((token_count, pad_rows), BF16)

    def bias_cols(part, columns):
        row = qvb_ref[part : part + 1, :]
        block = jnp.transpose(jnp.broadcast_to(row, (128, local_width)))
        return jnp.concatenate([block] * (columns // 128), axis=1)

    load_tok.wait()
    load_wt.wait()
    load_qvb.wait()
    rows_q, rows_k, rows_v = [slice(p * local_width, (p + 1) * local_width) for p in range(3)]
    query_bias = bias_cols(0, half)
    q_away[...] = (dot_nt(wt[c, rows_q, :], tok[away_rows, :]) + query_bias).astype(BF16)
    wide_k = jnp.concatenate([wt[c, rows_k, :], jnp.zeros((pad_rows, width), BF16)], axis=0)
    k_pad[c] = dot_nt(tok[...], wide_k).astype(BF16)
    v_tr[c] = (dot_nt(wt[c, rows_v, :], tok[...]) + bias_cols(1, token_count)).astype(BF16)
    q_pad[c, 0:local_width, :] = (dot_nt(wt[c, rows_q, :], tok[own_rows, :]) + query_bias).astype(BF16)

    pl.semaphore_wait(barrier, len(peers))
    mark("sends")
    send_q = remote.start(q_away, q_pad.at[c, pl.ds(0, local_width)], core_dev)
    send_k = remote.start(k_pad.at[c], k_pad.at[c], core_dev)
    send_v = remote.start(v_tr.at[c], v_tr.at[c], core_dev)
    send_wo = remote.start(wout_hbm, wo.at[c], core_dev)
    send_bias = remote.start(up_bias.at[c], up_bias.at[c], core_dev)
    send_wup = remote.start(wup_hbm, wup.at[c], core_dev)
    send_wdn = remote.start(wdn_hbm, wdn.at[c], core_dev)
    send_cnt_y = remote.start(cnt, cnt_y, y_dev)
    send_wt = remote.start(wqkv_hbm, wt.at[c], core_dev)

    half_row = lax.broadcasted_iota(jnp.int32, (128, half), 0) < HD
    inv_root = HD ** (-0.5)

    def half_of(block, i):
        if i == heads - 1 and i % 2 == 0:
            return block
        zero = jnp.zeros_like(block)
        return jnp.where(half_row, block, zero) if i % 2 == 0 else jnp.where(half_row, zero, block)

    def pair_of(i):
        return slice((i // 2) * 128, (i // 2 + 1) * 128)

    def attend(core):
        for i in range(heads):
            head_rows = slice(i * HD, (i + 1) * HD)
            scores = dot_nn(k_pad[core, :, pair_of(i)], half_of(q_pad[core, pair_of(i), :], i))
            scores = scores * inv_root + bias_mask[...]
            terms = jnp.exp(scores - jnp.max(scores, axis=0, keepdims=True))
            weights = terms * (1.0 / col_sum(terms))
            probs[core, i] = weights
            ctx[core, head_rows, :] = dot_nn(v_tr[core, head_rows, :], weights.astype(BF16)).astype(BF16)

    mark("attn_own")
    attend(c)
    send_q.wait_recv()
    send_k.wait_recv()
    send_v.wait_recv()
    mark("attn_other")
    attend(1 - c)
    mark("out")
    for load in load_small:
        load.wait()
    send_ctx = remote.start(ctx.at[1 - c], ctx_peer, core_dev)
    load_wo.wait()
    send_wo.wait_recv()

    def chunk_of(i):
        return slice(i * chunk, (i + 1) * chunk)

    def exchange(which, rows):
        block = parts.at[which, x, rows]
        return remote.start(block, block, x_dev)

    def fine_of(i):
        return slice(i * fine, (i + 1) * fine)

    def both_parts(which, rows):
        return parts[which, 0, rows, :].astype(F32) + parts[which, 1, rows, :].astype(F32)

    ATT, FFN, HIDDEN, TOKEN = 0, 1, 2, 3
    send_att = []
    for i in range(chunks):
        rows = chunk_of(i)
        partial_sum = dot_tn(ctx[0, :, rows], wo[0]) + dot_tn(ctx[1, :, rows], wo[1])
        parts[ATT, x, rows, :] = partial_sum.astype(BF16)
        for j in range(i * chunk // fine, (i + 1) * chunk // fine):
            send_att.append(exchange(ATT, fine_of(j)))
    send_cnt_y.wait_recv()
    cnt_s[...] = cnt[...] + cnt_y[...]
    send_cnt_r = remote.start(cnt_s, cnt_r, r_dev)

    mark("transposes")
    for b in range(2):
        k_tr[b] = jnp.transpose(k_pad[b])[0:local_width, :]
        v_pad[b, :, 0:local_width] = jnp.transpose(v_tr[b])
    tok_tr[0] = jnp.transpose(tok[own_rows, :])
    tok_tr[1] = jnp.transpose(tok[away_rows, :])

    load_wup.wait()
    load_wdn.wait()
    load_pool.wait()
    wpool_tr[...] = jnp.transpose(wpool[...])
    send_wup.wait_recv()
    send_wdn.wait_recv()
    for b in range(2):
        wup_tr[b] = jnp.transpose(wup[b])
        wdn_tr[b] = jnp.transpose(wdn[b])

    mark("ffn_f")
    send_ffn, send_hid, send_act = [], [], []
    for i in range(fines):
        rows = fine_of(i)
        send_att[i].wait_recv()
        token_rows = pl.ds(pl.multiple_of(c * half + i * fine, fine), fine)
        attention = both_parts(ATT, rows) + bb_ref[0:1, :]
        normed, inv_scale = norm_forward(tok[token_rows, :].astype(F32) + attention)
        n_one[rows, :] = normed
        scale_one[rows, :] = inv_scale
        value = normed * ng_ref[0:1, :] + ns_ref[0:1, :]
        hid[rows, :] = value
        hid_low[rows, :] = value.astype(BF16)
        send_hid.append(remote.start(hid_low.at[rows], hid_peer.at[rows], core_dev))
        for b in range(2):
            core = c if b == 0 else 1 - c
            if i == 0 and b == 1:
                send_bias.wait_recv()
                send_wup.wait_recv()
            for n in range(tiles):
                cols = slice(n * tile, (n + 1) * tile)
                pre_act = dot_nn(hid_low[rows, :], wup[core, :, cols]) + up_bias[core, 0:1, cols]
                value, slope = gelu_parts(pre_act)
                act_low[b, rows, cols] = value.astype(BF16)
                d_gelu[b, rows, cols] = slope
            if i == 0 and b == 1:
                send_wdn.wait_recv()
            product = dot_nn(act_low[b, rows, :], wdn[core])
            if b == 0:
                acc[0:fine, :] = product
            else:
                parts[FFN, x, rows, :] = (acc[0:fine, :] + product).astype(BF16)
        send_ffn.append(exchange(FFN, rows))
        send_act.append(remote.start(act_low.at[1, rows], act_peer.at[rows], core_dev))
        if i == 0:
            send_cnt_r.wait_recv()
            cnt_q[q] = cnt_s[...] + cnt_r[...]
            send_cnt_q = [remote.start(cnt_q.at[q], cnt_q.at[q], q_dev(k)) for k in away]

    mark("hid_tr")
    hid_tr[0] = jnp.transpose(hid_low[...])
    for copy in send_hid:
        copy.wait_recv()
    hid_tr[1] = jnp.transpose(hid_peer[...])
    load_cot.wait()
    for copy in send_cnt_q:
        copy.wait_recv()
    item_count = cnt_q[0]
    for k in away:
        item_count = item_count + cnt_q[k]
    inv_count = 1.0 / item_count[0:1, 0:1]

    classes = wcls_ref.shape[0]
    class_rows = wcls_ref[...].astype(F32)
    class_pad = jnp.concatenate([class_rows, jnp.zeros((16 - classes, width), F32)], axis=0).astype(BF16)
    class_lane = lax.broadcasted_iota(jnp.int32, (slots, 16), 1)
    class_bias = jnp.zeros((slots, 16), F32)
    for k in range(classes):
        class_bias = class_bias + jnp.where(class_lane == k, cb_ref[0, k], 0.0)
    label_hot = jnp.where(class_lane == lab_col[:, 0:1], 1.0, 0.0)
    lane = lax.broadcasted_iota(jnp.int32, (1, 128), 1)

    def add_rows(first, value):
        vec[first : first + value.shape[0], 0 : value.shape[1]] += value

    mark("ln2")
    up_sums = [[None] * tiles, [None] * tiles]
    send_hidden, send_br, send_pre = [], [], []
    for i in range(chunks):
        rows = chunk_of(i)
        place = c * half + i * chunk
        for j in range(i * chunk // fine, (i + 1) * chunk // fine):
            send_ffn[j].wait_recv()
        normed, inv_scale = norm_forward(hid[rows, :] + (both_parts(FFN, rows) + bb_ref[1:2, :]))
        low = (normed * ng_ref[1:2, :] + ns_ref[1:2, :]).astype(BF16)
        bout_out[pl.ds(pl.multiple_of(place, chunk), chunk), :] = low

        local_first = first_col[:, 0:1] - place
        pick = (lax.broadcasted_iota(jnp.int32, (slots, chunk), 1) == local_first).astype(F32).astype(BF16)
        picked = dot_nn(pick, low).astype(BF16)
        pooled = jnp.tanh(dot_nn(picked, wpool[...]) + pb_ref[...].reshape(1, width))
        pooled_low = pooled.astype(BF16)
        logits = jnp.where(class_lane < classes, dot_nt(pooled_low, class_pad) + class_bias, masked_score)
        shifted = logits - jnp.max(logits, axis=1, keepdims=True)
        log_probs = shifted - jnp.log(jnp.sum(jnp.exp(shifted), axis=1, keepdims=True))
        class_probs = jnp.exp(log_probs)
        owned = jnp.where((local_first >= 0) & (local_first < chunk), live_all[:, 0:1], 0.0)
        item_ce = -jnp.sum(label_hot * log_probs, axis=1, keepdims=True) * owned
        item_ent = -jnp.sum(class_probs * log_probs, axis=1, keepdims=True) * owned
        d_logits = (class_probs - label_hot) * (owned * inv_count)
        d_pooled = jnp.zeros((slots, width), F32)
        for k in range(classes):
            d_pooled = d_pooled + d_logits[:, k : k + 1] * class_rows[k : k + 1, :]
            add_rows(7 + k, col_sum(d_logits[:, k : k + 1] * pooled_low.astype(F32)))
        d_pre = (d_pooled * (1.0 - pooled * pooled)).astype(BF16)
        add_rows(6, col_sum(d_pre.astype(F32)))
        add_rows(
            10, jnp.where(lane == 0, col_sum(item_ce), 0.0) + jnp.where(lane == 1, col_sum(item_ent), 0.0)
        )
        vec[10:11, 128:144] += col_sum(d_logits)
        if i == 0:
            items[0] = picked
            items[1] = d_pre
        else:
            items[0] += picked
            items[1] += d_pre
        if i == chunks - 1:
            send_items = remote.start(items.at[1 - c], items_c, core_dev)
        d_picked = dot_nn(d_pre, wpool_tr[...])
        d_high = d_picked.astype(BF16)
        d_both = jnp.concatenate([d_high, (d_picked - d_high.astype(F32)).astype(BF16)], axis=0)

        token_place = lax.broadcasted_iota(jnp.int32, (chunk, 2 * slots), 0) + place
        spread = dot_nn((token_place == first_row).astype(F32).astype(BF16), d_both)
        live = jnp.where(token_place[:, 0:1] < total, 1.0, 0.0)
        d_output = cot[rows, :].astype(F32) * live + spread
        add_rows(3, col_sum(d_output * normed))
        add_rows(5, col_sum(d_output))
        d_second = norm_backward(d_output, normed, inv_scale, ng_ref[1:2, :])
        add_rows(1, col_sum(d_second))
        d_sec[rows, :] = d_second
        d_br[rows, :] = d_second.astype(BF16)
        send_br.append(remote.start(d_br.at[rows], d_br_peer.at[rows], core_dev))
        for b in range(2):
            core = c if b == 0 else 1 - c
            for n in range(tiles):
                cols = slice(n * tile, (n + 1) * tile)
                d_act = dot_nn(d_br[rows, :], wdn_tr[core, :, cols])
                low = (d_act * d_gelu[b, rows, cols]).astype(BF16)
                d_pre_low[b, rows, cols] = low
                up_sum = col_sum(low.astype(F32))
                up_sums[b][n] = up_sum if i == 0 else up_sums[b][n] + up_sum
            product = dot_nn(d_pre_low[b, rows, :], wup_tr[core])
            if b == 0:
                acc[...] = product
            else:
                parts[HIDDEN, x, rows, :] = (acc[...] + product).astype(BF16)
        send_hidden.append(exchange(HIDDEN, rows))
        send_pre.append(remote.start(d_pre_low.at[1, rows], d_pre_peer.at[rows], core_dev))
    vec[pl.ds(11 + c, 1), :] = jnp.concatenate(up_sums[0], axis=1)
    vec[pl.ds(12 - c, 1), :] = jnp.concatenate(up_sums[1], axis=1)
    send_out = remote.start(bout_out.at[own_rows], bout_out.at[own_rows], core_dev)

    DOWN, UP, QKVO = 0, tiles, 2 * tiles
    y_first, r_first = (y, r, y_dev, r_dev), (r, y, r_dev, y_dev)
    along = [y_first if letter == "y" else r_first for letter in ORDERS]
    row_major = [letter == "r" for letter in ORDERS]
    reach = {1: list(away), 0: [0]}
    slot_of = {(flip, k): (1 - flip) * pairs + (k - 1) % pairs for flip in range(2) for k in range(pairs)}
    sent = {}
    step = {}

    def store_blocks(block, product):
        for j in range(n_dp):
            bits = (j % 2, (j // 2) % 2)
            if row_major[block]:
                bits = bits[::-1]
            g_low[block, bits[0], bits[1], j // 4] = product[j * shard : (j + 1) * shard, :].astype(BF16)

    def fill(block, product_of):
        for n in range(tiles):
            store_blocks(block + n, product_of(slice(n * tile, (n + 1) * tile)))

    def first_step(block, flip, group):
        first, second, device, _ = along[block]
        for k in reach[group]:
            source = g_low.at[block, 1 - first, 1 - second if flip else second, q_of(k)]
            sent[block, 1, flip, k] = remote.start(source, first_recv.at[block, slot_of[flip, k]], device)

    def first_sum(block, flip, k):
        first, second, _, _ = along[block]
        sent[block, 1, flip, k].wait_recv()
        value = g_low[block, first, 1 - second if flip else second, q_of(k)].astype(F32)
        return value + first_recv[block, slot_of[flip, k]].astype(F32)

    def second_step(block, group):
        for k in reach[group]:
            second_send[block, k] = first_sum(block, 1, k).astype(BF16)
            sent[block, 2, k] = remote.start(second_send.at[block, k], second_recv.at[block, k], along[block][3])

    def second_sum(block, k):
        sent[block, 2, k].wait_recv()
        return first_sum(block, 0, k) + second_recv[block, k].astype(F32)

    def last_step(block):
        for k in away:
            last_send[block, k - 1] = second_sum(block, k).astype(BF16)
            sent[block, 3, k] = remote.start(last_send.at[block, k - 1], last_recv.at[block, k - 1], q_dev(k))

    def end_step(block, out):
        result = second_sum(block, 0)
        for k in away:
            sent[block, 3, k].wait_recv()
            result = result + last_recv[block, k - 1].astype(F32)
        n = block % tiles
        out[:, n * tile : (n + 1) * tile] = result

    for letter, first_block, out in (("D", DOWN, gdn_out), ("U", UP, gup_out), ("Q", QKVO, gqkvo_out)):
        for n in range(tiles):
            block, name = first_block + n, letter + str(n)
            for group in range(2):
                for flip in range(2):
                    step["F%s_%d%d" % (name, flip, group)] = partial(first_step, block, flip, group)
                step["S%s_%d" % (name, group)] = partial(second_step, block, group)
            step["L" + name] = partial(last_step, block)
            step["E" + name] = partial(end_step, block, out)

    def fill_down():
        d_br_tr[0] = jnp.transpose(d_br[...])
        for copy in send_br + send_act:
            copy.wait_recv()
        d_br_tr[1] = jnp.transpose(d_br_peer[...])
        fill(DOWN, lambda cols: dot_nn(d_br_tr[0], act_low[0, :, cols]) + dot_nn(d_br_tr[1], act_peer[:, cols]))

    def fill_up():
        for copy in send_pre:
            copy.wait_recv()
        fill(UP, lambda cols: dot_nn(hid_tr[0], d_pre_low[0, :, cols]) + dot_nn(hid_tr[1], d_pre_peer[:, cols]))

    step["fd"] = fill_down
    step["fu"] = fill_up

    def item_rows(first, count):
        return pl.ds(pl.multiple_of(first * slots, count * slots), count * slots)

    def pass_items(name, rows, devices):
        sent[name] = [remote.start(item_all.at[c, rows], item_all.at[c, rows], device) for device in devices]

    def settle(name):
        for copy in sent[name]:
            copy.wait_recv()

    def items_y():
        send_items.wait_recv()
        item_all[c, item_rows(dp, 1), :] = items[c] + items_c[...]
        pass_items("items_y", item_rows(dp, 1), [y_dev])

    def items_r():
        settle("items_y")
        pass_items("items_r", item_rows(dp - y, 2), [r_dev])

    def items_q():
        settle("items_r")
        pass_items("items_q", item_rows(q * 4, 4), [q_dev(k) for k in away])

    def items_core():
        settle("items_q")
        sent["items_core"] = [remote.start(item_all.at[c], item_all.at[c], core_dev)]

    def pool():
        settle("items_core")
        pool_fin[...] = dot_tn(item_all[0], item_all[1])
        gpool_out[...] = pool_fin[pl.ds(pl.multiple_of(dp * shard, 8), shard), :]

    step.update(I_y=items_y, I_r=items_r, I_q=items_q, I_c=items_core, pool=pool)

    def norm_one_back(i):
        rows = chunk_of(i)
        send_hidden[i].wait_recv()
        d_hidden = both_parts(HIDDEN, rows) + d_sec[rows, :]
        normed = n_one[rows, :]
        add_rows(2, col_sum(d_hidden * normed))
        add_rows(4, col_sum(d_hidden))
        gradient = norm_backward(d_hidden, normed, scale_one[rows, :], ng_ref[0:1, :])
        add_rows(0, col_sum(gradient))
        d_first[rows, :] = gradient
        d_att[rows, :] = gradient.astype(BF16)
        sent["d_att", i] = remote.start(d_att.at[rows], d_att_peer.at[rows], core_dev)

    def context_back():
        for b in range(2):
            d_ctx[b, 0:local_width, :] = dot_nt(wo[b], d_att[...]).astype(BF16)

    def head_back(n):
        b, i = n // heads, n % heads
        head_rows = slice(i * HD, (i + 1) * HD)
        d_probs = dot_nn(v_pad[b, :, pair_of(i)], half_of(d_ctx[b, pair_of(i), :], i))
        weights = probs[b, i]
        delta = col_sum(weights * d_probs)
        d_scores = (weights * (d_probs - delta)).astype(BF16)
        d_value = dot_nt(d_ctx[b, head_rows, :], weights.astype(BF16))
        d_key = dot_nt(q_pad[b, head_rows, :], d_scores) * inv_root
        d_query = dot_nn(k_tr[b, head_rows, :], d_scores) * inv_root
        d_qkv[b, head_rows, :] = d_query.astype(BF16)
        for part, value in ((0, d_key), (1, d_value)):
            part_rows = slice(part * local_width + i * HD, part * local_width + (i + 1) * HD)
            for side in range(2):
                lanes = slice(side * half, (side + 1) * half)
                d_kv_f32[side, b, part_rows, :] = value[:, lanes]
                d_kv_send[side, b, part_rows, :] = value[:, lanes].astype(BF16)
        if n == 2 * heads - 1:
            sent["kv"] = remote.start(d_kv_send.at[1 - c], d_kv_recv, core_dev)

    def turn_attention():
        d_att_tr[0] = jnp.transpose(d_att[...])
        for i in range(chunks):
            sent["d_att", i].wait_recv()
        d_att_tr[1] = jnp.transpose(d_att_peer[...])

    def join_cores():
        sent["kv"].wait_recv()
        for b in range(2):
            d_qkv[b, local_width:, :] = (d_kv_f32[c, b] + d_kv_recv[b].astype(F32)).astype(BF16)
        sent["d_qkv"] = remote.start(d_qkv.at[1 - c], d_qkv_peer, core_dev)

    for i in range(chunks):
        step["ln1b%d" % i] = partial(norm_one_back, i)
    step["dctx"] = context_back
    for n in range(2 * heads):
        step["ab%d" % n] = partial(head_back, n)
    step["dattT"] = turn_attention
    step["dsum"] = join_cores

    def fill_qkvo():
        sent["d_qkv"].wait_recv()
        send_ctx.wait_recv()
        first_part = dot_nt(tok_tr[0], d_qkv[c]) + dot_nt(tok_tr[1], d_qkv_peer[...])
        second_part = dot_nt(d_att_tr[0], ctx[c]) + dot_nt(d_att_tr[1], ctx_peer[...])
        both = jnp.concatenate([first_part, second_part], axis=1)
        fill(QKVO, lambda cols: both[:, cols])

    def token_part(i):
        send_wt.wait_recv()
        rows = chunk_of(i)
        partial_sum = dot_tn(d_qkv[0, :, rows], wt[0]) + dot_tn(d_qkv[1, :, rows], wt[1])
        parts[TOKEN, x, rows, :] = partial_sum.astype(BF16)
        sent["token", i] = exchange(TOKEN, rows)

    def token_end(i):
        sent["token", i].wait_recv()
        rows = chunk_of(i)
        place = pl.ds(pl.multiple_of(c * half + i * chunk, chunk), chunk)
        gtok_out[place, :] = (both_parts(TOKEN, rows) + d_first[rows, :]).astype(BF16)
        if i == chunks - 1:
            sent["gtok"] = remote.start(gtok_out.at[own_rows], gtok_out.at[own_rows], core_dev)

    step["fq"] = fill_qkvo
    for i in range(chunks):
        step["dtok%d" % i] = partial(token_part, i)
        step["gtok%d" % i] = partial(token_end, i)

    def vec_core():
        ones = jnp.ones((8, half), BF16)
        sums = [dot_nt(ones, d_qkv[b])[0:1, :] for b in range(2)]
        columns = [v[:, :local_width] for v in sums] + [v[:, 2 * local_width :] for v in sums]
        vec[13:14, :] = jnp.concatenate(columns, axis=1)
        vec[14:15, 0:128] = item_count[0:1, :]
        sent["vec"] = remote.start(vec, vec_c, core_dev)

    def vec_along_y():
        sent["vec"].wait_recv()
        vec_s[...] = vec[...] + vec_c[...]
        sent["vec_y"] = remote.start(vec_s, vec_y, y_dev)

    def vec_along_r():
        sent["vec_y"].wait_recv()
        vec_t[...] = vec_s[...] + vec_y[...]
        sent["vec_r"] = remote.start(vec_t, vec_r, r_dev)

    def vec_along_q():
        sent["vec_r"].wait_recv()
        vec_q[q] = vec_t[...] + vec_r[...]
        sent["vec_q"] = [remote.start(vec_q.at[q], vec_q.at[q], q_dev(k)) for k in away]

    def vec_end():
        settle("vec_q")
        vec_total = vec_q[0]
        for k in away:
            vec_total = vec_total + vec_q[k]
        vec_out[...] = vec_total

    step.update(qv=vec_core, V_y=vec_along_y, V_r=vec_along_r, V_q=vec_along_q, V_e=vec_end)

    assert sorted(PLAN) == sorted(step)
    for name in PLAN:
        mark(name)
        step[name]()
    mark("finish")
    send_out.wait_recv()
    sent["gtok"].wait_recv()
    remote.finish()


def place_kernel(
    n_dp,
    bout_in,
    gtok_in,
    gqkvo_in,
    gup_in,
    gdn_in,
    gpool_in,
    vec_in,
    bout_out,
    gtok_out,
    loss_out,
    entropy_out,
    gqkv_out,
    gqv_out,
    gout_out,
    gbranch_out,
    ggain_out,
    gshift_out,
    gup_out,
    gupb_out,
    gdn_out,
    gpool_out,
    gpoolb_out,
    gclass_out,
    gclassb_out,
    loss,
    entropy,
    gqkv,
    gqv,
    gout,
    gbranch,
    ggain,
    gshift,
    gupb,
    gpoolb,
    gclass,
    gclassb,
    sems,
):
    moves = ((bout_in, bout_out), (gtok_in, gtok_out), (gup_in, gup_out), (gdn_in, gdn_out), (gpool_in, gpool_out))
    copies = []

    def send(src, dst):
        copy = pltpu.make_async_copy(src, dst, sems.at[len(copies)])
        copy.start()
        copies.append(copy)

    for src, dst in moves:
        send(src, dst)
    dp = lax.axis_index("dp")
    c = lax.rem(lax.axis_index("tensor"), 2)
    width = vec_in.shape[1]
    shard = width // n_dp
    local_width = gout.shape[0]
    for part in range(3):
        gqkv[part] = gqkvo_in[:, part * local_width : (part + 1) * local_width]
    send(gqkv, gqkv_out)
    gout[...] = jnp.transpose(gqkvo_in[:, 3 * local_width :])
    send(gout, gout_out)
    sums = vec_in[...]
    mine = pltpu.roll(sums, lax.rem(width - dp * shard, width), axis=1)
    gbranch[...] = mine[0:2, :shard]
    ggain[...] = mine[2:4, :shard]
    gshift[...] = mine[4:6, :shard]
    gpoolb[...] = mine[6:7, :shard]
    gclass[...] = mine[7 : 7 + gclass.shape[0], :shard]
    gupb[...] = jnp.where(c == 0, mine[11:12, :shard], mine[12:13, :shard])
    small = local_width // n_dp
    quarter = pltpu.roll(sums, lax.rem(width - (c * local_width + dp * small), width), axis=1)
    gqv[0:1, :] = quarter[13:14, :small]
    gqv[1:2, :] = quarter[13:14, 2 * local_width : 2 * local_width + small]
    inv_count = 2.0 * n_dp / sums[14:15, 0:1]
    loss[...] = sums[10:11, 0:1] * inv_count
    entropy[...] = sums[10:11, 1:2] * inv_count
    gclassb[...] = sums[10:11, 128 : 128 + gclassb.shape[1]]
    small_moves = (
        (loss, loss_out),
        (entropy, entropy_out),
        (gqv, gqv_out),
        (gbranch, gbranch_out),
        (ggain, ggain_out),
        (gshift, gshift_out),
        (gupb, gupb_out),
        (gpoolb, gpoolb_out),
        (gclass, gclass_out),
        (gclassb, gclassb_out),
    )
    for src, dst in small_moves:
        send(src, dst)
    for copy in copies:
        copy.wait()


def on_device(
    n_dp,
    tokens,
    cotangent,
    lengths,
    labels,
    w_qkv,
    qv_bias,
    w_out,
    branch_bias,
    norm_gain,
    norm_shift,
    w_up,
    up_bias,
    w_down,
    w_pool,
    pool_bias,
    w_class,
    class_bias,
):
    token_count, width = tokens.shape
    local_width = w_out.shape[0]
    hidden = w_up.shape[1]
    classes = w_class.shape[1]
    slots = lengths.shape[1]
    pairs = n_dp // 4
    shard = width // n_dp
    half = token_count // 2
    heads = local_width // HD
    padded = (local_width + 127) // 128 * 128
    assert hidden == width and 4 * local_width == width and lengths.shape[0] == 1
    shape = jax.ShapeDtypeStruct
    anywhere = pl.BlockSpec(memory_space=pl.ANY)
    vmem = pl.BlockSpec(memory_space=pltpu.VMEM)
    pieces = 3 * width // 256
    blocks = (pieces, 2, 2, pairs, shard, 256)
    copies = remote_copy_count(pairs)
    V = pltpu.VMEM
    S = pltpu.SMEM
    scratch = dict(
        len_ref=S(lengths.shape, jnp.int32),
        lab_ref=S(labels.shape, jnp.int32),
        cb_ref=S((1, classes), F32),
        qvb_ref=V(qv_bias.shape, F32),
        bb_ref=V(branch_bias.shape, F32),
        ng_ref=V(norm_gain.shape, F32),
        ns_ref=V(norm_shift.shape, F32),
        upb_ref=V(up_bias.shape, BF16),
        pb_ref=V(pool_bias.shape, F32),
        wcls_ref=V((classes, width), BF16),
        tok=V((token_count, width), BF16),
        cot=V((half, width), BF16),
        wt=V((2, 3 * local_width, width), BF16),
        wo=V((2, local_width, width), BF16),
        wup=V((2, width, hidden), BF16),
        wdn=V((2, hidden, width), BF16),
        wpool=V((width, width), BF16),
        wup_tr=V((2, hidden, width), BF16),
        wdn_tr=V((2, width, hidden), BF16),
        wpool_tr=V((width, width), BF16),
        up_bias=V((2, 8, width), F32),
        bias_mask=V((token_count, half), F32),
        k_pad=V((2, token_count, padded), BF16),
        v_pad=V((2, token_count, padded), BF16),
        k_tr=V((2, local_width, token_count), BF16),
        v_tr=V((2, local_width, token_count), BF16),
        q_pad=V((2, padded, half), BF16),
        q_away=V((local_width, half), BF16),
        probs=V((2, heads, token_count, half), F32),
        ctx=V((2, local_width, half), BF16),
        hid=V((half, width), F32),
        hid_low=V((half, width), BF16),
        hid_tr=V((2, width, half), BF16),
        tok_tr=V((2, width, half), BF16),
        n_one=V((half, width), F32),
        scale_one=V((half, 1), F32),
        act_low=V((2, half, hidden), BF16),
        d_gelu=V((2, half, hidden), F32),
        acc=V((128, width), F32),
        parts=V((4, 2, half, width), BF16),
        d_sec=V((half, width), F32),
        d_br=V((half, width), BF16),
        d_br_tr=V((2, width, half), BF16),
        d_br_peer=V((half, width), BF16),
        d_pre_low=V((2, half, hidden), BF16),
        d_pre_peer=V((half, hidden), BF16),
        act_peer=V((half, hidden), BF16),
        hid_peer=V((half, width), BF16),
        ctx_peer=V((local_width, half), BF16),
        d_att_peer=V((half, width), BF16),
        d_qkv_peer=V((3 * local_width, half), BF16),
        d_first=V((half, width), F32),
        d_att=V((half, width), BF16),
        d_att_tr=V((2, width, half), BF16),
        d_ctx=V((2, padded, half), BF16),
        d_kv_f32=V((2, 2, 2 * local_width, half), F32),
        d_kv_send=V((2, 2, 2 * local_width, half), BF16),
        d_kv_recv=V((2, 2 * local_width, half), BF16),
        d_qkv=V((2, 3 * local_width, half), BF16),
        g_low=V(blocks, BF16),
        first_recv=V((pieces, 2 * pairs, shard, 256), BF16),
        second_send=V((pieces, pairs, shard, 256), BF16),
        second_recv=V((pieces, pairs, shard, 256), BF16),
        last_send=V((pieces, pairs - 1, shard, 256), BF16),
        last_recv=V((pieces, pairs - 1, shard, 256), BF16),
        pool_fin=V((width, width), F32),
        items=V((2, slots, width), BF16),
        items_c=V((slots, width), BF16),
        item_all=V((2, n_dp * slots, width), BF16),
        vec=V((VEC_ROWS, width), F32),
        vec_c=V((VEC_ROWS, width), F32),
        vec_s=V((VEC_ROWS, width), F32),
        vec_y=V((VEC_ROWS, width), F32),
        vec_t=V((VEC_ROWS, width), F32),
        vec_r=V((VEC_ROWS, width), F32),
        vec_q=V((pairs, VEC_ROWS, width), F32),
        cnt=V((8, 128), F32),
        cnt_y=V((8, 128), F32),
        cnt_s=V((8, 128), F32),
        cnt_r=V((8, 128), F32),
        cnt_q=V((pairs, 8, 128), F32),
    )
    found = pl.pallas_call(
        partial(layer_kernel, n_dp),
        out_shape=[
            V((token_count, width), BF16),
            V((token_count, width), BF16),
            V((shard, width), F32),
            V((shard, width), F32),
            V((shard, width), F32),
            V((shard, width), F32),
            V((VEC_ROWS, width), F32),
        ],
        in_specs=[anywhere] * 17,
        out_specs=[vmem] * 7,
        scratch_shapes=list(scratch.values())
        + [
            pltpu.SemaphoreType.DMA((20,)),
            pltpu.SemaphoreType.DMA((copies,)),
            pltpu.SemaphoreType.DMA((copies,)),
        ],
        compiler_params=pltpu.CompilerParams(
            collective_id=0, has_side_effects=True, vmem_limit_bytes=VMEM_LIMIT
        ),
        name="layer",
    )(
        tokens,
        cotangent,
        lengths,
        labels,
        jnp.transpose(w_qkv, (1, 2, 0)).reshape(3 * local_width, width),
        qv_bias,
        w_out,
        branch_bias,
        norm_gain,
        norm_shift,
        w_up,
        up_bias,
        w_down,
        w_pool,
        pool_bias,
        w_class.T,
        class_bias.reshape(1, classes),
    )
    small = local_width // n_dp
    outputs = [
        shape((token_count, width), BF16),
        shape((token_count, width), BF16),
        shape((1, 1), F32),
        shape((1, 1), F32),
        shape((3, shard, local_width), F32),
        shape((2, small), F32),
        shape((local_width, shard), F32),
        shape((2, shard), F32),
        shape((2, shard), F32),
        shape((2, shard), F32),
        shape((shard, hidden), F32),
        shape((1, hidden // n_dp), F32),
        shape((shard, hidden), F32),
        shape((shard, width), F32),
        shape((1, shard), F32),
        shape((classes, shard), F32),
        shape((1, classes), F32),
    ]
    held = [out for i, out in enumerate(outputs) if i not in (0, 1, 10, 12, 13)]
    placed = pl.pallas_call(
        partial(place_kernel, n_dp),
        out_shape=outputs,
        in_specs=[vmem] * 7,
        out_specs=[anywhere] * 17,
        scratch_shapes=[V(out.shape, out.dtype) for out in held] + [pltpu.SemaphoreType.DMA((17,))],
        name="place",
    )(*[pltpu.with_memory_space_constraint(value, pltpu.VMEM) for value in found])
    (
        block_out,
        grad_tokens,
        loss,
        entropy,
        grad_qkv,
        grad_qv,
        grad_out,
        grad_branch,
        grad_gain,
        grad_shift,
        grad_up,
        grad_upb,
        grad_down,
        grad_pool,
        grad_poolb,
        grad_class,
        grad_classb,
    ) = placed
    return (
        block_out,
        grad_tokens,
        loss.reshape(()),
        entropy.reshape(()),
        jnp.transpose(grad_qkv, (1, 0, 2)),
        grad_qv,
        grad_out,
        grad_branch,
        grad_gain,
        grad_shift,
        grad_up,
        grad_upb.reshape(-1),
        grad_down.T,
        grad_pool,
        grad_poolb.reshape(-1),
        grad_class.T,
        grad_classb.reshape(-1),
    )


def solution(mesh):
    in_specs = (
        P("dp", None),
        P("dp", None),
        P("dp", None),
        P("dp", None),
        P(None, None, "tensor"),
        P(None, "tensor"),
        P("tensor", None),
        P(),
        P(),
        P(),
        P(None, "tensor"),
        P("tensor"),
        P("tensor", None),
        P(),
        P(),
        P(),
        P(),
    )
    out_specs = (
        P("dp", None),
        P("dp", None),
        P(),
        P(),
        P("dp", None, "tensor"),
        P(None, ("tensor", "dp")),
        P("tensor", "dp"),
        P(None, "dp"),
        P(None, "dp"),
        P(None, "dp"),
        P("dp", "tensor"),
        P(("tensor", "dp")),
        P("tensor", "dp"),
        P("dp", None),
        P("dp"),
        P("dp", None),
        P(),
    )
    return jax.shard_map(
        partial(on_device, mesh.shape["dp"]),
        mesh=mesh,
        in_specs=in_specs,
        out_specs=out_specs,
        check_vma=False,
    )
```

```python
from functools import partial

import jax
import jax.numpy as jnp
from jax import lax
from jax.experimental import pallas as pl
from jax.experimental.pallas import tpu as pltpu
from jax.sharding import PartitionSpec as P

HD = 64
MESH = pl.DeviceIdType.MESH
F32 = jnp.float32
BF16 = jnp.bfloat16
masked_score = -1e30
norm_eps = 1e-12
SQRT_HALF = 0.7071067811865476
PDF_SCALE = 0.3989422804014327
VEC_ROWS = 16
ORDERS = "yyryyrryy"
PLAN = (
    "fd0", "FD0_11", "FD0_10", "fd1", "fd2", "FD2_11", "FD2_10", "FD1_11", "fu0", "fu1",
    "FD2_01", "fu2", "ln1b0", "I_y", "FD1_10", "FD2_00", "FD1_01", "FU2_11", "SD0_1", "FD1_00",
    "SD2_1", "SD0_0", "SD2_0", "ln1b1", "SD1_1", "dctx", "ab0", "ab1", "FU1_11", "SD1_0",
    "ab2", "ab3", "I_r", "FU1_10", "ab4", "SU2_1", "ab5", "FU2_10", "dattT", "LD2",
    "FU1_01", "dsum", "FU2_01", "dtok0", "LD1", "FU1_00", "dtok1", "SU1_1", "FU0_11", "fq",
    "SU1_0", "FQ1_11", "qv", "SU2_0", "I_q", "ED2", "FQ1_10", "LU2", "FQ1_01", "V_y",
    "SU0_1", "FQ1_00", "LU1", "SQ1_1", "FU0_10", "ED1", "FU0_01", "gtok0", "FQ0_11", "SQ1_0",
    "FU0_00", "I_x", "FD0_01", "FQ0_10", "FD0_00", "FQ0_01", "V_r", "SU0_0", "FQ2_11", "LQ1",
    "gtok1", "LU0", "FQ2_10", "SQ0_1", "EU1", "LD0", "FQ2_01", "SQ0_0", "SQ2_1", "EQ1",
    "FQ2_00", "SQ2_0", "V_q", "LQ0", "I_c", "FQ0_00", "EU0", "FU2_00", "LQ2", "ED0",
    "V_e", "EQ0", "pool", "EU2", "EQ2",
)
VMEM_LIMIT = 56 * 1024 * 1024


def dot_nn(a, b):
    return lax.dot_general(a, b, (((1,), (0,)), ((), ())), preferred_element_type=F32)


def dot_nt(a, b):
    return lax.dot_general(a, b, (((1,), (1,)), ((), ())), preferred_element_type=F32)


def dot_tn(a, b):
    return lax.dot_general(a, b, (((0,), (0,)), ((), ())), preferred_element_type=F32)


def row_mean(v):
    return jnp.sum(v, axis=1, keepdims=True) * (1.0 / v.shape[1])


def col_sum(v):
    return jnp.sum(v, axis=0, keepdims=True)


def norm_forward(values):
    centered = values - row_mean(values)
    inv_scale = lax.rsqrt(row_mean(centered * centered) + norm_eps)
    return centered * inv_scale, inv_scale


def norm_backward(gradient, normed, inv_scale, gain_row):
    scaled = gradient * gain_row
    inner = scaled - row_mean(scaled) - normed * row_mean(scaled * normed)
    return inner * inv_scale


def gelu_parts(pre_act):
    cdf = 0.5 * (1.0 + lax.erf(pre_act * SQRT_HALF))
    pdf = PDF_SCALE * jnp.exp(-0.5 * pre_act * pre_act)
    return pre_act * cdf, cdf + pre_act * pdf


class Stop(Exception):
    pass


STOP = None


def mark(name):
    if STOP is not None and name == STOP:
        raise Stop()


class Tracked:
    def __init__(self, copy):
        self.copy, self.received = copy, False

    def wait_recv(self):
        if not self.received:
            self.received = True
            self.copy.wait_recv()

    def wait_send(self):
        self.copy.wait_send()


class Copies:
    def __init__(self, send_sems, recv_sems):
        self.send_sems, self.recv_sems, self.used, self.open = send_sems, recv_sems, 0, []

    def start(self, src, dst, device):
        copy = pltpu.make_async_remote_copy(
            src_ref=src,
            dst_ref=dst,
            send_sem=self.send_sems.at[self.used],
            recv_sem=self.recv_sems.at[self.used],
            device_id=device,
            device_id_type=MESH,
        )
        self.used += 1
        copy.start()
        copy = Tracked(copy)
        self.open.append(copy)
        return copy

    def finish(self):
        for copy in self.open:
            copy.wait_send()


class Loads:
    def __init__(self, sems):
        self.sems, self.used = sems, 0

    def start(self, src, dst):
        copy = pltpu.make_async_copy(src, dst, self.sems.at[self.used])
        self.used += 1
        copy.start()
        return copy


def remote_copy_count(pairs):
    return 72 + 9 * 4 * pairs + 8 * pairs


def layer_kernel(
    n_dp,
    tok_hbm,
    cot_hbm,
    len_hbm,
    lab_hbm,
    wqkv_hbm,
    qvb_hbm,
    wout_hbm,
    bb_hbm,
    ng_hbm,
    ns_hbm,
    wup_hbm,
    upb_hbm,
    wdn_hbm,
    wpool_hbm,
    pb_hbm,
    wcls_hbm,
    cb_hbm,
    bout_out,
    gtok_out,
    gqkvo_out,
    gup_out,
    gdn_out,
    gpool_out,
    vec_out,
    len_ref,
    lab_ref,
    cb_ref,
    qvb_ref,
    bb_ref,
    ng_ref,
    ns_ref,
    upb_ref,
    pb_ref,
    wcls_ref,
    tok,
    cot,
    wt,
    wo,
    wup,
    wdn,
    wpool,
    wup_tr,
    wdn_tr,
    wpool_tr,
    up_bias,
    bias_mask,
    k_pad,
    v_pad,
    k_tr,
    v_tr,
    q_pad,
    q_away,
    probs,
    ctx,
    hid,
    hid_low,
    hid_tr,
    tok_tr,
    n_one,
    scale_one,
    act_low,
    d_gelu,
    acc,
    parts,
    d_sec,
    d_br,
    d_br_tr,
    d_br_peer,
    d_pre_low,
    d_pre_peer,
    act_peer,
    hid_peer,
    ctx_peer,
    d_att_peer,
    d_qkv_peer,
    d_first,
    d_att,
    d_att_tr,
    d_ctx,
    d_kv_f32,
    d_kv_send,
    d_kv_recv,
    d_qkv,
    g_low,
    first_recv,
    second_send,
    second_recv,
    last_send,
    last_recv,
    pool_fin,
    items,
    items_c,
    item_all,
    vec,
    vec_c,
    vec_s,
    vec_y,
    vec_t,
    vec_r,
    vec_q,
    cnt,
    cnt_y,
    cnt_s,
    cnt_r,
    cnt_q,
    load_sems,
    send_sems,
    recv_sems,
):
    pairs = n_dp // 4
    dp = lax.axis_index("dp")
    me = lax.axis_index("tensor")
    x = me // 2
    c = lax.rem(me, 2)
    y = lax.rem(dp, 2)
    r = lax.rem(dp // 2, 2)
    q = dp // 4
    core_dev = (dp, me + 1 - 2 * c)
    x_dev = (dp, 2 * (1 - x) + c)
    y_dev = (dp + 1 - 2 * y, me)
    r_dev = (dp + 2 - 4 * r, me)

    def q_of(k):
        return lax.rem(q + k, pairs)

    def q_dev(k):
        return (q_of(k) * 4 + r * 2 + y, me)

    away = range(1, pairs)
    token_count, width = tok.shape
    half = token_count // 2
    local_width = wo.shape[1]
    heads = local_width // HD
    slots = len_ref.shape[1]
    shard = width // n_dp
    chunk = 128
    chunks = half // chunk
    fine = 128
    fines = half // fine
    tile = 256
    tiles = width // tile
    own_rows = pl.ds(pl.multiple_of(c * half, half), half)
    away_rows = pl.ds(pl.multiple_of((1 - c) * half, half), half)

    barrier = pltpu.get_barrier_semaphore()
    peers = [core_dev, x_dev, y_dev, r_dev] + [q_dev(k) for k in away]
    for peer in peers:
        pl.semaphore_signal(barrier, inc=1, device_id=peer, device_id_type=MESH)

    loads = Loads(load_sems)
    remote = Copies(send_sems, recv_sems)
    load_len = loads.start(len_hbm, len_ref)
    load_tok = loads.start(tok_hbm, tok)
    load_wt = loads.start(wqkv_hbm, wt.at[c])
    load_qvb = loads.start(qvb_hbm, qvb_ref)
    load_upb = loads.start(upb_hbm, upb_ref)
    load_lab = loads.start(lab_hbm, lab_ref)
    load_small = [
        loads.start(src, dst)
        for src, dst in (
            (cb_hbm, cb_ref),
            (bb_hbm, bb_ref),
            (ng_hbm, ng_ref),
            (ns_hbm, ns_ref),
            (pb_hbm, pb_ref),
            (wcls_hbm, wcls_ref),
        )
    ]
    load_wo = loads.start(wout_hbm, wo.at[c])
    load_wup = loads.start(wup_hbm, wup.at[c])
    load_wdn = loads.start(wdn_hbm, wdn.at[c])
    load_pool = loads.start(wpool_hbm, wpool)
    load_cot = loads.start(cot_hbm.at[own_rows], cot)

    load_len.wait()
    load_lab.wait()
    lengths = [len_ref[0, i] for i in range(slots)]
    ends, total = [], 0
    for i in range(slots):
        total = total + lengths[i]
        ends.append(total)
    firsts = [jnp.minimum(ends[i] - lengths[i], token_count - 1) for i in range(slots)]
    key_place = lax.broadcasted_iota(jnp.int32, (token_count, 128), 0)
    query_place = lax.broadcasted_iota(jnp.int32, (8, half), 1) + c * half
    key_segment = jnp.zeros((token_count, 128), jnp.int32)
    query_segment = jnp.zeros((8, half), jnp.int32)
    for i in range(slots):
        key_segment = key_segment + (key_place >= ends[i]).astype(jnp.int32)
        query_segment = query_segment + (query_place >= ends[i]).astype(jnp.int32)
    for n in range(half // 128):
        cols = slice(n * 128, (n + 1) * 128)
        bias_mask[:, cols] = jnp.where(key_segment == query_segment[0:1, cols], 0.0, masked_score)
    item_row = lax.broadcasted_iota(jnp.int32, (slots, 128), 0)
    first_col = jnp.zeros((slots, 128), jnp.int32)
    len_col = jnp.zeros((slots, 128), jnp.int32)
    lab_col = jnp.zeros((slots, 128), jnp.int32)
    for i in range(slots):
        first_col = first_col + jnp.where(item_row == i, firsts[i], 0)
        len_col = len_col + jnp.where(item_row == i, lengths[i], 0)
        lab_col = lab_col + jnp.where(item_row == i, lab_ref[0, i], 0)
    live_all = jnp.where(len_col > 0, 1.0, 0.0)
    cnt[...] = jnp.broadcast_to(col_sum(live_all), cnt.shape)
    lane_item = lax.broadcasted_iota(jnp.int32, (1, 2 * slots), 1)
    first_row = jnp.zeros((1, 2 * slots), jnp.int32)
    for i in range(slots):
        first_row = first_row + jnp.where((lane_item == i) | (lane_item == i + slots), firsts[i], 0)

    load_upb.wait()
    up_bias[c] = jnp.broadcast_to(upb_ref[...].astype(F32).reshape(1, width), (8, width))
    vec[...] = jnp.zeros_like(vec)
    pad_rows = q_pad.shape[1] - local_width
    for b in range(2):
        q_pad[b, local_width:, :] = jnp.zeros((pad_rows, half), BF16)
        d_ctx[b, local_width:, :] = jnp.zeros((pad_rows, half), BF16)
        v_pad[b, :, local_width:] = jnp.zeros((token_count, pad_rows), BF16)

    def bias_cols(part, columns):
        row = qvb_ref[part : part + 1, :]
        block = jnp.transpose(jnp.broadcast_to(row, (128, local_width)))
        return jnp.concatenate([block] * (columns // 128), axis=1)

    load_tok.wait()
    load_wt.wait()
    load_qvb.wait()
    rows_q, rows_k, rows_v = [slice(p * local_width, (p + 1) * local_width) for p in range(3)]
    query_bias = bias_cols(0, half)
    q_away[...] = (dot_nt(wt[c, rows_q, :], tok[away_rows, :]) + query_bias).astype(BF16)
    wide_k = jnp.concatenate([wt[c, rows_k, :], jnp.zeros((pad_rows, width), BF16)], axis=0)
    k_pad[c] = dot_nt(tok[...], wide_k).astype(BF16)
    v_tr[c] = (dot_nt(wt[c, rows_v, :], tok[...]) + bias_cols(1, token_count)).astype(BF16)
    q_pad[c, 0:local_width, :] = (dot_nt(wt[c, rows_q, :], tok[own_rows, :]) + query_bias).astype(BF16)

    pl.semaphore_wait(barrier, len(peers))
    mark("sends")
    send_q = remote.start(q_away, q_pad.at[c, pl.ds(0, local_width)], core_dev)
    send_k = remote.start(k_pad.at[c], k_pad.at[c], core_dev)
    send_v = remote.start(v_tr.at[c], v_tr.at[c], core_dev)
    send_wo = remote.start(wout_hbm, wo.at[c], core_dev)
    send_bias = remote.start(up_bias.at[c], up_bias.at[c], core_dev)
    send_wup = remote.start(wup_hbm, wup.at[c], core_dev)
    send_wdn = remote.start(wdn_hbm, wdn.at[c], core_dev)
    send_cnt_y = remote.start(cnt, cnt_y, y_dev)
    send_wt = remote.start(wqkv_hbm, wt.at[c], core_dev)

    half_row = lax.broadcasted_iota(jnp.int32, (128, half), 0) < HD
    inv_root = HD ** (-0.5)

    def half_of(block, i):
        if i == heads - 1 and i % 2 == 0:
            return block
        zero = jnp.zeros_like(block)
        return jnp.where(half_row, block, zero) if i % 2 == 0 else jnp.where(half_row, zero, block)

    def pair_of(i):
        return slice((i // 2) * 128, (i // 2 + 1) * 128)

    def attend(core):
        for i in range(heads):
            head_rows = slice(i * HD, (i + 1) * HD)
            scores = dot_nn(k_pad[core, :, pair_of(i)], half_of(q_pad[core, pair_of(i), :], i))
            scores = scores * inv_root + bias_mask[...]
            terms = jnp.exp(scores - jnp.max(scores, axis=0, keepdims=True))
            weights = terms * (1.0 / col_sum(terms))
            probs[core, i] = weights
            ctx[core, head_rows, :] = dot_nn(v_tr[core, head_rows, :], weights.astype(BF16)).astype(BF16)

    mark("attn_own")
    attend(c)
    send_q.wait_recv()
    send_k.wait_recv()
    send_v.wait_recv()
    mark("attn_other")
    attend(1 - c)
    mark("out")
    for load in load_small:
        load.wait()
    send_ctx = remote.start(ctx.at[1 - c], ctx_peer, core_dev)
    load_wo.wait()
    send_wo.wait_recv()

    def chunk_of(i):
        return slice(i * chunk, (i + 1) * chunk)

    def exchange(which, rows):
        block = parts.at[which, x, rows]
        return remote.start(block, block, x_dev)

    def fine_of(i):
        return slice(i * fine, (i + 1) * fine)

    def both_parts(which, rows):
        return parts[which, 0, rows, :].astype(F32) + parts[which, 1, rows, :].astype(F32)

    ATT, FFN, HIDDEN, TOKEN = 0, 1, 2, 3
    send_att = []
    for i in range(chunks):
        rows = chunk_of(i)
        partial_sum = dot_tn(ctx[0, :, rows], wo[0]) + dot_tn(ctx[1, :, rows], wo[1])
        parts[ATT, x, rows, :] = partial_sum.astype(BF16)
        for j in range(i * chunk // fine, (i + 1) * chunk // fine):
            send_att.append(exchange(ATT, fine_of(j)))
    send_cnt_y.wait_recv()
    cnt_s[...] = cnt[...] + cnt_y[...]
    send_cnt_r = remote.start(cnt_s, cnt_r, r_dev)

    mark("transposes")
    for b in range(2):
        k_tr[b] = jnp.transpose(k_pad[b])[0:local_width, :]
        v_pad[b, :, 0:local_width] = jnp.transpose(v_tr[b])
    tok_tr[0] = jnp.transpose(tok[own_rows, :])
    tok_tr[1] = jnp.transpose(tok[away_rows, :])

    load_wup.wait()
    load_wdn.wait()
    load_pool.wait()
    wpool_tr[...] = jnp.transpose(wpool[...])
    send_wup.wait_recv()
    send_wdn.wait_recv()
    for b in range(2):
        wup_tr[b] = jnp.transpose(wup[b])
        wdn_tr[b] = jnp.transpose(wdn[b])

    mark("ffn_f")
    send_ffn, send_hid, send_act = [], [], []
    for i in range(fines):
        rows = fine_of(i)
        send_att[i].wait_recv()
        token_rows = pl.ds(pl.multiple_of(c * half + i * fine, fine), fine)
        attention = both_parts(ATT, rows) + bb_ref[0:1, :]
        normed, inv_scale = norm_forward(tok[token_rows, :].astype(F32) + attention)
        n_one[rows, :] = normed
        scale_one[rows, :] = inv_scale
        value = normed * ng_ref[0:1, :] + ns_ref[0:1, :]
        hid[rows, :] = value
        hid_low[rows, :] = value.astype(BF16)
        send_hid.append(remote.start(hid_low.at[rows], hid_peer.at[rows], core_dev))
        for b in range(2):
            core = c if b == 0 else 1 - c
            if i == 0 and b == 1:
                send_bias.wait_recv()
                send_wup.wait_recv()
            for n in range(tiles):
                cols = slice(n * tile, (n + 1) * tile)
                pre_act = dot_nn(hid_low[rows, :], wup[core, :, cols]) + up_bias[core, 0:1, cols]
                value, slope = gelu_parts(pre_act)
                act_low[b, rows, cols] = value.astype(BF16)
                d_gelu[b, rows, cols] = slope
            if i == 0 and b == 1:
                send_wdn.wait_recv()
            product = dot_nn(act_low[b, rows, :], wdn[core])
            if b == 0:
                acc[0:fine, :] = product
            else:
                parts[FFN, x, rows, :] = (acc[0:fine, :] + product).astype(BF16)
        send_ffn.append(exchange(FFN, rows))
        send_act.append(remote.start(act_low.at[1, rows], act_peer.at[rows], core_dev))
        if i == 0:
            send_cnt_r.wait_recv()
            cnt_q[q] = cnt_s[...] + cnt_r[...]
            send_cnt_q = [remote.start(cnt_q.at[q], cnt_q.at[q], q_dev(k)) for k in away]

    mark("hid_tr")
    hid_tr[0] = jnp.transpose(hid_low[...])
    for copy in send_hid:
        copy.wait_recv()
    hid_tr[1] = jnp.transpose(hid_peer[...])
    load_cot.wait()
    for copy in send_cnt_q:
        copy.wait_recv()
    item_count = cnt_q[0]
    for k in away:
        item_count = item_count + cnt_q[k]
    inv_count = 1.0 / item_count[0:1, 0:1]

    classes = wcls_ref.shape[0]
    class_rows = wcls_ref[...].astype(F32)
    class_pad = jnp.concatenate([class_rows, jnp.zeros((16 - classes, width), F32)], axis=0).astype(BF16)
    class_lane = lax.broadcasted_iota(jnp.int32, (slots, 16), 1)
    class_bias = jnp.zeros((slots, 16), F32)
    for k in range(classes):
        class_bias = class_bias + jnp.where(class_lane == k, cb_ref[0, k], 0.0)
    label_hot = jnp.where(class_lane == lab_col[:, 0:1], 1.0, 0.0)
    lane = lax.broadcasted_iota(jnp.int32, (1, 128), 1)

    def add_rows(first, value):
        vec[first : first + value.shape[0], 0 : value.shape[1]] += value

    mark("ln2")
    up_sums = [[None] * tiles, [None] * tiles]
    send_hidden, send_br, send_pre = [], [], []
    for i in range(chunks):
        rows = chunk_of(i)
        place = c * half + i * chunk
        for j in range(i * chunk // fine, (i + 1) * chunk // fine):
            send_ffn[j].wait_recv()
        normed, inv_scale = norm_forward(hid[rows, :] + (both_parts(FFN, rows) + bb_ref[1:2, :]))
        low = (normed * ng_ref[1:2, :] + ns_ref[1:2, :]).astype(BF16)
        bout_out[pl.ds(pl.multiple_of(place, chunk), chunk), :] = low

        local_first = first_col[:, 0:1] - place
        pick = (lax.broadcasted_iota(jnp.int32, (slots, chunk), 1) == local_first).astype(F32).astype(BF16)
        picked = dot_nn(pick, low).astype(BF16)
        pooled = jnp.tanh(dot_nn(picked, wpool[...]) + pb_ref[...].reshape(1, width))
        pooled_low = pooled.astype(BF16)
        logits = jnp.where(class_lane < classes, dot_nt(pooled_low, class_pad) + class_bias, masked_score)
        shifted = logits - jnp.max(logits, axis=1, keepdims=True)
        log_probs = shifted - jnp.log(jnp.sum(jnp.exp(shifted), axis=1, keepdims=True))
        class_probs = jnp.exp(log_probs)
        owned = jnp.where((local_first >= 0) & (local_first < chunk), live_all[:, 0:1], 0.0)
        item_ce = -jnp.sum(label_hot * log_probs, axis=1, keepdims=True) * owned
        item_ent = -jnp.sum(class_probs * log_probs, axis=1, keepdims=True) * owned
        d_logits = (class_probs - label_hot) * (owned * inv_count)
        d_pooled = jnp.zeros((slots, width), F32)
        for k in range(classes):
            d_pooled = d_pooled + d_logits[:, k : k + 1] * class_rows[k : k + 1, :]
            add_rows(7 + k, col_sum(d_logits[:, k : k + 1] * pooled_low.astype(F32)))
        d_pre = (d_pooled * (1.0 - pooled * pooled)).astype(BF16)
        add_rows(6, col_sum(d_pre.astype(F32)))
        add_rows(
            10, jnp.where(lane == 0, col_sum(item_ce), 0.0) + jnp.where(lane == 1, col_sum(item_ent), 0.0)
        )
        vec[10:11, 128:144] += col_sum(d_logits)
        if i == 0:
            items[0] = picked
            items[1] = d_pre
        else:
            items[0] += picked
            items[1] += d_pre
        if i == chunks - 1:
            send_items = remote.start(items.at[1 - c], items_c, core_dev)
        d_picked = dot_nn(d_pre, wpool_tr[...])
        d_high = d_picked.astype(BF16)
        d_both = jnp.concatenate([d_high, (d_picked - d_high.astype(F32)).astype(BF16)], axis=0)

        token_place = lax.broadcasted_iota(jnp.int32, (chunk, 2 * slots), 0) + place
        spread = dot_nn((token_place == first_row).astype(F32).astype(BF16), d_both)
        live = jnp.where(token_place[:, 0:1] < total, 1.0, 0.0)
        d_output = cot[rows, :].astype(F32) * live + spread
        add_rows(3, col_sum(d_output * normed))
        add_rows(5, col_sum(d_output))
        d_second = norm_backward(d_output, normed, inv_scale, ng_ref[1:2, :])
        add_rows(1, col_sum(d_second))
        d_sec[rows, :] = d_second
        d_br[rows, :] = d_second.astype(BF16)
        send_br.append(remote.start(d_br.at[rows], d_br_peer.at[rows], core_dev))
        for b in range(2):
            core = c if b == 0 else 1 - c
            for n in range(tiles):
                cols = slice(n * tile, (n + 1) * tile)
                d_act = dot_nn(d_br[rows, :], wdn_tr[core, :, cols])
                low = (d_act * d_gelu[b, rows, cols]).astype(BF16)
                d_pre_low[b, rows, cols] = low
                up_sum = col_sum(low.astype(F32))
                up_sums[b][n] = up_sum if i == 0 else up_sums[b][n] + up_sum
            product = dot_nn(d_pre_low[b, rows, :], wup_tr[core])
            if b == 0:
                acc[...] = product
            else:
                parts[HIDDEN, x, rows, :] = (acc[...] + product).astype(BF16)
        send_hidden.append(exchange(HIDDEN, rows))
        send_pre.append(remote.start(d_pre_low.at[1, rows], d_pre_peer.at[rows], core_dev))
    vec[pl.ds(11 + c, 1), :] = jnp.concatenate(up_sums[0], axis=1)
    vec[pl.ds(12 - c, 1), :] = jnp.concatenate(up_sums[1], axis=1)
    send_out = remote.start(bout_out.at[own_rows], bout_out.at[own_rows], core_dev)

    DOWN, UP, QKVO = 0, tiles, 2 * tiles
    y_first, r_first = (y, r, y_dev, r_dev), (r, y, r_dev, y_dev)
    along = [y_first if letter == "y" else r_first for letter in ORDERS]
    row_major = [letter == "r" for letter in ORDERS]
    reach = {1: list(away), 0: [0]}
    slot_of = {(flip, k): (1 - flip) * pairs + (k - 1) % pairs for flip in range(2) for k in range(pairs)}
    sent = {}
    step = {}

    def store_blocks(block, product):
        for j in range(n_dp):
            bits = (j % 2, (j // 2) % 2)
            if row_major[block]:
                bits = bits[::-1]
            g_low[block, bits[0], bits[1], j // 4] = product[j * shard : (j + 1) * shard, :].astype(BF16)

    def fill(block, product_of):
        for n in range(tiles):
            store_blocks(block + n, product_of(slice(n * tile, (n + 1) * tile)))

    def first_step(block, flip, group):
        first, second, device, _ = along[block]
        for k in reach[group]:
            source = g_low.at[block, 1 - first, 1 - second if flip else second, q_of(k)]
            sent[block, 1, flip, k] = remote.start(source, first_recv.at[block, slot_of[flip, k]], device)

    def first_sum(block, flip, k):
        first, second, _, _ = along[block]
        sent[block, 1, flip, k].wait_recv()
        value = g_low[block, first, 1 - second if flip else second, q_of(k)].astype(F32)
        return value + first_recv[block, slot_of[flip, k]].astype(F32)

    def second_step(block, group):
        for k in reach[group]:
            second_send[block, k] = first_sum(block, 1, k).astype(BF16)
            sent[block, 2, k] = remote.start(second_send.at[block, k], second_recv.at[block, k], along[block][3])

    def second_sum(block, k):
        sent[block, 2, k].wait_recv()
        return first_sum(block, 0, k) + second_recv[block, k].astype(F32)

    def last_step(block):
        for k in away:
            last_send[block, k - 1] = second_sum(block, k).astype(BF16)
            sent[block, 3, k] = remote.start(last_send.at[block, k - 1], last_recv.at[block, k - 1], q_dev(k))

    def end_step(block, out):
        result = second_sum(block, 0)
        for k in away:
            sent[block, 3, k].wait_recv()
            result = result + last_recv[block, k - 1].astype(F32)
        n = block % tiles
        out[:, n * tile : (n + 1) * tile] = result

    for letter, first_block, out in (("D", DOWN, gdn_out), ("U", UP, gup_out), ("Q", QKVO, gqkvo_out)):
        for n in range(tiles):
            block, name = first_block + n, letter + str(n)
            for group in range(2):
                for flip in range(2):
                    step["F%s_%d%d" % (name, flip, group)] = partial(first_step, block, flip, group)
                step["S%s_%d" % (name, group)] = partial(second_step, block, group)
            step["L" + name] = partial(last_step, block)
            step["E" + name] = partial(end_step, block, out)

    def fill_down(n):
        if n == 0:
            d_br_tr[0] = jnp.transpose(d_br[...])
            for copy in send_br + send_act:
                copy.wait_recv()
            d_br_tr[1] = jnp.transpose(d_br_peer[...])
        cols = slice(n * tile, (n + 1) * tile)
        store_blocks(DOWN + n, dot_nn(d_br_tr[0], act_low[0, :, cols]) + dot_nn(d_br_tr[1], act_peer[:, cols]))

    def fill_up(n):
        for copy in send_pre:
            copy.wait_recv()
        cols = slice(n * tile, (n + 1) * tile)
        store_blocks(UP + n, dot_nn(hid_tr[0], d_pre_low[0, :, cols]) + dot_nn(hid_tr[1], d_pre_peer[:, cols]))

    for n in range(tiles):
        step["fd%d" % n] = partial(fill_down, n)
        step["fu%d" % n] = partial(fill_up, n)

    def item_rows(first, count):
        return pl.ds(pl.multiple_of(first * slots, count * slots), count * slots)

    def pass_items(name, rows, devices):
        block = item_all.at[c, x, rows]
        sent[name] = [remote.start(block, block, device) for device in devices]

    def settle(name):
        for copy in sent[name]:
            copy.wait_recv()

    def items_y():
        send_items.wait_recv()
        both = items[c] + items_c[...]
        item_all[c, x, item_rows(dp, 1), :] = jnp.where(x == 0, both[:, : width // 2], both[:, width // 2 :])
        pass_items("items_y", item_rows(dp, 1), [y_dev])

    def items_r():
        settle("items_y")
        pass_items("items_r", item_rows(dp - y, 2), [r_dev])

    def items_q():
        settle("items_r")
        pass_items("items_q", item_rows(q * 4, 4), [q_dev(k) for k in away])

    def items_x():
        settle("items_q")
        sent["items_x"] = [remote.start(item_all.at[c, x], item_all.at[c, x], x_dev)]

    def items_core():
        settle("items_x")
        sent["items_core"] = [remote.start(item_all.at[c], item_all.at[c], core_dev)]

    def pool():
        settle("items_core")
        picked_all, d_pre_all = [jnp.concatenate([item_all[p, 0], item_all[p, 1]], axis=1) for p in range(2)]
        pool_fin[...] = dot_tn(picked_all, d_pre_all)
        gpool_out[...] = pool_fin[pl.ds(pl.multiple_of(dp * shard, 8), shard), :]

    step.update(I_y=items_y, I_r=items_r, I_q=items_q, I_x=items_x, I_c=items_core, pool=pool)

    def norm_one_back(i):
        rows = chunk_of(i)
        send_hidden[i].wait_recv()
        d_hidden = both_parts(HIDDEN, rows) + d_sec[rows, :]
        normed = n_one[rows, :]
        add_rows(2, col_sum(d_hidden * normed))
        add_rows(4, col_sum(d_hidden))
        gradient = norm_backward(d_hidden, normed, scale_one[rows, :], ng_ref[0:1, :])
        add_rows(0, col_sum(gradient))
        d_first[rows, :] = gradient
        d_att[rows, :] = gradient.astype(BF16)
        sent["d_att", i] = remote.start(d_att.at[rows], d_att_peer.at[rows], core_dev)

    def context_back():
        for b in range(2):
            d_ctx[b, 0:local_width, :] = dot_nt(wo[b], d_att[...]).astype(BF16)

    def head_back(n):
        b, i = n // heads, n % heads
        head_rows = slice(i * HD, (i + 1) * HD)
        d_probs = dot_nn(v_pad[b, :, pair_of(i)], half_of(d_ctx[b, pair_of(i), :], i))
        weights = probs[b, i]
        delta = col_sum(weights * d_probs)
        d_scores = (weights * (d_probs - delta)).astype(BF16)
        d_value = dot_nt(d_ctx[b, head_rows, :], weights.astype(BF16))
        d_key = dot_nt(q_pad[b, head_rows, :], d_scores) * inv_root
        d_query = dot_nn(k_tr[b, head_rows, :], d_scores) * inv_root
        d_qkv[b, head_rows, :] = d_query.astype(BF16)
        for part, value in ((0, d_key), (1, d_value)):
            part_rows = slice(part * local_width + i * HD, part * local_width + (i + 1) * HD)
            for side in range(2):
                lanes = slice(side * half, (side + 1) * half)
                d_kv_f32[side, b, part_rows, :] = value[:, lanes]
                d_kv_send[side, b, part_rows, :] = value[:, lanes].astype(BF16)
        if n == 2 * heads - 1:
            sent["kv"] = remote.start(d_kv_send.at[1 - c], d_kv_recv, core_dev)

    def turn_attention():
        d_att_tr[0] = jnp.transpose(d_att[...])
        for i in range(chunks):
            sent["d_att", i].wait_recv()
        d_att_tr[1] = jnp.transpose(d_att_peer[...])

    def join_cores():
        sent["kv"].wait_recv()
        for b in range(2):
            d_qkv[b, local_width:, :] = (d_kv_f32[c, b] + d_kv_recv[b].astype(F32)).astype(BF16)
        sent["d_qkv"] = remote.start(d_qkv.at[1 - c], d_qkv_peer, core_dev)

    for i in range(chunks):
        step["ln1b%d" % i] = partial(norm_one_back, i)
    step["dctx"] = context_back
    for n in range(2 * heads):
        step["ab%d" % n] = partial(head_back, n)
    step["dattT"] = turn_attention
    step["dsum"] = join_cores

    def fill_qkvo():
        sent["d_qkv"].wait_recv()
        send_ctx.wait_recv()
        first_part = dot_nt(tok_tr[0], d_qkv[c]) + dot_nt(tok_tr[1], d_qkv_peer[...])
        second_part = dot_nt(d_att_tr[0], ctx[c]) + dot_nt(d_att_tr[1], ctx_peer[...])
        both = jnp.concatenate([first_part, second_part], axis=1)
        fill(QKVO, lambda cols: both[:, cols])

    def token_part(i):
        send_wt.wait_recv()
        rows = chunk_of(i)
        partial_sum = dot_tn(d_qkv[0, :, rows], wt[0]) + dot_tn(d_qkv[1, :, rows], wt[1])
        parts[TOKEN, x, rows, :] = partial_sum.astype(BF16)
        sent["token", i] = exchange(TOKEN, rows)

    def token_end(i):
        sent["token", i].wait_recv()
        rows = chunk_of(i)
        place = pl.ds(pl.multiple_of(c * half + i * chunk, chunk), chunk)
        gtok_out[place, :] = (both_parts(TOKEN, rows) + d_first[rows, :]).astype(BF16)
        if i == chunks - 1:
            sent["gtok"] = remote.start(gtok_out.at[own_rows], gtok_out.at[own_rows], core_dev)

    step["fq"] = fill_qkvo
    for i in range(chunks):
        step["dtok%d" % i] = partial(token_part, i)
        step["gtok%d" % i] = partial(token_end, i)

    def vec_rows(core):
        return pl.ds(pl.multiple_of(core * VEC_ROWS // 2, VEC_ROWS // 2), VEC_ROWS // 2)

    def vec_core():
        ones = jnp.ones((8, half), BF16)
        sums = [dot_nt(ones, d_qkv[b])[0:1, :] for b in range(2)]
        columns = [v[:, :local_width] for v in sums] + [v[:, 2 * local_width :] for v in sums]
        vec[13:14, :] = jnp.concatenate(columns, axis=1)
        vec[14:15, 0:128] = item_count[0:1, :]
        sent["vec"] = remote.start(vec.at[vec_rows(1 - c)], vec_c, core_dev)

    def vec_along_y():
        sent["vec"].wait_recv()
        vec_s[...] = vec[vec_rows(c), :] + vec_c[...]
        sent["vec_y"] = remote.start(vec_s, vec_y, y_dev)

    def vec_along_r():
        sent["vec_y"].wait_recv()
        vec_t[...] = vec_s[...] + vec_y[...]
        sent["vec_r"] = remote.start(vec_t, vec_r, r_dev)

    def vec_along_q():
        sent["vec_r"].wait_recv()
        vec_q[q] = vec_t[...] + vec_r[...]
        sent["vec_q"] = [remote.start(vec_q.at[q], vec_q.at[q], q_dev(k)) for k in away]

    def vec_end():
        settle("vec_q")
        vec_total = vec_q[0]
        for k in away:
            vec_total = vec_total + vec_q[k]
        vec_out[vec_rows(c), :] = vec_total
        sent["vec_out"] = remote.start(vec_out.at[vec_rows(c)], vec_out.at[vec_rows(c)], core_dev)

    step.update(qv=vec_core, V_y=vec_along_y, V_r=vec_along_r, V_q=vec_along_q, V_e=vec_end)

    assert sorted(PLAN) == sorted(step)
    for name in PLAN:
        mark(name)
        step[name]()
    mark("finish")
    send_out.wait_recv()
    sent["gtok"].wait_recv()
    sent["vec_out"].wait_recv()
    remote.finish()


def place_kernel(
    n_dp,
    bout_in,
    gtok_in,
    gqkvo_in,
    gup_in,
    gdn_in,
    gpool_in,
    vec_in,
    bout_out,
    gtok_out,
    loss_out,
    entropy_out,
    gqkv_out,
    gqv_out,
    gout_out,
    gbranch_out,
    ggain_out,
    gshift_out,
    gup_out,
    gupb_out,
    gdn_out,
    gpool_out,
    gpoolb_out,
    gclass_out,
    gclassb_out,
    loss,
    entropy,
    gqkv,
    gqv,
    gout,
    gbranch,
    ggain,
    gshift,
    gupb,
    gpoolb,
    gclass,
    gclassb,
    sems,
):
    moves = ((bout_in, bout_out), (gtok_in, gtok_out), (gup_in, gup_out), (gdn_in, gdn_out), (gpool_in, gpool_out))
    copies = []

    def send(src, dst):
        copy = pltpu.make_async_copy(src, dst, sems.at[len(copies)])
        copy.start()
        copies.append(copy)

    for src, dst in moves:
        send(src, dst)
    dp = lax.axis_index("dp")
    c = lax.rem(lax.axis_index("tensor"), 2)
    width = vec_in.shape[1]
    shard = width // n_dp
    local_width = gout.shape[0]
    for part in range(3):
        gqkv[part] = gqkvo_in[:, part * local_width : (part + 1) * local_width]
    send(gqkv, gqkv_out)
    gout[...] = jnp.transpose(gqkvo_in[:, 3 * local_width :])
    send(gout, gout_out)
    sums = vec_in[...]
    mine = pltpu.roll(sums, lax.rem(width - dp * shard, width), axis=1)
    gbranch[...] = mine[0:2, :shard]
    ggain[...] = mine[2:4, :shard]
    gshift[...] = mine[4:6, :shard]
    gpoolb[...] = mine[6:7, :shard]
    gclass[...] = mine[7 : 7 + gclass.shape[0], :shard]
    gupb[...] = jnp.where(c == 0, mine[11:12, :shard], mine[12:13, :shard])
    small = local_width // n_dp
    quarter = pltpu.roll(sums, lax.rem(width - (c * local_width + dp * small), width), axis=1)
    gqv[0:1, :] = quarter[13:14, :small]
    gqv[1:2, :] = quarter[13:14, 2 * local_width : 2 * local_width + small]
    inv_count = 2.0 * n_dp / sums[14:15, 0:1]
    loss[...] = sums[10:11, 0:1] * inv_count
    entropy[...] = sums[10:11, 1:2] * inv_count
    gclassb[...] = sums[10:11, 128 : 128 + gclassb.shape[1]]
    small_moves = (
        (loss, loss_out),
        (entropy, entropy_out),
        (gqv, gqv_out),
        (gbranch, gbranch_out),
        (ggain, ggain_out),
        (gshift, gshift_out),
        (gupb, gupb_out),
        (gpoolb, gpoolb_out),
        (gclass, gclass_out),
        (gclassb, gclassb_out),
    )
    for src, dst in small_moves:
        send(src, dst)
    for copy in copies:
        copy.wait()


def on_device(
    n_dp,
    tokens,
    cotangent,
    lengths,
    labels,
    w_qkv,
    qv_bias,
    w_out,
    branch_bias,
    norm_gain,
    norm_shift,
    w_up,
    up_bias,
    w_down,
    w_pool,
    pool_bias,
    w_class,
    class_bias,
):
    token_count, width = tokens.shape
    local_width = w_out.shape[0]
    hidden = w_up.shape[1]
    classes = w_class.shape[1]
    slots = lengths.shape[1]
    pairs = n_dp // 4
    shard = width // n_dp
    half = token_count // 2
    heads = local_width // HD
    padded = (local_width + 127) // 128 * 128
    assert hidden == width and 4 * local_width == width and lengths.shape[0] == 1
    shape = jax.ShapeDtypeStruct
    anywhere = pl.BlockSpec(memory_space=pl.ANY)
    vmem = pl.BlockSpec(memory_space=pltpu.VMEM)
    pieces = 3 * width // 256
    blocks = (pieces, 2, 2, pairs, shard, 256)
    copies = remote_copy_count(pairs)
    V = pltpu.VMEM
    S = pltpu.SMEM
    scratch = dict(
        len_ref=S(lengths.shape, jnp.int32),
        lab_ref=S(labels.shape, jnp.int32),
        cb_ref=S((1, classes), F32),
        qvb_ref=V(qv_bias.shape, F32),
        bb_ref=V(branch_bias.shape, F32),
        ng_ref=V(norm_gain.shape, F32),
        ns_ref=V(norm_shift.shape, F32),
        upb_ref=V(up_bias.shape, BF16),
        pb_ref=V(pool_bias.shape, F32),
        wcls_ref=V((classes, width), BF16),
        tok=V((token_count, width), BF16),
        cot=V((half, width), BF16),
        wt=V((2, 3 * local_width, width), BF16),
        wo=V((2, local_width, width), BF16),
        wup=V((2, width, hidden), BF16),
        wdn=V((2, hidden, width), BF16),
        wpool=V((width, width), BF16),
        wup_tr=V((2, hidden, width), BF16),
        wdn_tr=V((2, width, hidden), BF16),
        wpool_tr=V((width, width), BF16),
        up_bias=V((2, 8, width), F32),
        bias_mask=V((token_count, half), F32),
        k_pad=V((2, token_count, padded), BF16),
        v_pad=V((2, token_count, padded), BF16),
        k_tr=V((2, local_width, token_count), BF16),
        v_tr=V((2, local_width, token_count), BF16),
        q_pad=V((2, padded, half), BF16),
        q_away=V((local_width, half), BF16),
        probs=V((2, heads, token_count, half), F32),
        ctx=V((2, local_width, half), BF16),
        hid=V((half, width), F32),
        hid_low=V((half, width), BF16),
        hid_tr=V((2, width, half), BF16),
        tok_tr=V((2, width, half), BF16),
        n_one=V((half, width), F32),
        scale_one=V((half, 1), F32),
        act_low=V((2, half, hidden), BF16),
        d_gelu=V((2, half, hidden), F32),
        acc=V((128, width), F32),
        parts=V((4, 2, half, width), BF16),
        d_sec=V((half, width), F32),
        d_br=V((half, width), BF16),
        d_br_tr=V((2, width, half), BF16),
        d_br_peer=V((half, width), BF16),
        d_pre_low=V((2, half, hidden), BF16),
        d_pre_peer=V((half, hidden), BF16),
        act_peer=V((half, hidden), BF16),
        hid_peer=V((half, width), BF16),
        ctx_peer=V((local_width, half), BF16),
        d_att_peer=V((half, width), BF16),
        d_qkv_peer=V((3 * local_width, half), BF16),
        d_first=V((half, width), F32),
        d_att=V((half, width), BF16),
        d_att_tr=V((2, width, half), BF16),
        d_ctx=V((2, padded, half), BF16),
        d_kv_f32=V((2, 2, 2 * local_width, half), F32),
        d_kv_send=V((2, 2, 2 * local_width, half), BF16),
        d_kv_recv=V((2, 2 * local_width, half), BF16),
        d_qkv=V((2, 3 * local_width, half), BF16),
        g_low=V(blocks, BF16),
        first_recv=V((pieces, 2 * pairs, shard, 256), BF16),
        second_send=V((pieces, pairs, shard, 256), BF16),
        second_recv=V((pieces, pairs, shard, 256), BF16),
        last_send=V((pieces, pairs - 1, shard, 256), BF16),
        last_recv=V((pieces, pairs - 1, shard, 256), BF16),
        pool_fin=V((width, width), F32),
        items=V((2, slots, width), BF16),
        items_c=V((slots, width), BF16),
        item_all=V((2, 2, n_dp * slots, width // 2), BF16),
        vec=V((VEC_ROWS, width), F32),
        vec_c=V((VEC_ROWS // 2, width), F32),
        vec_s=V((VEC_ROWS // 2, width), F32),
        vec_y=V((VEC_ROWS // 2, width), F32),
        vec_t=V((VEC_ROWS // 2, width), F32),
        vec_r=V((VEC_ROWS // 2, width), F32),
        vec_q=V((pairs, VEC_ROWS // 2, width), F32),
        cnt=V((8, 128), F32),
        cnt_y=V((8, 128), F32),
        cnt_s=V((8, 128), F32),
        cnt_r=V((8, 128), F32),
        cnt_q=V((pairs, 8, 128), F32),
    )
    found = pl.pallas_call(
        partial(layer_kernel, n_dp),
        out_shape=[
            V((token_count, width), BF16),
            V((token_count, width), BF16),
            V((shard, width), F32),
            V((shard, width), F32),
            V((shard, width), F32),
            V((shard, width), F32),
            V((VEC_ROWS, width), F32),
        ],
        in_specs=[anywhere] * 17,
        out_specs=[vmem] * 7,
        scratch_shapes=list(scratch.values())
        + [
            pltpu.SemaphoreType.DMA((20,)),
            pltpu.SemaphoreType.DMA((copies,)),
            pltpu.SemaphoreType.DMA((copies,)),
        ],
        compiler_params=pltpu.CompilerParams(
            collective_id=0, has_side_effects=True, vmem_limit_bytes=VMEM_LIMIT
        ),
        name="layer",
    )(
        tokens,
        cotangent,
        lengths,
        labels,
        jnp.transpose(w_qkv, (1, 2, 0)).reshape(3 * local_width, width),
        qv_bias,
        w_out,
        branch_bias,
        norm_gain,
        norm_shift,
        w_up,
        up_bias,
        w_down,
        w_pool,
        pool_bias,
        w_class.T,
        class_bias.reshape(1, classes),
    )
    small = local_width // n_dp
    outputs = [
        shape((token_count, width), BF16),
        shape((token_count, width), BF16),
        shape((1, 1), F32),
        shape((1, 1), F32),
        shape((3, shard, local_width), F32),
        shape((2, small), F32),
        shape((local_width, shard), F32),
        shape((2, shard), F32),
        shape((2, shard), F32),
        shape((2, shard), F32),
        shape((shard, hidden), F32),
        shape((1, hidden // n_dp), F32),
        shape((shard, hidden), F32),
        shape((shard, width), F32),
        shape((1, shard), F32),
        shape((classes, shard), F32),
        shape((1, classes), F32),
    ]
    held = [out for i, out in enumerate(outputs) if i not in (0, 1, 10, 12, 13)]
    placed = pl.pallas_call(
        partial(place_kernel, n_dp),
        out_shape=outputs,
        in_specs=[vmem] * 7,
        out_specs=[anywhere] * 17,
        scratch_shapes=[V(out.shape, out.dtype) for out in held] + [pltpu.SemaphoreType.DMA((17,))],
        name="place",
    )(*[pltpu.with_memory_space_constraint(value, pltpu.VMEM) for value in found])
    (
        block_out,
        grad_tokens,
        loss,
        entropy,
        grad_qkv,
        grad_qv,
        grad_out,
        grad_branch,
        grad_gain,
        grad_shift,
        grad_up,
        grad_upb,
        grad_down,
        grad_pool,
        grad_poolb,
        grad_class,
        grad_classb,
    ) = placed
    return (
        block_out,
        grad_tokens,
        loss.reshape(()),
        entropy.reshape(()),
        jnp.transpose(grad_qkv, (1, 0, 2)),
        grad_qv,
        grad_out,
        grad_branch,
        grad_gain,
        grad_shift,
        grad_up,
        grad_upb.reshape(-1),
        grad_down.T,
        grad_pool,
        grad_poolb.reshape(-1),
        grad_class.T,
        grad_classb.reshape(-1),
    )


def solution(mesh):
    in_specs = (
        P("dp", None),
        P("dp", None),
        P("dp", None),
        P("dp", None),
        P(None, None, "tensor"),
        P(None, "tensor"),
        P("tensor", None),
        P(),
        P(),
        P(),
        P(None, "tensor"),
        P("tensor"),
        P("tensor", None),
        P(),
        P(),
        P(),
        P(),
    )
    out_specs = (
        P("dp", None),
        P("dp", None),
        P(),
        P(),
        P("dp", None, "tensor"),
        P(None, ("tensor", "dp")),
        P("tensor", "dp"),
        P(None, "dp"),
        P(None, "dp"),
        P(None, "dp"),
        P("dp", "tensor"),
        P(("tensor", "dp")),
        P("tensor", "dp"),
        P("dp", None),
        P("dp"),
        P("dp", None),
        P(),
    )
    return jax.shard_map(
        partial(on_device, mesh.shape["dp"]),
        mesh=mesh,
        in_specs=in_specs,
        out_specs=out_specs,
        check_vma=False,
    )
```

```python
from functools import partial

import jax
import jax.numpy as jnp
from jax import lax
from jax.experimental import pallas as pl
from jax.experimental.pallas import tpu as pltpu
from jax.sharding import PartitionSpec as P

HD = 64
MESH = pl.DeviceIdType.MESH
F32 = jnp.float32
BF16 = jnp.bfloat16
masked_score = -1e30
norm_eps = 1e-12
SQRT_HALF = 0.7071067811865476
PDF_SCALE = 0.3989422804014327
VEC_ROWS = 16
ORDERS = "yyryyrryy"
PLAN = (
    "fd0", "FD0_11", "FD0_10", "fd1", "fd2", "FD2_11", "FD2_10", "FD1_11", "fu0", "fu1",
    "FD2_01", "fu2", "ln1b0", "I_y", "FD1_10", "FD2_00", "FD1_01", "FU2_11", "SD0_1", "FD1_00",
    "SD2_1", "SD0_0", "SD2_0", "ln1b1", "SD1_1", "dctx", "ab0", "ab1", "FU1_11", "SD1_0",
    "ab2", "ab3", "I_r", "FU1_10", "ab4", "SU2_1", "ab5", "FU2_10", "dattT", "LD2",
    "FU1_01", "dsum", "FU2_01", "dtok0", "LD1", "FU1_00", "dtok1", "SU1_1", "FU0_11", "fq",
    "SU1_0", "FQ1_11", "qv", "SU2_0", "I_q", "ED2", "FQ1_10", "LU2", "FQ1_01", "V_y",
    "SU0_1", "FQ1_00", "LU1", "SQ1_1", "FU0_10", "ED1", "FU0_01", "gtok0", "FQ0_11", "SQ1_0",
    "FU0_00", "I_x", "FD0_01", "FQ0_10", "FD0_00", "FQ0_01", "V_r", "SU0_0", "FQ2_11", "LQ1",
    "gtok1", "LU0", "FQ2_10", "SQ0_1", "EU1", "LD0", "FQ2_01", "SQ0_0", "SQ2_1", "EQ1",
    "FQ2_00", "SQ2_0", "V_q", "LQ0", "I_c", "FQ0_00", "EU0", "FU2_00", "LQ2", "ED0",
    "V_e", "EQ0", "pool", "EU2", "EQ2",
)
VMEM_LIMIT = 56 * 1024 * 1024


def dot_nn(a, b):
    return lax.dot_general(a, b, (((1,), (0,)), ((), ())), preferred_element_type=F32)


def dot_nt(a, b):
    return lax.dot_general(a, b, (((1,), (1,)), ((), ())), preferred_element_type=F32)


def dot_tn(a, b):
    return lax.dot_general(a, b, (((0,), (0,)), ((), ())), preferred_element_type=F32)


def row_mean(v):
    return jnp.sum(v, axis=1, keepdims=True) * (1.0 / v.shape[1])


def col_sum(v):
    return jnp.sum(v, axis=0, keepdims=True)


def norm_forward(values):
    centered = values - row_mean(values)
    inv_scale = lax.rsqrt(row_mean(centered * centered) + norm_eps)
    return centered * inv_scale, inv_scale


def norm_backward(gradient, normed, inv_scale, gain_row):
    scaled = gradient * gain_row
    inner = scaled - row_mean(scaled) - normed * row_mean(scaled * normed)
    return inner * inv_scale


def gelu_parts(pre_act):
    cdf = 0.5 * (1.0 + lax.erf(pre_act * SQRT_HALF))
    pdf = PDF_SCALE * jnp.exp(-0.5 * pre_act * pre_act)
    return pre_act * cdf, cdf + pre_act * pdf


class Stop(Exception):
    pass


STOP = None


def mark(name):
    if STOP is not None and name == STOP:
        raise Stop()


class Tracked:
    def __init__(self, copy):
        self.copy, self.received = copy, False

    def wait_recv(self):
        if not self.received:
            self.received = True
            self.copy.wait_recv()

    def wait_send(self):
        self.copy.wait_send()


class Copies:
    def __init__(self, send_sems, recv_sems):
        self.send_sems, self.recv_sems, self.used, self.open = send_sems, recv_sems, 0, []

    def start(self, src, dst, device):
        copy = pltpu.make_async_remote_copy(
            src_ref=src,
            dst_ref=dst,
            send_sem=self.send_sems.at[self.used],
            recv_sem=self.recv_sems.at[self.used],
            device_id=device,
            device_id_type=MESH,
        )
        self.used += 1
        copy.start()
        copy = Tracked(copy)
        self.open.append(copy)
        return copy

    def finish(self):
        for copy in self.open:
            copy.wait_send()


class Loads:
    def __init__(self, sems):
        self.sems, self.used = sems, 0

    def start(self, src, dst):
        copy = pltpu.make_async_copy(src, dst, self.sems.at[self.used])
        self.used += 1
        copy.start()
        return copy


def remote_copy_count(pairs):
    return 72 + 9 * 4 * pairs + 8 * pairs


def layer_kernel(
    n_dp,
    tok_hbm,
    cot_hbm,
    len_hbm,
    lab_hbm,
    wqkv_hbm,
    qvb_hbm,
    wout_hbm,
    bb_hbm,
    ng_hbm,
    ns_hbm,
    wup_hbm,
    upb_hbm,
    wdn_hbm,
    wpool_hbm,
    pb_hbm,
    wcls_hbm,
    cb_hbm,
    bout_out,
    gtok_out,
    gqkvo_out,
    gup_out,
    gdn_out,
    gpool_out,
    vec_out,
    len_ref,
    lab_ref,
    cb_ref,
    qvb_ref,
    bb_ref,
    ng_ref,
    ns_ref,
    upb_ref,
    pb_ref,
    wcls_ref,
    tok,
    cot,
    wt,
    wo,
    wup,
    wdn,
    wpool,
    wup_tr,
    wdn_tr,
    wpool_tr,
    up_bias,
    bias_mask,
    k_pad,
    v_pad,
    k_tr,
    v_tr,
    q_pad,
    q_away,
    probs,
    ctx,
    hid,
    hid_low,
    hid_tr,
    tok_tr,
    n_one,
    scale_one,
    act_low,
    d_gelu,
    acc,
    parts,
    d_sec,
    d_br,
    d_br_tr,
    d_br_peer,
    d_pre_low,
    d_pre_peer,
    act_peer,
    hid_peer,
    ctx_peer,
    d_att_peer,
    d_qkv_peer,
    d_first,
    d_att,
    d_att_tr,
    d_ctx,
    d_kv_f32,
    d_kv_send,
    d_kv_recv,
    d_qkv,
    g_low,
    first_recv,
    second_send,
    second_recv,
    last_send,
    last_recv,
    pool_fin,
    items,
    items_c,
    item_all,
    vec,
    vec_c,
    vec_s,
    vec_y,
    vec_t,
    vec_r,
    vec_q,
    cnt,
    cnt_y,
    cnt_s,
    cnt_r,
    cnt_q,
    load_sems,
    send_sems,
    recv_sems,
):
    pairs = n_dp // 4
    dp = lax.axis_index("dp")
    me = lax.axis_index("tensor")
    x = me // 2
    c = lax.rem(me, 2)
    y = lax.rem(dp, 2)
    r = lax.rem(dp // 2, 2)
    q = dp // 4
    core_dev = (dp, me + 1 - 2 * c)
    x_dev = (dp, 2 * (1 - x) + c)
    y_dev = (dp + 1 - 2 * y, me)
    r_dev = (dp + 2 - 4 * r, me)

    def q_of(k):
        return lax.rem(q + k, pairs)

    def q_dev(k):
        return (q_of(k) * 4 + r * 2 + y, me)

    away = range(1, pairs)
    token_count, width = tok.shape
    half = token_count // 2
    local_width = wo.shape[1]
    heads = local_width // HD
    slots = len_ref.shape[1]
    shard = width // n_dp
    chunk = 128
    chunks = half // chunk
    fine = 128
    fines = half // fine
    tile = 256
    tiles = width // tile
    own_rows = pl.ds(pl.multiple_of(c * half, half), half)
    away_rows = pl.ds(pl.multiple_of((1 - c) * half, half), half)

    barrier = pltpu.get_barrier_semaphore()
    peers = [core_dev, x_dev, y_dev, r_dev] + [q_dev(k) for k in away]
    for peer in peers:
        pl.semaphore_signal(barrier, inc=1, device_id=peer, device_id_type=MESH)

    loads = Loads(load_sems)
    remote = Copies(send_sems, recv_sems)
    load_len = loads.start(len_hbm, len_ref)
    load_tok = loads.start(tok_hbm, tok)
    load_wt = loads.start(wqkv_hbm, wt.at[c])
    load_qvb = loads.start(qvb_hbm, qvb_ref)
    load_upb = loads.start(upb_hbm, upb_ref)
    load_lab = loads.start(lab_hbm, lab_ref)
    load_small = [
        loads.start(src, dst)
        for src, dst in (
            (cb_hbm, cb_ref),
            (bb_hbm, bb_ref),
            (ng_hbm, ng_ref),
            (ns_hbm, ns_ref),
            (pb_hbm, pb_ref),
            (wcls_hbm, wcls_ref),
        )
    ]
    load_wo = loads.start(wout_hbm, wo.at[c])
    load_wup = loads.start(wup_hbm, wup.at[c])
    load_wdn = loads.start(wdn_hbm, wdn.at[c])
    load_pool = loads.start(wpool_hbm, wpool)
    load_cot = loads.start(cot_hbm.at[own_rows], cot)

    load_len.wait()
    load_lab.wait()
    lengths = [len_ref[0, i] for i in range(slots)]
    ends, total = [], 0
    for i in range(slots):
        total = total + lengths[i]
        ends.append(total)
    firsts = [jnp.minimum(ends[i] - lengths[i], token_count - 1) for i in range(slots)]
    key_place = lax.broadcasted_iota(jnp.int32, (token_count, 128), 0)
    query_place = lax.broadcasted_iota(jnp.int32, (8, half), 1) + c * half
    key_segment = jnp.zeros((token_count, 128), jnp.int32)
    query_segment = jnp.zeros((8, half), jnp.int32)
    for i in range(slots):
        key_segment = key_segment + (key_place >= ends[i]).astype(jnp.int32)
        query_segment = query_segment + (query_place >= ends[i]).astype(jnp.int32)
    for n in range(half // 128):
        cols = slice(n * 128, (n + 1) * 128)
        bias_mask[:, cols] = jnp.where(key_segment == query_segment[0:1, cols], 0.0, masked_score)
    item_row = lax.broadcasted_iota(jnp.int32, (slots, 128), 0)
    first_col = jnp.zeros((slots, 128), jnp.int32)
    len_col = jnp.zeros((slots, 128), jnp.int32)
    lab_col = jnp.zeros((slots, 128), jnp.int32)
    for i in range(slots):
        first_col = first_col + jnp.where(item_row == i, firsts[i], 0)
        len_col = len_col + jnp.where(item_row == i, lengths[i], 0)
        lab_col = lab_col + jnp.where(item_row == i, lab_ref[0, i], 0)
    live_all = jnp.where(len_col > 0, 1.0, 0.0)
    cnt[...] = jnp.broadcast_to(col_sum(live_all), cnt.shape)
    lane_item = lax.broadcasted_iota(jnp.int32, (1, 2 * slots), 1)
    first_row = jnp.zeros((1, 2 * slots), jnp.int32)
    for i in range(slots):
        first_row = first_row + jnp.where((lane_item == i) | (lane_item == i + slots), firsts[i], 0)

    load_upb.wait()
    up_bias[c] = jnp.broadcast_to(upb_ref[...].astype(F32).reshape(1, width), (8, width))
    vec[...] = jnp.zeros_like(vec)
    pad_rows = q_pad.shape[1] - local_width
    for b in range(2):
        q_pad[b, local_width:, :] = jnp.zeros((pad_rows, half), BF16)
        d_ctx[b, local_width:, :] = jnp.zeros((pad_rows, half), BF16)
        v_pad[b, :, local_width:] = jnp.zeros((token_count, pad_rows), BF16)

    def bias_cols(part, columns):
        row = qvb_ref[part : part + 1, :]
        block = jnp.transpose(jnp.broadcast_to(row, (128, local_width)))
        return jnp.concatenate([block] * (columns // 128), axis=1)

    load_tok.wait()
    load_wt.wait()
    load_qvb.wait()
    rows_q, rows_k, rows_v = [slice(p * local_width, (p + 1) * local_width) for p in range(3)]
    query_bias = bias_cols(0, half)
    q_away[...] = (dot_nt(wt[c, rows_q, :], tok[away_rows, :]) + query_bias).astype(BF16)
    wide_k = jnp.concatenate([wt[c, rows_k, :], jnp.zeros((pad_rows, width), BF16)], axis=0)
    k_pad[c] = dot_nt(tok[...], wide_k).astype(BF16)
    pl.semaphore_wait(barrier, len(peers))
    mark("sends")
    send_q = remote.start(q_away, q_pad.at[c, pl.ds(0, local_width)], core_dev)
    send_k = remote.start(k_pad.at[c], k_pad.at[c], core_dev)
    v_tr[c] = (dot_nt(wt[c, rows_v, :], tok[...]) + bias_cols(1, token_count)).astype(BF16)
    send_v = remote.start(v_tr.at[c], v_tr.at[c], core_dev)
    send_wo = remote.start(wout_hbm, wo.at[c], core_dev)
    send_bias = remote.start(up_bias.at[c], up_bias.at[c], core_dev)
    send_wup = remote.start(wup_hbm, wup.at[c], core_dev)
    send_wdn = remote.start(wdn_hbm, wdn.at[c], core_dev)
    send_cnt_y = remote.start(cnt, cnt_y, y_dev)
    send_wt = remote.start(wqkv_hbm, wt.at[c], core_dev)

    q_pad[c, 0:local_width, :] = (dot_nt(wt[c, rows_q, :], tok[own_rows, :]) + query_bias).astype(BF16)

    half_row = lax.broadcasted_iota(jnp.int32, (128, half), 0) < HD
    inv_root = HD ** (-0.5)

    def half_of(block, i):
        if i == heads - 1 and i % 2 == 0:
            return block
        zero = jnp.zeros_like(block)
        return jnp.where(half_row, block, zero) if i % 2 == 0 else jnp.where(half_row, zero, block)

    def pair_of(i):
        return slice((i // 2) * 128, (i // 2 + 1) * 128)

    def attend(core):
        for i in range(heads):
            head_rows = slice(i * HD, (i + 1) * HD)
            scores = dot_nn(k_pad[core, :, pair_of(i)], half_of(q_pad[core, pair_of(i), :], i))
            scores = scores * inv_root + bias_mask[...]
            terms = jnp.exp(scores - jnp.max(scores, axis=0, keepdims=True))
            weights = terms * (1.0 / col_sum(terms))
            probs[core, i] = weights
            ctx[core, head_rows, :] = dot_nn(v_tr[core, head_rows, :], weights.astype(BF16)).astype(BF16)

    mark("attn_own")
    attend(c)
    send_q.wait_recv()
    send_k.wait_recv()
    send_v.wait_recv()
    mark("attn_other")
    attend(1 - c)
    mark("out")
    for load in load_small:
        load.wait()
    send_ctx = remote.start(ctx.at[1 - c], ctx_peer, core_dev)
    load_wo.wait()
    send_wo.wait_recv()

    def chunk_of(i):
        return slice(i * chunk, (i + 1) * chunk)

    def exchange(which, rows):
        block = parts.at[which, x, rows]
        return remote.start(block, block, x_dev)

    def fine_of(i):
        return slice(i * fine, (i + 1) * fine)

    def both_parts(which, rows):
        return parts[which, 0, rows, :].astype(F32) + parts[which, 1, rows, :].astype(F32)

    ATT, FFN, HIDDEN, TOKEN = 0, 1, 2, 3
    send_att = []
    for i in range(chunks):
        rows = chunk_of(i)
        partial_sum = dot_tn(ctx[0, :, rows], wo[0]) + dot_tn(ctx[1, :, rows], wo[1])
        parts[ATT, x, rows, :] = partial_sum.astype(BF16)
        for j in range(i * chunk // fine, (i + 1) * chunk // fine):
            send_att.append(exchange(ATT, fine_of(j)))
    send_cnt_y.wait_recv()
    cnt_s[...] = cnt[...] + cnt_y[...]
    send_cnt_r = remote.start(cnt_s, cnt_r, r_dev)

    mark("transposes")
    for b in range(2):
        k_tr[b] = jnp.transpose(k_pad[b])[0:local_width, :]
        v_pad[b, :, 0:local_width] = jnp.transpose(v_tr[b])
    tok_tr[0] = jnp.transpose(tok[own_rows, :])
    tok_tr[1] = jnp.transpose(tok[away_rows, :])

    load_wup.wait()
    load_wdn.wait()
    load_pool.wait()
    wpool_tr[...] = jnp.transpose(wpool[...])
    send_wup.wait_recv()
    send_wdn.wait_recv()
    for b in range(2):
        wup_tr[b] = jnp.transpose(wup[b])
        wdn_tr[b] = jnp.transpose(wdn[b])

    mark("ffn_f")
    send_ffn, send_hid, send_act = [], [], []
    for i in range(fines):
        rows = fine_of(i)
        send_att[i].wait_recv()
        token_rows = pl.ds(pl.multiple_of(c * half + i * fine, fine), fine)
        attention = both_parts(ATT, rows) + bb_ref[0:1, :]
        normed, inv_scale = norm_forward(tok[token_rows, :].astype(F32) + attention)
        n_one[rows, :] = normed
        scale_one[rows, :] = inv_scale
        value = normed * ng_ref[0:1, :] + ns_ref[0:1, :]
        hid[rows, :] = value
        hid_low[rows, :] = value.astype(BF16)
        send_hid.append(remote.start(hid_low.at[rows], hid_peer.at[rows], core_dev))
        for b in range(2):
            core = c if b == 0 else 1 - c
            if i == 0 and b == 1:
                send_bias.wait_recv()
                send_wup.wait_recv()
            for n in range(tiles):
                cols = slice(n * tile, (n + 1) * tile)
                pre_act = dot_nn(hid_low[rows, :], wup[core, :, cols]) + up_bias[core, 0:1, cols]
                value, slope = gelu_parts(pre_act)
                act_low[b, rows, cols] = value.astype(BF16)
                d_gelu[b, rows, cols] = slope
            if i == 0 and b == 1:
                send_wdn.wait_recv()
            product = dot_nn(act_low[b, rows, :], wdn[core])
            if b == 0:
                acc[0:fine, :] = product
            else:
                parts[FFN, x, rows, :] = (acc[0:fine, :] + product).astype(BF16)
        send_ffn.append(exchange(FFN, rows))
        send_act.append(remote.start(act_low.at[1, rows], act_peer.at[rows], core_dev))
        if i == 0:
            send_cnt_r.wait_recv()
            cnt_q[q] = cnt_s[...] + cnt_r[...]
            send_cnt_q = [remote.start(cnt_q.at[q], cnt_q.at[q], q_dev(k)) for k in away]

    mark("hid_tr")
    hid_tr[0] = jnp.transpose(hid_low[...])
    for copy in send_hid:
        copy.wait_recv()
    hid_tr[1] = jnp.transpose(hid_peer[...])
    load_cot.wait()
    for copy in send_cnt_q:
        copy.wait_recv()
    item_count = cnt_q[0]
    for k in away:
        item_count = item_count + cnt_q[k]
    inv_count = 1.0 / item_count[0:1, 0:1]

    classes = wcls_ref.shape[0]
    class_rows = wcls_ref[...].astype(F32)
    class_pad = jnp.concatenate([class_rows, jnp.zeros((16 - classes, width), F32)], axis=0).astype(BF16)
    class_lane = lax.broadcasted_iota(jnp.int32, (slots, 16), 1)
    class_bias = jnp.zeros((slots, 16), F32)
    for k in range(classes):
        class_bias = class_bias + jnp.where(class_lane == k, cb_ref[0, k], 0.0)
    label_hot = jnp.where(class_lane == lab_col[:, 0:1], 1.0, 0.0)
    lane = lax.broadcasted_iota(jnp.int32, (1, 128), 1)

    def add_rows(first, value):
        vec[first : first + value.shape[0], 0 : value.shape[1]] += value

    mark("ln2")
    up_sums = [[None] * tiles, [None] * tiles]
    send_hidden, send_br, send_pre = [], [], []
    for i in range(chunks):
        rows = chunk_of(i)
        place = c * half + i * chunk
        for j in range(i * chunk // fine, (i + 1) * chunk // fine):
            send_ffn[j].wait_recv()
        normed, inv_scale = norm_forward(hid[rows, :] + (both_parts(FFN, rows) + bb_ref[1:2, :]))
        low = (normed * ng_ref[1:2, :] + ns_ref[1:2, :]).astype(BF16)
        bout_out[pl.ds(pl.multiple_of(place, chunk), chunk), :] = low

        local_first = first_col[:, 0:1] - place
        pick = (lax.broadcasted_iota(jnp.int32, (slots, chunk), 1) == local_first).astype(F32).astype(BF16)
        picked = dot_nn(pick, low).astype(BF16)
        pooled = jnp.tanh(dot_nn(picked, wpool[...]) + pb_ref[...].reshape(1, width))
        pooled_low = pooled.astype(BF16)
        logits = jnp.where(class_lane < classes, dot_nt(pooled_low, class_pad) + class_bias, masked_score)
        shifted = logits - jnp.max(logits, axis=1, keepdims=True)
        log_probs = shifted - jnp.log(jnp.sum(jnp.exp(shifted), axis=1, keepdims=True))
        class_probs = jnp.exp(log_probs)
        owned = jnp.where((local_first >= 0) & (local_first < chunk), live_all[:, 0:1], 0.0)
        item_ce = -jnp.sum(label_hot * log_probs, axis=1, keepdims=True) * owned
        item_ent = -jnp.sum(class_probs * log_probs, axis=1, keepdims=True) * owned
        d_logits = (class_probs - label_hot) * (owned * inv_count)
        d_pooled = jnp.zeros((slots, width), F32)
        for k in range(classes):
            d_pooled = d_pooled + d_logits[:, k : k + 1] * class_rows[k : k + 1, :]
            add_rows(7 + k, col_sum(d_logits[:, k : k + 1] * pooled_low.astype(F32)))
        d_pre = (d_pooled * (1.0 - pooled * pooled)).astype(BF16)
        add_rows(6, col_sum(d_pre.astype(F32)))
        add_rows(
            10, jnp.where(lane == 0, col_sum(item_ce), 0.0) + jnp.where(lane == 1, col_sum(item_ent), 0.0)
        )
        vec[10:11, 128:144] += col_sum(d_logits)
        if i == 0:
            items[0] = picked
            items[1] = d_pre
        else:
            items[0] += picked
            items[1] += d_pre
        if i == chunks - 1:
            send_items = remote.start(items.at[1 - c], items_c, core_dev)
        d_picked = dot_nn(d_pre, wpool_tr[...])
        d_high = d_picked.astype(BF16)
        d_both = jnp.concatenate([d_high, (d_picked - d_high.astype(F32)).astype(BF16)], axis=0)

        token_place = lax.broadcasted_iota(jnp.int32, (chunk, 2 * slots), 0) + place
        spread = dot_nn((token_place == first_row).astype(F32).astype(BF16), d_both)
        live = jnp.where(token_place[:, 0:1] < total, 1.0, 0.0)
        d_output = cot[rows, :].astype(F32) * live + spread
        add_rows(3, col_sum(d_output * normed))
        add_rows(5, col_sum(d_output))
        d_second = norm_backward(d_output, normed, inv_scale, ng_ref[1:2, :])
        add_rows(1, col_sum(d_second))
        d_sec[rows, :] = d_second
        d_br[rows, :] = d_second.astype(BF16)
        send_br.append(remote.start(d_br.at[rows], d_br_peer.at[rows], core_dev))
        for b in range(2):
            core = c if b == 0 else 1 - c
            for n in range(tiles):
                cols = slice(n * tile, (n + 1) * tile)
                d_act = dot_nn(d_br[rows, :], wdn_tr[core, :, cols])
                low = (d_act * d_gelu[b, rows, cols]).astype(BF16)
                d_pre_low[b, rows, cols] = low
                up_sum = col_sum(low.astype(F32))
                up_sums[b][n] = up_sum if i == 0 else up_sums[b][n] + up_sum
            product = dot_nn(d_pre_low[b, rows, :], wup_tr[core])
            if b == 0:
                acc[...] = product
            else:
                parts[HIDDEN, x, rows, :] = (acc[...] + product).astype(BF16)
        send_hidden.append(exchange(HIDDEN, rows))
        send_pre.append(remote.start(d_pre_low.at[1, rows], d_pre_peer.at[rows], core_dev))
    vec[pl.ds(11 + c, 1), :] = jnp.concatenate(up_sums[0], axis=1)
    vec[pl.ds(12 - c, 1), :] = jnp.concatenate(up_sums[1], axis=1)
    send_out = remote.start(bout_out.at[own_rows], bout_out.at[own_rows], core_dev)

    DOWN, UP, QKVO = 0, tiles, 2 * tiles
    y_first, r_first = (y, r, y_dev, r_dev), (r, y, r_dev, y_dev)
    along = [y_first if letter == "y" else r_first for letter in ORDERS]
    row_major = [letter == "r" for letter in ORDERS]
    reach = {1: list(away), 0: [0]}
    slot_of = {(flip, k): (1 - flip) * pairs + (k - 1) % pairs for flip in range(2) for k in range(pairs)}
    sent = {}
    step = {}

    def store_blocks(block, product):
        for j in range(n_dp):
            bits = (j % 2, (j // 2) % 2)
            if row_major[block]:
                bits = bits[::-1]
            g_low[block, bits[0], bits[1], j // 4] = product[j * shard : (j + 1) * shard, :].astype(BF16)

    def fill(block, product_of):
        for n in range(tiles):
            store_blocks(block + n, product_of(slice(n * tile, (n + 1) * tile)))

    def first_step(block, flip, group):
        first, second, device, _ = along[block]
        for k in reach[group]:
            source = g_low.at[block, 1 - first, 1 - second if flip else second, q_of(k)]
            sent[block, 1, flip, k] = remote.start(source, first_recv.at[block, slot_of[flip, k]], device)

    def first_sum(block, flip, k):
        first, second, _, _ = along[block]
        sent[block, 1, flip, k].wait_recv()
        value = g_low[block, first, 1 - second if flip else second, q_of(k)].astype(F32)
        return value + first_recv[block, slot_of[flip, k]].astype(F32)

    def second_step(block, group):
        for k in reach[group]:
            second_send[block, k] = first_sum(block, 1, k).astype(BF16)
            sent[block, 2, k] = remote.start(second_send.at[block, k], second_recv.at[block, k], along[block][3])

    def second_sum(block, k):
        sent[block, 2, k].wait_recv()
        return first_sum(block, 0, k) + second_recv[block, k].astype(F32)

    def last_step(block):
        for k in away:
            last_send[block, k - 1] = second_sum(block, k).astype(BF16)
            sent[block, 3, k] = remote.start(last_send.at[block, k - 1], last_recv.at[block, k - 1], q_dev(k))

    def end_step(block, out):
        result = second_sum(block, 0)
        for k in away:
            sent[block, 3, k].wait_recv()
            result = result + last_recv[block, k - 1].astype(F32)
        n = block % tiles
        out[:, n * tile : (n + 1) * tile] = result

    for letter, first_block, out in (("D", DOWN, gdn_out), ("U", UP, gup_out), ("Q", QKVO, gqkvo_out)):
        for n in range(tiles):
            block, name = first_block + n, letter + str(n)
            for group in range(2):
                for flip in range(2):
                    step["F%s_%d%d" % (name, flip, group)] = partial(first_step, block, flip, group)
                step["S%s_%d" % (name, group)] = partial(second_step, block, group)
            step["L" + name] = partial(last_step, block)
            step["E" + name] = partial(end_step, block, out)

    def fill_down(n):
        if n == 0:
            d_br_tr[0] = jnp.transpose(d_br[...])
            for copy in send_br + send_act:
                copy.wait_recv()
            d_br_tr[1] = jnp.transpose(d_br_peer[...])
        cols = slice(n * tile, (n + 1) * tile)
        store_blocks(DOWN + n, dot_nn(d_br_tr[0], act_low[0, :, cols]) + dot_nn(d_br_tr[1], act_peer[:, cols]))

    def fill_up(n):
        for copy in send_pre:
            copy.wait_recv()
        cols = slice(n * tile, (n + 1) * tile)
        store_blocks(UP + n, dot_nn(hid_tr[0], d_pre_low[0, :, cols]) + dot_nn(hid_tr[1], d_pre_peer[:, cols]))

    for n in range(tiles):
        step["fd%d" % n] = partial(fill_down, n)
        step["fu%d" % n] = partial(fill_up, n)

    def item_rows(first, count):
        return pl.ds(pl.multiple_of(first * slots, count * slots), count * slots)

    def pass_items(name, rows, devices):
        block = item_all.at[c, x, rows]
        sent[name] = [remote.start(block, block, device) for device in devices]

    def settle(name):
        for copy in sent[name]:
            copy.wait_recv()

    def items_y():
        send_items.wait_recv()
        both = items[c] + items_c[...]
        item_all[c, x, item_rows(dp, 1), :] = jnp.where(x == 0, both[:, : width // 2], both[:, width // 2 :])
        pass_items("items_y", item_rows(dp, 1), [y_dev])

    def items_r():
        settle("items_y")
        pass_items("items_r", item_rows(dp - y, 2), [r_dev])

    def items_q():
        settle("items_r")
        pass_items("items_q", item_rows(q * 4, 4), [q_dev(k) for k in away])

    def items_x():
        settle("items_q")
        sent["items_x"] = [remote.start(item_all.at[c, x], item_all.at[c, x], x_dev)]

    def items_core():
        settle("items_x")
        sent["items_core"] = [remote.start(item_all.at[c], item_all.at[c], core_dev)]

    def pool():
        settle("items_core")
        picked_all, d_pre_all = [jnp.concatenate([item_all[p, 0], item_all[p, 1]], axis=1) for p in range(2)]
        pool_fin[...] = dot_tn(picked_all, d_pre_all)
        gpool_out[...] = pool_fin[pl.ds(pl.multiple_of(dp * shard, 8), shard), :]

    step.update(I_y=items_y, I_r=items_r, I_q=items_q, I_x=items_x, I_c=items_core, pool=pool)

    def norm_one_back(i):
        rows = chunk_of(i)
        send_hidden[i].wait_recv()
        d_hidden = both_parts(HIDDEN, rows) + d_sec[rows, :]
        normed = n_one[rows, :]
        add_rows(2, col_sum(d_hidden * normed))
        add_rows(4, col_sum(d_hidden))
        gradient = norm_backward(d_hidden, normed, scale_one[rows, :], ng_ref[0:1, :])
        add_rows(0, col_sum(gradient))
        d_first[rows, :] = gradient
        d_att[rows, :] = gradient.astype(BF16)
        sent["d_att", i] = remote.start(d_att.at[rows], d_att_peer.at[rows], core_dev)

    def context_back():
        for b in range(2):
            d_ctx[b, 0:local_width, :] = dot_nt(wo[b], d_att[...]).astype(BF16)

    def head_back(n):
        b, i = n // heads, n % heads
        head_rows = slice(i * HD, (i + 1) * HD)
        d_probs = dot_nn(v_pad[b, :, pair_of(i)], half_of(d_ctx[b, pair_of(i), :], i))
        weights = probs[b, i]
        delta = col_sum(weights * d_probs)
        d_scores = (weights * (d_probs - delta)).astype(BF16)
        d_value = dot_nt(d_ctx[b, head_rows, :], weights.astype(BF16))
        d_key = dot_nt(q_pad[b, head_rows, :], d_scores) * inv_root
        d_query = dot_nn(k_tr[b, head_rows, :], d_scores) * inv_root
        d_qkv[b, head_rows, :] = d_query.astype(BF16)
        for part, value in ((0, d_key), (1, d_value)):
            part_rows = slice(part * local_width + i * HD, part * local_width + (i + 1) * HD)
            for side in range(2):
                lanes = slice(side * half, (side + 1) * half)
                d_kv_f32[side, b, part_rows, :] = value[:, lanes]
                d_kv_send[side, b, part_rows, :] = value[:, lanes].astype(BF16)
        if n == 2 * heads - 1:
            sent["kv"] = remote.start(d_kv_send.at[1 - c], d_kv_recv, core_dev)

    def turn_attention():
        d_att_tr[0] = jnp.transpose(d_att[...])
        for i in range(chunks):
            sent["d_att", i].wait_recv()
        d_att_tr[1] = jnp.transpose(d_att_peer[...])

    def join_cores():
        sent["kv"].wait_recv()
        for b in range(2):
            d_qkv[b, local_width:, :] = (d_kv_f32[c, b] + d_kv_recv[b].astype(F32)).astype(BF16)
        sent["d_qkv"] = remote.start(d_qkv.at[1 - c], d_qkv_peer, core_dev)

    for i in range(chunks):
        step["ln1b%d" % i] = partial(norm_one_back, i)
    step["dctx"] = context_back
    for n in range(2 * heads):
        step["ab%d" % n] = partial(head_back, n)
    step["dattT"] = turn_attention
    step["dsum"] = join_cores

    def fill_qkvo():
        sent["d_qkv"].wait_recv()
        send_ctx.wait_recv()
        first_part = dot_nt(tok_tr[0], d_qkv[c]) + dot_nt(tok_tr[1], d_qkv_peer[...])
        second_part = dot_nt(d_att_tr[0], ctx[c]) + dot_nt(d_att_tr[1], ctx_peer[...])
        both = jnp.concatenate([first_part, second_part], axis=1)
        fill(QKVO, lambda cols: both[:, cols])

    def token_part(i):
        send_wt.wait_recv()
        rows = chunk_of(i)
        partial_sum = dot_tn(d_qkv[0, :, rows], wt[0]) + dot_tn(d_qkv[1, :, rows], wt[1])
        parts[TOKEN, x, rows, :] = partial_sum.astype(BF16)
        sent["token", i] = exchange(TOKEN, rows)

    def token_end(i):
        sent["token", i].wait_recv()
        rows = chunk_of(i)
        place = pl.ds(pl.multiple_of(c * half + i * chunk, chunk), chunk)
        gtok_out[place, :] = (both_parts(TOKEN, rows) + d_first[rows, :]).astype(BF16)
        if i == chunks - 1:
            sent["gtok"] = remote.start(gtok_out.at[own_rows], gtok_out.at[own_rows], core_dev)

    step["fq"] = fill_qkvo
    for i in range(chunks):
        step["dtok%d" % i] = partial(token_part, i)
        step["gtok%d" % i] = partial(token_end, i)

    def vec_rows(core):
        return pl.ds(pl.multiple_of(core * VEC_ROWS // 2, VEC_ROWS // 2), VEC_ROWS // 2)

    def vec_core():
        ones = jnp.ones((8, half), BF16)
        sums = [dot_nt(ones, d_qkv[b])[0:1, :] for b in range(2)]
        columns = [v[:, :local_width] for v in sums] + [v[:, 2 * local_width :] for v in sums]
        vec[13:14, :] = jnp.concatenate(columns, axis=1)
        vec[14:15, 0:128] = item_count[0:1, :]
        sent["vec"] = remote.start(vec.at[vec_rows(1 - c)], vec_c, core_dev)

    def vec_along_y():
        sent["vec"].wait_recv()
        vec_s[...] = vec[vec_rows(c), :] + vec_c[...]
        sent["vec_y"] = remote.start(vec_s, vec_y, y_dev)

    def vec_along_r():
        sent["vec_y"].wait_recv()
        vec_t[...] = vec_s[...] + vec_y[...]
        sent["vec_r"] = remote.start(vec_t, vec_r, r_dev)

    def vec_along_q():
        sent["vec_r"].wait_recv()
        vec_q[q] = vec_t[...] + vec_r[...]
        sent["vec_q"] = [remote.start(vec_q.at[q], vec_q.at[q], q_dev(k)) for k in away]

    def vec_end():
        settle("vec_q")
        vec_total = vec_q[0]
        for k in away:
            vec_total = vec_total + vec_q[k]
        vec_out[vec_rows(c), :] = vec_total
        sent["vec_out"] = remote.start(vec_out.at[vec_rows(c)], vec_out.at[vec_rows(c)], core_dev)

    step.update(qv=vec_core, V_y=vec_along_y, V_r=vec_along_r, V_q=vec_along_q, V_e=vec_end)

    assert sorted(PLAN) == sorted(step)
    for name in PLAN:
        mark(name)
        step[name]()
    mark("finish")
    send_out.wait_recv()
    sent["gtok"].wait_recv()
    sent["vec_out"].wait_recv()
    remote.finish()


def place_kernel(
    n_dp,
    bout_in,
    gtok_in,
    gqkvo_in,
    gup_in,
    gdn_in,
    gpool_in,
    vec_in,
    bout_out,
    gtok_out,
    loss_out,
    entropy_out,
    gqkv_out,
    gqv_out,
    gout_out,
    gbranch_out,
    ggain_out,
    gshift_out,
    gup_out,
    gupb_out,
    gdn_out,
    gpool_out,
    gpoolb_out,
    gclass_out,
    gclassb_out,
    loss,
    entropy,
    gqkv,
    gqv,
    gout,
    gbranch,
    ggain,
    gshift,
    gupb,
    gpoolb,
    gclass,
    gclassb,
    sems,
):
    moves = ((bout_in, bout_out), (gtok_in, gtok_out), (gup_in, gup_out), (gdn_in, gdn_out), (gpool_in, gpool_out))
    copies = []

    def send(src, dst):
        copy = pltpu.make_async_copy(src, dst, sems.at[len(copies)])
        copy.start()
        copies.append(copy)

    for src, dst in moves:
        send(src, dst)
    dp = lax.axis_index("dp")
    c = lax.rem(lax.axis_index("tensor"), 2)
    width = vec_in.shape[1]
    shard = width // n_dp
    local_width = gout.shape[0]
    for part in range(3):
        gqkv[part] = gqkvo_in[:, part * local_width : (part + 1) * local_width]
    send(gqkv, gqkv_out)
    gout[...] = jnp.transpose(gqkvo_in[:, 3 * local_width :])
    send(gout, gout_out)
    sums = vec_in[...]
    mine = pltpu.roll(sums, lax.rem(width - dp * shard, width), axis=1)
    gbranch[...] = mine[0:2, :shard]
    ggain[...] = mine[2:4, :shard]
    gshift[...] = mine[4:6, :shard]
    gpoolb[...] = mine[6:7, :shard]
    gclass[...] = mine[7 : 7 + gclass.shape[0], :shard]
    gupb[...] = jnp.where(c == 0, mine[11:12, :shard], mine[12:13, :shard])
    small = local_width // n_dp
    quarter = pltpu.roll(sums, lax.rem(width - (c * local_width + dp * small), width), axis=1)
    gqv[0:1, :] = quarter[13:14, :small]
    gqv[1:2, :] = quarter[13:14, 2 * local_width : 2 * local_width + small]
    inv_count = 2.0 * n_dp / sums[14:15, 0:1]
    loss[...] = sums[10:11, 0:1] * inv_count
    entropy[...] = sums[10:11, 1:2] * inv_count
    gclassb[...] = sums[10:11, 128 : 128 + gclassb.shape[1]]
    small_moves = (
        (loss, loss_out),
        (entropy, entropy_out),
        (gqv, gqv_out),
        (gbranch, gbranch_out),
        (ggain, ggain_out),
        (gshift, gshift_out),
        (gupb, gupb_out),
        (gpoolb, gpoolb_out),
        (gclass, gclass_out),
        (gclassb, gclassb_out),
    )
    for src, dst in small_moves:
        send(src, dst)
    for copy in copies:
        copy.wait()


def on_device(
    n_dp,
    tokens,
    cotangent,
    lengths,
    labels,
    w_qkv,
    qv_bias,
    w_out,
    branch_bias,
    norm_gain,
    norm_shift,
    w_up,
    up_bias,
    w_down,
    w_pool,
    pool_bias,
    w_class,
    class_bias,
):
    token_count, width = tokens.shape
    local_width = w_out.shape[0]
    hidden = w_up.shape[1]
    classes = w_class.shape[1]
    slots = lengths.shape[1]
    pairs = n_dp // 4
    shard = width // n_dp
    half = token_count // 2
    heads = local_width // HD
    padded = (local_width + 127) // 128 * 128
    assert hidden == width and 4 * local_width == width and lengths.shape[0] == 1
    shape = jax.ShapeDtypeStruct
    anywhere = pl.BlockSpec(memory_space=pl.ANY)
    vmem = pl.BlockSpec(memory_space=pltpu.VMEM)
    pieces = 3 * width // 256
    blocks = (pieces, 2, 2, pairs, shard, 256)
    copies = remote_copy_count(pairs)
    V = pltpu.VMEM
    S = pltpu.SMEM
    scratch = dict(
        len_ref=S(lengths.shape, jnp.int32),
        lab_ref=S(labels.shape, jnp.int32),
        cb_ref=S((1, classes), F32),
        qvb_ref=V(qv_bias.shape, F32),
        bb_ref=V(branch_bias.shape, F32),
        ng_ref=V(norm_gain.shape, F32),
        ns_ref=V(norm_shift.shape, F32),
        upb_ref=V(up_bias.shape, BF16),
        pb_ref=V(pool_bias.shape, F32),
        wcls_ref=V((classes, width), BF16),
        tok=V((token_count, width), BF16),
        cot=V((half, width), BF16),
        wt=V((2, 3 * local_width, width), BF16),
        wo=V((2, local_width, width), BF16),
        wup=V((2, width, hidden), BF16),
        wdn=V((2, hidden, width), BF16),
        wpool=V((width, width), BF16),
        wup_tr=V((2, hidden, width), BF16),
        wdn_tr=V((2, width, hidden), BF16),
        wpool_tr=V((width, width), BF16),
        up_bias=V((2, 8, width), F32),
        bias_mask=V((token_count, half), F32),
        k_pad=V((2, token_count, padded), BF16),
        v_pad=V((2, token_count, padded), BF16),
        k_tr=V((2, local_width, token_count), BF16),
        v_tr=V((2, local_width, token_count), BF16),
        q_pad=V((2, padded, half), BF16),
        q_away=V((local_width, half), BF16),
        probs=V((2, heads, token_count, half), F32),
        ctx=V((2, local_width, half), BF16),
        hid=V((half, width), F32),
        hid_low=V((half, width), BF16),
        hid_tr=V((2, width, half), BF16),
        tok_tr=V((2, width, half), BF16),
        n_one=V((half, width), F32),
        scale_one=V((half, 1), F32),
        act_low=V((2, half, hidden), BF16),
        d_gelu=V((2, half, hidden), F32),
        acc=V((128, width), F32),
        parts=V((4, 2, half, width), BF16),
        d_sec=V((half, width), F32),
        d_br=V((half, width), BF16),
        d_br_tr=V((2, width, half), BF16),
        d_br_peer=V((half, width), BF16),
        d_pre_low=V((2, half, hidden), BF16),
        d_pre_peer=V((half, hidden), BF16),
        act_peer=V((half, hidden), BF16),
        hid_peer=V((half, width), BF16),
        ctx_peer=V((local_width, half), BF16),
        d_att_peer=V((half, width), BF16),
        d_qkv_peer=V((3 * local_width, half), BF16),
        d_first=V((half, width), F32),
        d_att=V((half, width), BF16),
        d_att_tr=V((2, width, half), BF16),
        d_ctx=V((2, padded, half), BF16),
        d_kv_f32=V((2, 2, 2 * local_width, half), F32),
        d_kv_send=V((2, 2, 2 * local_width, half), BF16),
        d_kv_recv=V((2, 2 * local_width, half), BF16),
        d_qkv=V((2, 3 * local_width, half), BF16),
        g_low=V(blocks, BF16),
        first_recv=V((pieces, 2 * pairs, shard, 256), BF16),
        second_send=V((pieces, pairs, shard, 256), BF16),
        second_recv=V((pieces, pairs, shard, 256), BF16),
        last_send=V((pieces, pairs - 1, shard, 256), BF16),
        last_recv=V((pieces, pairs - 1, shard, 256), BF16),
        pool_fin=V((width, width), F32),
        items=V((2, slots, width), BF16),
        items_c=V((slots, width), BF16),
        item_all=V((2, 2, n_dp * slots, width // 2), BF16),
        vec=V((VEC_ROWS, width), F32),
        vec_c=V((VEC_ROWS // 2, width), F32),
        vec_s=V((VEC_ROWS // 2, width), F32),
        vec_y=V((VEC_ROWS // 2, width), F32),
        vec_t=V((VEC_ROWS // 2, width), F32),
        vec_r=V((VEC_ROWS // 2, width), F32),
        vec_q=V((pairs, VEC_ROWS // 2, width), F32),
        cnt=V((8, 128), F32),
        cnt_y=V((8, 128), F32),
        cnt_s=V((8, 128), F32),
        cnt_r=V((8, 128), F32),
        cnt_q=V((pairs, 8, 128), F32),
    )
    found = pl.pallas_call(
        partial(layer_kernel, n_dp),
        out_shape=[
            V((token_count, width), BF16),
            V((token_count, width), BF16),
            V((shard, width), F32),
            V((shard, width), F32),
            V((shard, width), F32),
            V((shard, width), F32),
            V((VEC_ROWS, width), F32),
        ],
        in_specs=[anywhere] * 17,
        out_specs=[vmem] * 7,
        scratch_shapes=list(scratch.values())
        + [
            pltpu.SemaphoreType.DMA((20,)),
            pltpu.SemaphoreType.DMA((copies,)),
            pltpu.SemaphoreType.DMA((copies,)),
        ],
        compiler_params=pltpu.CompilerParams(
            collective_id=0, has_side_effects=True, vmem_limit_bytes=VMEM_LIMIT
        ),
        name="layer",
    )(
        tokens,
        cotangent,
        lengths,
        labels,
        jnp.transpose(w_qkv, (1, 2, 0)).reshape(3 * local_width, width),
        qv_bias,
        w_out,
        branch_bias,
        norm_gain,
        norm_shift,
        w_up,
        up_bias,
        w_down,
        w_pool,
        pool_bias,
        w_class.T,
        class_bias.reshape(1, classes),
    )
    small = local_width // n_dp
    outputs = [
        shape((token_count, width), BF16),
        shape((token_count, width), BF16),
        shape((1, 1), F32),
        shape((1, 1), F32),
        shape((3, shard, local_width), F32),
        shape((2, small), F32),
        shape((local_width, shard), F32),
        shape((2, shard), F32),
        shape((2, shard), F32),
        shape((2, shard), F32),
        shape((shard, hidden), F32),
        shape((1, hidden // n_dp), F32),
        shape((shard, hidden), F32),
        shape((shard, width), F32),
        shape((1, shard), F32),
        shape((classes, shard), F32),
        shape((1, classes), F32),
    ]
    held = [out for i, out in enumerate(outputs) if i not in (0, 1, 10, 12, 13)]
    placed = pl.pallas_call(
        partial(place_kernel, n_dp),
        out_shape=outputs,
        in_specs=[vmem] * 7,
        out_specs=[anywhere] * 17,
        scratch_shapes=[V(out.shape, out.dtype) for out in held] + [pltpu.SemaphoreType.DMA((17,))],
        name="place",
    )(*[pltpu.with_memory_space_constraint(value, pltpu.VMEM) for value in found])
    (
        block_out,
        grad_tokens,
        loss,
        entropy,
        grad_qkv,
        grad_qv,
        grad_out,
        grad_branch,
        grad_gain,
        grad_shift,
        grad_up,
        grad_upb,
        grad_down,
        grad_pool,
        grad_poolb,
        grad_class,
        grad_classb,
    ) = placed
    return (
        block_out,
        grad_tokens,
        loss.reshape(()),
        entropy.reshape(()),
        jnp.transpose(grad_qkv, (1, 0, 2)),
        grad_qv,
        grad_out,
        grad_branch,
        grad_gain,
        grad_shift,
        grad_up,
        grad_upb.reshape(-1),
        grad_down.T,
        grad_pool,
        grad_poolb.reshape(-1),
        grad_class.T,
        grad_classb.reshape(-1),
    )


def solution(mesh):
    in_specs = (
        P("dp", None),
        P("dp", None),
        P("dp", None),
        P("dp", None),
        P(None, None, "tensor"),
        P(None, "tensor"),
        P("tensor", None),
        P(),
        P(),
        P(),
        P(None, "tensor"),
        P("tensor"),
        P("tensor", None),
        P(),
        P(),
        P(),
        P(),
    )
    out_specs = (
        P("dp", None),
        P("dp", None),
        P(),
        P(),
        P("dp", None, "tensor"),
        P(None, ("tensor", "dp")),
        P("tensor", "dp"),
        P(None, "dp"),
        P(None, "dp"),
        P(None, "dp"),
        P("dp", "tensor"),
        P(("tensor", "dp")),
        P("tensor", "dp"),
        P("dp", None),
        P("dp"),
        P("dp", None),
        P(),
    )
    return jax.shard_map(
        partial(on_device, mesh.shape["dp"]),
        mesh=mesh,
        in_specs=in_specs,
        out_specs=out_specs,
        check_vma=False,
    )
```
